32 devices in a mesh: dp: 8 (over y, x, core), expert: 4 (over z).
Axes of the slice: x: 2, y: 2, z: 4, core: 2. Of those that a mesh axis runs over, the one named last changes fastest.
Arguments:
- tokens: bfloat16 [4096, 1024], P(('dp', 'expert')), may hold values from -6 to 6
- cotangent: bfloat16 [4096, 1024], P(('dp', 'expert')), may hold values from -6 to 6
- expert_ids: int32 [4096, 8], P(('dp', 'expert')), may hold values from 0 to 15, all different within a row
- gate_scores: float32 [4096, 8], P(('dp', 'expert')), may hold values from 0.05 to 0.5
- hot_list: int32 [1], replicated, may hold values from 0 to 15
- capacity: int32 [16], replicated, may hold values from 51 to 64, as said below
- w_gate: bfloat16 [32, 1024, 192], P(('dp', 'expert')), may hold values from -0.1875 to 0.1875
- w_up: bfloat16 [32, 1024, 192], P(('dp', 'expert')), may hold values from -0.1875 to 0.1875
- w_down: bfloat16 [32, 192, 1024], P(('dp', 'expert')), may hold values from -0.3125 to 0.3125
Outputs:
- mixed: bfloat16 [4096, 1024], P(('dp', 'expert'))
- token_grad: bfloat16 [4096, 1024], P(('dp', 'expert'))
- grad_gate: bfloat16 [32, 1024, 192], P(('dp', 'expert'))
- grad_up: bfloat16 [32, 1024, 192], P(('dp', 'expert'))
- grad_down: bfloat16 [32, 192, 1024], P(('dp', 'expert'))
The draws below stay inside these ranges and needn't reach their ends.
Inputs may be any that keep to these rules, and one draw needn't show every extreme that they name: `expert_ids`: each token names 8 different experts. Some expert's capacity equals 64.
All inputs are finite; a program needn't handle non-finite values.
Results may differ from the reference program's by a relative error of at most 0.0071.
Values may be sent and summed in bfloat16 or wider, within the bound.
No kernel may reach another device: no remote copies, remote signals or barrier semaphores. Data moves between devices by JAX's collectives and lax.ppermute only.
A program may use at most 128 MiB of HBM per device.

```python
import math
from functools import partial
import jax
import jax.numpy as jnp
from jax import lax

D = 1024
FF = 384
FFH = 192
TOPK = 8
HOT = 1
TOK_DEV = 128
EXPERTS = 16
CAP = 64
TOKENS = 4096
N_DP = 8
N_EXPERT = 4


def draw_capacity(key, part):
    first_key, second_key = jax.random.split(key)
    lowest = max(2, CAP - 1 - CAP // 5)
    drawn = jax.random.randint(first_key, (EXPERTS,), lowest, CAP + 1)
    chosen = jax.random.randint(second_key, (), 0, EXPERTS)
    expert_iota = jnp.arange(EXPERTS, dtype=jnp.int32)
    return jnp.where(expert_iota == chosen, CAP, drawn).astype(jnp.int32)


def level_of(key, extent, shards, smallest, top_value):
    def one(dim, shards_of):
        heights = jax.random.uniform(jax.random.fold_in(jax.random.fold_in(key, 6), dim), (shards_of,), jnp.float32, smallest / len(shards), top_value / len(shards))
        return jnp.repeat(jnp.exp(heights), extent[dim] // shards_of).reshape((-1,) + (1,) * (len(extent) - dim - 1))

    loudness = one(*shards[0])
    for cut in shards[1:]:
        loudness = loudness * one(*cut)
    return loudness


def distinct(key, rows, count, top, lift):
    sequence = jax.random.permutation(jax.random.fold_in(key, 1), count)
    pull = sequence
    for power in range(3):
        pull = pull * pull // count
    pull = pull * lift // count
    chance = jax.random.randint(jax.random.fold_in(key, 2), (rows, count), 0, 4096) + pull
    sure = jax.random.permutation(jax.random.fold_in(key, 3), rows)[jnp.arange(count) % rows]
    chance = jnp.where(jnp.arange(rows)[:, None] == sure[None, :], 1 << 14, chance)
    priority = chance * count + jnp.arange(count)
    return lax.top_k(priority.astype(jnp.int32), top)[1].astype(jnp.int32)


def centred(own_key, extent, scale, bound, cuts=(), kind=jnp.bfloat16):
    result = jax.random.normal(own_key, extent, jnp.float32) * scale
    if len(cuts) > 0:
        result = level_of(own_key, extent, cuts, -0.22, 0.18) * result
    return jnp.clip(result, min=-bound, max=bound).astype(kind)


def setup_inputs(seed: int = 0) -> dict:
    keys = jax.random.split(jax.random.key(seed), 10)
    tokens = centred(keys[0], (TOKENS, D), 1.0, 6.0, ((0, 32),))
    cotangent = centred(keys[1], (TOKENS, D), 1.0, 6.0, ((0, 32),))
    expert_ids = distinct(keys[2], TOKENS, EXPERTS, TOPK, 8192)
    gate_scores = jnp.clip(jnp.exp(math.log(0.5) - 2.3025851 * jax.random.uniform(keys[3], (TOKENS, TOPK), jnp.float32) ** level_of(keys[3], (TOKENS, TOPK), ((0, 32),), -0.2, 0.2)), 0.05, 0.5)
    hot_list = jax.random.randint(keys[4], (HOT,), 0, EXPERTS).astype(jnp.int32)
    capacity = draw_capacity(jax.random.fold_in(keys[9], 71), 0)
    w_gate = centred(keys[6], (2 * EXPERTS, D, FFH), D ** -0.5, 0.1875, ((0, 32),))
    w_up = centred(keys[7], (2 * EXPERTS, D, FFH), D ** -0.5, 0.1875, ((0, 32),))
    w_down = centred(keys[8], (2 * EXPERTS, FFH, D), FF ** -0.5, 0.3125, ((0, 32),))
    return {"tokens": tokens, "cotangent": cotangent, "expert_ids": expert_ids, "gate_scores": gate_scores, "hot_list": hot_list, "capacity": capacity, "w_gate": w_gate, "w_up": w_up, "w_down": w_down}


def activation(pre_gate):
    sigmoid_value = jax.nn.sigmoid(pre_gate)
    return pre_gate * sigmoid_value, sigmoid_value * (1.0 + pre_gate * (1.0 - sigmoid_value))


def half_pass(rows_in, rows_back, gate_half, up_half, down_half):
    pre_gate = jnp.dot(rows_in, gate_half, preferred_element_type=jnp.float32)
    pre_up = jnp.dot(rows_in, up_half, preferred_element_type=jnp.float32)
    activated, slope_value = activation(pre_gate)
    hidden = (activated * pre_up).astype(jnp.bfloat16)
    part_out = jnp.dot(hidden, down_half, preferred_element_type=jnp.float32).astype(jnp.bfloat16)
    back_hidden = jnp.dot(rows_back, down_half.T, preferred_element_type=jnp.float32)
    grad_up_rows = (back_hidden * activated).astype(jnp.bfloat16)
    grad_gate_rows = (back_hidden * pre_up * slope_value).astype(jnp.bfloat16)
    part_grad = (jnp.dot(grad_gate_rows, gate_half.T, preferred_element_type=jnp.float32)
                 + jnp.dot(grad_up_rows, up_half.T, preferred_element_type=jnp.float32)).astype(jnp.bfloat16)
    w_gate_grad = jnp.dot(rows_in.T, grad_gate_rows, preferred_element_type=jnp.float32)
    w_up_grad = jnp.dot(rows_in.T, grad_up_rows, preferred_element_type=jnp.float32)
    w_down_grad = jnp.dot(hidden.T, rows_back, preferred_element_type=jnp.float32)
    return part_out, part_grad, w_gate_grad, w_up_grad, w_down_grad


def block_rank(block_ids, expert_count):
    iota_experts = jnp.arange(expert_count, dtype=jnp.int32)
    onehot = (block_ids[:, :, None] == iota_experts[None, None, :]).astype(jnp.int32)
    per_token = jnp.sum(onehot, axis=1).astype(jnp.int32)
    earlier = (jnp.cumsum(per_token, axis=0) - per_token).astype(jnp.int32)
    return jnp.sum(onehot * earlier[:, None, :], axis=2).astype(jnp.int32)


def reference(tokens, cotangent, expert_ids, gate_scores, hot_list, capacity, w_gate, w_up, w_down):
    token_count, model_width = tokens.shape
    expert_count = capacity.shape[0]
    assign_count = token_count * TOPK
    row_limit = N_DP * N_EXPERT * CAP
    block_ids = expert_ids.reshape(token_count // TOK_DEV, TOK_DEV, TOPK)
    slot_rank = lax.map(partial(block_rank, expert_count=expert_count), block_ids).reshape(token_count, TOPK)
    cap_limit = capacity[expert_ids]
    is_hot = jnp.any(expert_ids[:, :, None] == hot_list[None, None, :], axis=2)
    is_cold = jnp.logical_and(jnp.logical_not(is_hot), slot_rank < cap_limit)
    flat_ids = expert_ids.reshape(-1)
    sort_key = jnp.where(is_cold.reshape(-1), flat_ids, expert_count).astype(jnp.int32)
    sort_order = jnp.argsort(sort_key, stable=True).astype(jnp.int32)
    group_sizes = jnp.zeros((expert_count + 1,), jnp.int32).at[sort_key].add(1)
    group_starts = (jnp.cumsum(group_sizes) - group_sizes).astype(jnp.int32)
    padded_order = jnp.concatenate([sort_order, jnp.full((row_limit,), assign_count, jnp.int32)])
    row_iota = jnp.arange(row_limit, dtype=jnp.int32)
    positions = group_starts[:expert_count, None] + row_iota[None, :]
    picked = padded_order[positions]
    valid_rows = row_iota[None, :] < group_sizes[:expert_count, None]
    safe_pick = jnp.minimum(picked, assign_count - 1)
    row_tokens = (safe_pick // TOPK).astype(jnp.int32)
    row_gate = jnp.where(valid_rows, gate_scores.reshape(-1)[safe_pick], 0.0)
    valid_mask = valid_rows.astype(jnp.float32)

    def cold_expert(operands):
        expert_index, token_index, gate_row, mask_row = operands
        rows_in = tokens[token_index] * mask_row[:, None].astype(tokens.dtype)
        rows_back = (gate_row[:, None] * cotangent[token_index].astype(jnp.float32)).astype(jnp.bfloat16)
        first = half_pass(rows_in, rows_back, w_gate[2 * expert_index], w_up[2 * expert_index], w_down[2 * expert_index])
        second = half_pass(rows_in, rows_back, w_gate[2 * expert_index + 1], w_up[2 * expert_index + 1], w_down[2 * expert_index + 1])
        row_out = (first[0].astype(jnp.float32) + second[0].astype(jnp.float32)).astype(jnp.bfloat16)
        row_grad = (first[1].astype(jnp.float32) + second[1].astype(jnp.float32)).astype(jnp.bfloat16)
        gate_pair = jnp.stack([first[2], second[2]]).astype(jnp.bfloat16)
        up_pair = jnp.stack([first[3], second[3]]).astype(jnp.bfloat16)
        down_pair = jnp.stack([first[4], second[4]]).astype(jnp.bfloat16)
        return row_out, row_grad, gate_pair, up_pair, down_pair

    expert_iota = jnp.arange(expert_count, dtype=jnp.int32)
    row_out, row_grad, gate_pairs, up_pairs, down_pairs = lax.map(cold_expert, (expert_iota, row_tokens, row_gate, valid_mask))
    flat_tokens = row_tokens.reshape(-1)
    mixed = jnp.zeros((token_count, model_width), jnp.float32).at[flat_tokens].add(
        (row_gate[:, :, None] * row_out.astype(jnp.float32)).reshape(-1, model_width))
    token_grad = jnp.zeros((token_count, model_width), jnp.float32).at[flat_tokens].add(
        (valid_mask[:, :, None] * row_grad.astype(jnp.float32)).reshape(-1, model_width))
    grad_gate = gate_pairs.reshape(2 * expert_count, model_width, -1)
    grad_up = up_pairs.reshape(2 * expert_count, model_width, -1)
    grad_down = down_pairs.reshape(2 * expert_count, -1, model_width)
    for hot_slot in range(HOT):
        hot_expert = hot_list[hot_slot]
        matches = expert_ids == hot_expert
        hot_coef = jnp.sum(jnp.where(matches, gate_scores, 0.0), axis=1)
        present = jnp.any(matches, axis=1).astype(jnp.float32)
        hot_back = (hot_coef[:, None] * cotangent.astype(jnp.float32)).astype(jnp.bfloat16)
        first = half_pass(tokens, hot_back, w_gate[2 * hot_expert], w_up[2 * hot_expert], w_down[2 * hot_expert])
        second = half_pass(tokens, hot_back, w_gate[2 * hot_expert + 1], w_up[2 * hot_expert + 1], w_down[2 * hot_expert + 1])
        hot_out = (first[0].astype(jnp.float32) + second[0].astype(jnp.float32)).astype(jnp.bfloat16)
        hot_grad = (first[1].astype(jnp.float32) + second[1].astype(jnp.float32)).astype(jnp.bfloat16)
        mixed = mixed + hot_coef[:, None] * hot_out.astype(jnp.float32)
        token_grad = token_grad + present[:, None] * hot_grad.astype(jnp.float32)
        grad_gate = grad_gate.at[2 * hot_expert].set(first[2].astype(jnp.bfloat16)).at[2 * hot_expert + 1].set(second[2].astype(jnp.bfloat16))
        grad_up = grad_up.at[2 * hot_expert].set(first[3].astype(jnp.bfloat16)).at[2 * hot_expert + 1].set(second[3].astype(jnp.bfloat16))
        grad_down = grad_down.at[2 * hot_expert].set(first[4].astype(jnp.bfloat16)).at[2 * hot_expert + 1].set(second[4].astype(jnp.bfloat16))
    return mixed.astype(jnp.bfloat16), token_grad.astype(jnp.bfloat16), grad_gate, grad_up, grad_down
```

```python
import jax
import jax.numpy as jnp
from jax import lax
from jax.sharding import PartitionSpec as P


F32 = jnp.float32
BF16 = jnp.bfloat16


def swap(value, count, mask):
    return lax.ppermute(value, "dp", [(i, i ^ mask) for i in range(count)])


def rotate(value, count, step):
    return lax.ppermute(value, "expert", [(i, (i + step) % count) for i in range(count)])


def nt(left, right):
    return lax.dot_general(left, right, (((1,), (1,)), ((), ())), preferred_element_type=F32)


def tn(left, right, **kw):
    return lax.dot_general(left, right, (((0,), (0,)), ((), ())), preferred_element_type=F32, **kw)


def coefficients(expert_ids, gate_scores, hot_list, capacity):
    count = capacity.shape[0]
    tokens = expert_ids.shape[0]
    iota = jnp.arange(count, dtype=jnp.int32)
    match = expert_ids.T[:, None, :] == iota[None, :, None]
    gates = jnp.sum(jnp.where(match, gate_scores.T[:, None, :], 0.0), axis=0)
    present = jnp.any(match, axis=0)
    order = jnp.arange(tokens, dtype=jnp.int32)
    before = (order[:, None] < order[None, :]).astype(BF16)
    rank = jnp.dot(present.astype(BF16), before, preferred_element_type=F32)
    hot = jnp.any(iota[:, None] == hot_list[None, :], axis=1)
    kept = present & (hot[:, None] | (rank < capacity[:, None].astype(F32)))
    return jnp.where(kept, gates, 0.0)


def gather_slots(own, order, dp_count):
    slots = {0: own}
    for bit in order:
        slots.update({r | bit: swap(v, dp_count, 2 * bit) for r, v in list(slots.items())})
    return slots


def reduce_slots(parts, order, dp_count):
    parts = dict(parts)
    for bit in order:
        moved = {r: swap(parts[r].astype(BF16), dp_count, 2 * bit) for r in parts if r & bit}
        parts = {
            r: v.astype(F32) + moved[r | bit].astype(F32) for r, v in parts.items() if not r & bit
        }
    return parts[0]


def on_device(tokens, cotangent, expert_ids, gate_scores, hot_list, capacity, w_gate, w_up, w_down):
    dp_count = lax.axis_size("dp")
    ring = lax.axis_size("expert")
    groups = dp_count // 2
    bits = [1 << b for b in range(groups.bit_length() - 1)]
    orders = (bits, bits[::-1])
    token_count, width = tokens.shape
    hidden = w_gate.shape[2]
    rows = 3 * hidden
    cut = rows // 2
    packed = jnp.concatenate([w_gate[0].T, w_up[0].T, w_down[0]], axis=0)

    def spread(value):
        own = [value]
        for _ in range(ring - 1):
            own.append(rotate(own[-1], ring, 1))
        return own + [swap(v, dp_count, 1) for v in own]

    x_all = jnp.concatenate(spread(tokens), axis=0)
    c_all = jnp.concatenate(spread(cotangent), axis=0)
    coef = coefficients(expert_ids, gate_scores, hot_list, capacity)
    coef_all = jnp.concatenate(spread(coef), axis=1)

    first = gather_slots(packed[:cut], orders[0], dp_count)
    second = gather_slots(packed[cut:], orders[1], dp_count)
    full = [jnp.concatenate([first[r], second[r]], axis=0) for r in range(groups)]
    gate_t = jnp.concatenate([f[:hidden] for f in full], axis=0)
    up_t = jnp.concatenate([f[hidden : 2 * hidden] for f in full], axis=0)
    down = jnp.concatenate([f[2 * hidden :] for f in full], axis=0)

    my_dp = lax.axis_index("dp")
    my_expert = lax.axis_index("expert")
    slot_of = jnp.arange(groups * hidden, dtype=jnp.int32) // hidden
    expert_of = (((my_dp ^ (2 * slot_of)) * ring + my_expert) // 2).astype(jnp.int32)
    pick = (jnp.arange(capacity.shape[0], dtype=jnp.int32)[:, None] == expert_of[None, :]).astype(F32)
    def compute(x_part, c_part, coef_part):
        weight = tn(coef_part, pick, precision=lax.Precision.HIGHEST)
        gate_pre = nt(x_part, gate_t)
        up_pre = nt(x_part, up_t)
        back = nt(c_part, down) * weight
        sig = jax.nn.sigmoid(gate_pre)
        act = gate_pre * sig
        scaled_hidden = (act * up_pre * weight).astype(BF16)
        d_up = (back * act).astype(BF16)
        d_gate = (back * up_pre * (sig * (1.0 + gate_pre * (1.0 - sig)))).astype(BF16)
        out = jnp.dot(scaled_hidden, down, preferred_element_type=F32)
        grad = jnp.dot(d_gate, gate_t, preferred_element_type=F32) + jnp.dot(
            d_up, up_t, preferred_element_type=F32
        )
        return out, grad, tn(d_gate, x_part), tn(d_up, x_part), tn(scaled_hidden, c_part)

    all_tokens = x_all.shape[0]
    steps = max(1, all_tokens // 1024)
    if steps == 1:
        out, grad, gate_g, up_g, down_g = compute(x_all, c_all, coef_all)
    else:
        size = all_tokens // steps

        def step(carry, chunk):
            got = compute(*chunk)
            carry = tuple(a + b for a, b in zip(carry, got[2:]))
            return carry, (got[0].astype(BF16), got[1].astype(BF16))

        zero = jnp.zeros((groups * hidden, width), F32)
        chunks = (
            x_all.reshape(steps, size, width),
            c_all.reshape(steps, size, width),
            coef_all.reshape(-1, steps, size).swapaxes(0, 1),
        )
        (gate_g, up_g, down_g), (out, grad) = lax.scan(step, (zero, zero, zero), chunks)
        out = out.reshape(all_tokens, width).astype(F32)
        grad = grad.reshape(all_tokens, width).astype(F32)

    def collect(value):
        half = ring * token_count
        away = swap(value[half:].astype(BF16), dp_count, 1)
        mine = value[:half] + away.astype(F32)
        pieces = [mine[s * token_count : (s + 1) * token_count] for s in range(ring)]
        carry = pieces[ring - 1]
        for s in range(ring - 2, -1, -1):
            carry = pieces[s] + rotate(carry.astype(BF16), ring, -1).astype(F32)
        return carry.astype(BF16)

    parts = [
        jnp.concatenate([g[r * hidden : (r + 1) * hidden] for g in (gate_g, up_g, down_g)], axis=0)
        for r in range(groups)
    ]
    total_a = reduce_slots({r: parts[r][:cut] for r in range(groups)}, orders[0], dp_count)
    total_b = reduce_slots({r: parts[r][cut:] for r in range(groups)}, orders[1], dp_count)
    total = jnp.concatenate([total_a, total_b], axis=0).astype(BF16)
    return (
        collect(out),
        collect(grad),
        total[:hidden].T[None],
        total[hidden : 2 * hidden].T[None],
        total[2 * hidden :][None],
    )


def solution(mesh):
    rows = P(("dp", "expert"), None)
    weights = P(("dp", "expert"), None, None)
    return jax.shard_map(
        on_device,
        mesh=mesh,
        in_specs=(rows, rows, rows, rows, P(), P(), weights, weights, weights),
        out_specs=(rows, rows, weights, weights, weights),
        check_vma=False,
    )
```

```python
import jax
import jax.numpy as jnp
from jax import lax
from jax.experimental import pallas as pl
from jax.experimental.pallas import tpu as pltpu
from jax.sharding import PartitionSpec as P


F32 = jnp.float32
BF16 = jnp.bfloat16


def swap(value, count, mask):
    return lax.ppermute(value, "dp", [(i, i ^ mask) for i in range(count)])


def rotate(value, count, step):
    return lax.ppermute(value, "expert", [(i, (i + step) % count) for i in range(count)])


def nt(left, right):
    return lax.dot_general(left, right, (((1,), (1,)), ((), ())), preferred_element_type=F32)


def tn(left, right, **kw):
    return lax.dot_general(left, right, (((0,), (0,)), ((), ())), preferred_element_type=F32, **kw)


def coefficients(expert_ids, gate_scores, hot_list, capacity):
    count = capacity.shape[0]
    tokens = expert_ids.shape[0]
    iota = jnp.arange(count, dtype=jnp.int32)
    match = expert_ids.T[:, None, :] == iota[None, :, None]
    gates = jnp.sum(jnp.where(match, gate_scores.T[:, None, :], 0.0), axis=0)
    present = jnp.any(match, axis=0)
    order = jnp.arange(tokens, dtype=jnp.int32)
    before = (order[:, None] < order[None, :]).astype(BF16)
    rank = jnp.dot(present.astype(BF16), before, preferred_element_type=F32)
    hot = jnp.any(iota[:, None] == hot_list[None, :], axis=1)
    kept = present & (hot[:, None] | (rank < capacity[:, None].astype(F32)))
    return jnp.where(kept, gates, 0.0)


def gather_slots(own, order, dp_count):
    slots = {0: own}
    for bit in order:
        slots.update({r | bit: swap(v, dp_count, 2 * bit) for r, v in list(slots.items())})
    return slots


def reduce_slots(parts, order, dp_count):
    parts = dict(parts)
    for bit in order:
        moved = {r: swap(parts[r].astype(BF16), dp_count, 2 * bit) for r in parts if r & bit}
        parts = {
            r: v.astype(F32) + moved[r | bit].astype(F32) for r, v in parts.items() if not r & bit
        }
    return parts[0]


def large_device(tokens, cotangent, expert_ids, gate_scores, hot_list, capacity, w_gate, w_up, w_down):
    dp_count = lax.axis_size("dp")
    ring = lax.axis_size("expert")
    groups = dp_count // 2
    bits = [1 << b for b in range(groups.bit_length() - 1)]
    orders = (bits, bits[::-1])
    token_count, width = tokens.shape
    hidden = w_gate.shape[2]
    rows = 3 * hidden
    cut = rows // 2
    packed = jnp.concatenate([w_gate[0].T, w_up[0].T, w_down[0]], axis=0)

    def spread(value):
        own = [value]
        for _ in range(ring - 1):
            own.append(rotate(own[-1], ring, 1))
        return own + [swap(v, dp_count, 1) for v in own]

    x_all = jnp.concatenate(spread(tokens), axis=0)
    c_all = jnp.concatenate(spread(cotangent), axis=0)
    coef = coefficients(expert_ids, gate_scores, hot_list, capacity)
    coef_all = jnp.concatenate(spread(coef), axis=1)

    first = gather_slots(packed[:cut], orders[0], dp_count)
    second = gather_slots(packed[cut:], orders[1], dp_count)
    full = [jnp.concatenate([first[r], second[r]], axis=0) for r in range(groups)]
    gate_t = jnp.concatenate([f[:hidden] for f in full], axis=0)
    up_t = jnp.concatenate([f[hidden : 2 * hidden] for f in full], axis=0)
    down = jnp.concatenate([f[2 * hidden :] for f in full], axis=0)

    my_dp = lax.axis_index("dp")
    my_expert = lax.axis_index("expert")
    slot_of = jnp.arange(groups * hidden, dtype=jnp.int32) // hidden
    expert_of = (((my_dp ^ (2 * slot_of)) * ring + my_expert) // 2).astype(jnp.int32)
    pick = (jnp.arange(capacity.shape[0], dtype=jnp.int32)[:, None] == expert_of[None, :]).astype(F32)
    def compute(x_part, c_part, coef_part):
        weight = tn(coef_part, pick, precision=lax.Precision.HIGHEST)
        gate_pre = nt(x_part, gate_t)
        up_pre = nt(x_part, up_t)
        back = nt(c_part, down) * weight
        sig = jax.nn.sigmoid(gate_pre)
        act = gate_pre * sig
        scaled_hidden = (act * up_pre * weight).astype(BF16)
        d_up = (back * act).astype(BF16)
        d_gate = (back * up_pre * (sig * (1.0 + gate_pre * (1.0 - sig)))).astype(BF16)
        out = jnp.dot(scaled_hidden, down, preferred_element_type=F32)
        grad = jnp.dot(d_gate, gate_t, preferred_element_type=F32) + jnp.dot(
            d_up, up_t, preferred_element_type=F32
        )
        return out, grad, tn(d_gate, x_part), tn(d_up, x_part), tn(scaled_hidden, c_part)

    all_tokens = x_all.shape[0]
    steps = max(1, all_tokens // 1024)
    if steps == 1:
        out, grad, gate_g, up_g, down_g = compute(x_all, c_all, coef_all)
    else:
        size = all_tokens // steps

        def step(carry, chunk):
            got = compute(*chunk)
            carry = tuple(a + b for a, b in zip(carry, got[2:]))
            return carry, (got[0].astype(BF16), got[1].astype(BF16))

        zero = jnp.zeros((groups * hidden, width), F32)
        chunks = (
            x_all.reshape(steps, size, width),
            c_all.reshape(steps, size, width),
            coef_all.reshape(-1, steps, size).swapaxes(0, 1),
        )
        (gate_g, up_g, down_g), (out, grad) = lax.scan(step, (zero, zero, zero), chunks)
        out = out.reshape(all_tokens, width).astype(F32)
        grad = grad.reshape(all_tokens, width).astype(F32)

    def collect(value):
        half = ring * token_count
        away = swap(value[half:].astype(BF16), dp_count, 1)
        mine = value[:half] + away.astype(F32)
        pieces = [mine[s * token_count : (s + 1) * token_count] for s in range(ring)]
        carry = pieces[ring - 1]
        for s in range(ring - 2, -1, -1):
            carry = pieces[s] + rotate(carry.astype(BF16), ring, -1).astype(F32)
        return carry.astype(BF16)

    parts = [
        jnp.concatenate([g[r * hidden : (r + 1) * hidden] for g in (gate_g, up_g, down_g)], axis=0)
        for r in range(groups)
    ]
    total_a = reduce_slots({r: parts[r][:cut] for r in range(groups)}, orders[0], dp_count)
    total_b = reduce_slots({r: parts[r][cut:] for r in range(groups)}, orders[1], dp_count)
    total = jnp.concatenate([total_a, total_b], axis=0).astype(BF16)
    return (
        collect(out),
        collect(grad),
        total[:hidden].T[None],
        total[hidden : 2 * hidden].T[None],
        total[2 * hidden :][None],
    )


def activation_kernel(slots, hidden, ring, *refs):
    x_own, x_other = refs[:ring], refs[ring : 2 * ring]
    c_own, c_other = refs[2 * ring : 3 * ring], refs[3 * ring : 4 * ring]
    refs = refs[4 * ring :]
    first, second, coef = refs[:slots], refs[slots : 2 * slots], refs[2 * slots]
    x_all, c_all, gates, ups, downs, scaled, d_gate, d_up, pre, back = refs[2 * slots + 1 :]
    half = hidden // 2
    size = x_own[0].shape[0]
    for r in range(slots):
        low = r * hidden
        gates[low : low + hidden] = first[r][:hidden]
        downs[low : low + half] = first[r][hidden:]
        ups[low : low + hidden] = second[r][:hidden]
        downs[low + half : low + hidden] = second[r][hidden:]
    for s in range(ring):
        block = slice(2 * s * size, 2 * (s + 1) * size)
        x_part = jnp.concatenate([x_own[s][...], x_other[s][...]], axis=0)
        c_part = jnp.concatenate([c_own[s][...], c_other[s][...]], axis=0)
        x_all[block] = x_part
        c_all[block] = c_part
        buf = s % 2
        pre[buf, 0] = nt(gates[...], x_part)
        pre[buf, 1] = nt(ups[...], x_part)
        back[buf] = nt(downs[...], c_part)
        for r in range(slots):
            rows = slice(r * hidden, (r + 1) * hidden)
            weight = coef[r : r + 1, block]
            gate_pre = pre[buf, 0, rows]
            up_pre = pre[buf, 1, rows]
            sig = jax.nn.sigmoid(gate_pre)
            act = gate_pre * sig
            grad_hidden = back[buf, rows] * weight
            scaled[rows, block] = (act * up_pre * weight).astype(BF16)
            d_up[rows, block] = (grad_hidden * act).astype(BF16)
            d_gate[rows, block] = (
                grad_hidden * up_pre * (sig * (1.0 + gate_pre * (1.0 - sig)))
            ).astype(BF16)


def on_device(tokens, cotangent, expert_ids, gate_scores, hot_list, capacity, w_gate, w_up, w_down):
    dp_count = lax.axis_size("dp")
    ring = lax.axis_size("expert")
    groups = dp_count // 2
    token_count, width = tokens.shape
    if groups != 4 or 2 * ring * token_count > 1024:
        return large_device(
            tokens, cotangent, expert_ids, gate_scores, hot_list, capacity, w_gate, w_up, w_down
        )
    hidden = w_gate.shape[2]
    half = hidden // 2
    cut = hidden + half
    total = 2 * ring * token_count

    def chain(value):
        own = [value]
        for _ in range(ring - 1):
            own.append(rotate(own[-1], ring, 1))
        return own

    x_own, c_own = chain(tokens), chain(cotangent)
    x_other = [swap(v, dp_count, 1) for v in x_own]
    c_other = [swap(v, dp_count, 1) for v in c_own]

    first0 = jnp.concatenate([w_gate[0].T, w_down[0][:half]], axis=0)
    second0 = jnp.concatenate([w_up[0].T, w_down[0][half:]], axis=0)
    first1, first2 = swap(first0, dp_count, 2), swap(first0, dp_count, 4)
    second1, second2 = swap(second0, dp_count, 2), swap(second0, dp_count, 4)
    first = (first0, first1, first2, swap(first1, dp_count, 4))
    second = (second0, second1, second2, swap(second2, dp_count, 2))

    coef = coefficients(expert_ids, gate_scores, hot_list, capacity)
    coef = jnp.concatenate([coef, swap(coef, dp_count, 1)], axis=1)
    coef = jnp.concatenate([coef] + [rotate(coef, ring, s) for s in range(1, ring)], axis=1)
    slot = jnp.arange(groups, dtype=jnp.int32)
    expert_of = ((lax.axis_index("dp") ^ (2 * slot)) * ring + lax.axis_index("expert")) // 2
    pick = expert_of[:, None] == jnp.arange(capacity.shape[0], dtype=jnp.int32)[None, :]
    weight = jnp.sum(jnp.where(pick[:, :, None], coef[None], 0.0), axis=1)

    whole = pl.BlockSpec(memory_space=pltpu.VMEM)
    units = groups * hidden
    ins = (*x_own, *x_other, *c_own, *c_other, *first, *second, weight)
    flops = 6 * units * width * total
    x_all, c_all, gates, ups, downs, scaled, d_gate, d_up = pl.pallas_call(
        lambda *refs: activation_kernel(groups, hidden, ring, *refs),
        out_shape=[jax.ShapeDtypeStruct((total, width), BF16)] * 2
        + [jax.ShapeDtypeStruct((units, width), BF16)] * 3
        + [jax.ShapeDtypeStruct((units, total), BF16)] * 3,
        in_specs=[whole] * len(ins),
        out_specs=[whole] * 8,
        scratch_shapes=[
            pltpu.VMEM((2, 2, units, 2 * token_count), F32),
            pltpu.VMEM((2, units, 2 * token_count), F32),
        ],
        compiler_params=pltpu.CompilerParams(vmem_limit_bytes=60 << 20),
        cost_estimate=pl.CostEstimate(
            flops=flops, bytes_accessed=16 << 20, transcendentals=units * total
        ),
        name="activation",
    )(*ins)

    def outputs(s):
        block = slice(2 * s * token_count, 2 * (s + 1) * token_count)
        out = tn(scaled[:, block], downs)
        grad = tn(d_gate[:, block], gates) + tn(d_up[:, block], ups)
        return out, grad

    def merge(value):
        away = swap(value[token_count:].astype(BF16), dp_count, 1)
        return value[:token_count] + away.astype(F32)

    carry = None
    for s in range(ring - 1, -1, -1):
        mine = [merge(v) for v in outputs(s)]
        if carry is not None:
            mine = [m + rotate(c, ring, -1).astype(F32) for m, c in zip(mine, carry)]
        carry = [m.astype(BF16) for m in mine]
    mixed, token_grad = carry

    def weight_part(r):
        rows = slice(r * hidden, (r + 1) * hidden)
        down_g = jnp.dot(scaled[rows], c_all, preferred_element_type=F32)
        gate_g = jnp.dot(d_gate[rows], x_all, preferred_element_type=F32)
        up_g = jnp.dot(d_up[rows], x_all, preferred_element_type=F32)
        return (
            jnp.concatenate([gate_g, down_g[:half]], axis=0),
            jnp.concatenate([up_g, down_g[half:]], axis=0),
        )

    part = {r: weight_part(r) for r in (3, 1, 2, 0)}
    a3 = swap(part[3][0].astype(BF16), dp_count, 2)
    b3 = swap(part[3][1].astype(BF16), dp_count, 4)
    a1 = swap(part[1][0].astype(BF16), dp_count, 2)
    b2 = swap(part[2][1].astype(BF16), dp_count, 4)
    a2 = swap((part[2][0] + a3.astype(F32)).astype(BF16), dp_count, 4)
    b1 = swap((part[1][1] + b3.astype(F32)).astype(BF16), dp_count, 2)
    a0 = (part[0][0] + a1.astype(F32) + a2.astype(F32)).astype(BF16)
    b0 = (part[0][1] + b2.astype(F32) + b1.astype(F32)).astype(BF16)
    return (
        mixed,
        token_grad,
        a0[:hidden].T[None],
        b0[:hidden].T[None],
        jnp.concatenate([a0[hidden:], b0[hidden:]], axis=0)[None],
    )


def solution(mesh):
    rows = P(("dp", "expert"), None)
    weights = P(("dp", "expert"), None, None)
    return jax.shard_map(
        on_device,
        mesh=mesh,
        in_specs=(rows, rows, rows, rows, P(), P(), weights, weights, weights),
        out_specs=(rows, rows, weights, weights, weights),
        check_vma=False,
    )
```

```python
import jax
import jax.numpy as jnp
from jax import lax
from jax.experimental import pallas as pl
from jax.experimental.pallas import tpu as pltpu
from jax.sharding import PartitionSpec as P


F32 = jnp.float32
BF16 = jnp.bfloat16


def swap(value, count, mask):
    return lax.ppermute(value, "dp", [(i, i ^ mask) for i in range(count)])


def rotate(value, count, step):
    return lax.ppermute(value, "expert", [(i, (i + step) % count) for i in range(count)])


def nt(left, right):
    return lax.dot_general(left, right, (((1,), (1,)), ((), ())), preferred_element_type=F32)


def tn(left, right, **kw):
    return lax.dot_general(left, right, (((0,), (0,)), ((), ())), preferred_element_type=F32, **kw)


def coefficients(expert_ids, gate_scores, hot_list, capacity):
    count = capacity.shape[0]
    tokens = expert_ids.shape[0]
    iota = jnp.arange(count, dtype=jnp.int32)
    match = expert_ids.T[:, None, :] == iota[None, :, None]
    gates = jnp.sum(jnp.where(match, gate_scores.T[:, None, :], 0.0), axis=0)
    present = jnp.any(match, axis=0)
    order = jnp.arange(tokens, dtype=jnp.int32)
    before = (order[:, None] < order[None, :]).astype(BF16)
    rank = jnp.dot(present.astype(BF16), before, preferred_element_type=F32)
    hot = jnp.any(iota[:, None] == hot_list[None, :], axis=1)
    kept = present & (hot[:, None] | (rank < capacity[:, None].astype(F32)))
    return jnp.where(kept, gates, 0.0)


def gather_slots(own, order, dp_count):
    slots = {0: own}
    for bit in order:
        slots.update({r | bit: swap(v, dp_count, 2 * bit) for r, v in list(slots.items())})
    return slots


def reduce_slots(parts, order, dp_count):
    parts = dict(parts)
    for bit in order:
        moved = {r: swap(parts[r].astype(BF16), dp_count, 2 * bit) for r in parts if r & bit}
        parts = {
            r: v.astype(F32) + moved[r | bit].astype(F32) for r, v in parts.items() if not r & bit
        }
    return parts[0]


def large_device(tokens, cotangent, expert_ids, gate_scores, hot_list, capacity, w_gate, w_up, w_down):
    dp_count = lax.axis_size("dp")
    ring = lax.axis_size("expert")
    groups = dp_count // 2
    bits = [1 << b for b in range(groups.bit_length() - 1)]
    orders = (bits, bits[::-1])
    token_count, width = tokens.shape
    hidden = w_gate.shape[2]
    rows = 3 * hidden
    cut = rows // 2
    packed = jnp.concatenate([w_gate[0].T, w_up[0].T, w_down[0]], axis=0)

    def spread(value):
        own = [value]
        for _ in range(ring - 1):
            own.append(rotate(own[-1], ring, 1))
        return own + [swap(v, dp_count, 1) for v in own]

    x_all = jnp.concatenate(spread(tokens), axis=0)
    c_all = jnp.concatenate(spread(cotangent), axis=0)
    coef = coefficients(expert_ids, gate_scores, hot_list, capacity)
    coef_all = jnp.concatenate(spread(coef), axis=1)

    first = gather_slots(packed[:cut], orders[0], dp_count)
    second = gather_slots(packed[cut:], orders[1], dp_count)
    full = [jnp.concatenate([first[r], second[r]], axis=0) for r in range(groups)]
    gate_t = jnp.concatenate([f[:hidden] for f in full], axis=0)
    up_t = jnp.concatenate([f[hidden : 2 * hidden] for f in full], axis=0)
    down = jnp.concatenate([f[2 * hidden :] for f in full], axis=0)

    my_dp = lax.axis_index("dp")
    my_expert = lax.axis_index("expert")
    slot_of = jnp.arange(groups * hidden, dtype=jnp.int32) // hidden
    expert_of = (((my_dp ^ (2 * slot_of)) * ring + my_expert) // 2).astype(jnp.int32)
    pick = (jnp.arange(capacity.shape[0], dtype=jnp.int32)[:, None] == expert_of[None, :]).astype(F32)

    def compute(x_part, c_part, coef_part):
        weight = tn(coef_part, pick, precision=lax.Precision.HIGHEST)
        gate_pre = nt(x_part, gate_t)
        up_pre = nt(x_part, up_t)
        back = nt(c_part, down) * weight
        sig = jax.nn.sigmoid(gate_pre)
        act = gate_pre * sig
        scaled_hidden = (act * up_pre * weight).astype(BF16)
        d_up = (back * act).astype(BF16)
        d_gate = (back * up_pre * (sig * (1.0 + gate_pre * (1.0 - sig)))).astype(BF16)
        out = jnp.dot(scaled_hidden, down, preferred_element_type=F32)
        grad = jnp.dot(d_gate, gate_t, preferred_element_type=F32) + jnp.dot(
            d_up, up_t, preferred_element_type=F32
        )
        return out, grad, tn(d_gate, x_part), tn(d_up, x_part), tn(scaled_hidden, c_part)

    all_tokens = x_all.shape[0]
    steps = max(1, all_tokens // 1024)
    if steps == 1:
        out, grad, gate_g, up_g, down_g = compute(x_all, c_all, coef_all)
    else:
        size = all_tokens // steps

        def step(carry, chunk):
            got = compute(*chunk)
            carry = tuple(a + b for a, b in zip(carry, got[2:]))
            return carry, (got[0].astype(BF16), got[1].astype(BF16))

        zero = jnp.zeros((groups * hidden, width), F32)
        chunks = (
            x_all.reshape(steps, size, width),
            c_all.reshape(steps, size, width),
            coef_all.reshape(-1, steps, size).swapaxes(0, 1),
        )
        (gate_g, up_g, down_g), (out, grad) = lax.scan(step, (zero, zero, zero), chunks)
        out = out.reshape(all_tokens, width).astype(F32)
        grad = grad.reshape(all_tokens, width).astype(F32)

    def collect(value):
        half = ring * token_count
        away = swap(value[half:].astype(BF16), dp_count, 1)
        mine = value[:half] + away.astype(F32)
        pieces = [mine[s * token_count : (s + 1) * token_count] for s in range(ring)]
        carry = pieces[ring - 1]
        for s in range(ring - 2, -1, -1):
            carry = pieces[s] + rotate(carry.astype(BF16), ring, -1).astype(F32)
        return carry.astype(BF16)

    parts = [
        jnp.concatenate([g[r * hidden : (r + 1) * hidden] for g in (gate_g, up_g, down_g)], axis=0)
        for r in range(groups)
    ]
    total_a = reduce_slots({r: parts[r][:cut] for r in range(groups)}, orders[0], dp_count)
    total_b = reduce_slots({r: parts[r][cut:] for r in range(groups)}, orders[1], dp_count)
    total = jnp.concatenate([total_a, total_b], axis=0).astype(BF16)
    return (
        collect(out),
        collect(grad),
        total[:hidden].T[None],
        total[hidden : 2 * hidden].T[None],
        total[2 * hidden :][None],
    )


def large_device(tokens, cotangent, expert_ids, gate_scores, hot_list, capacity, w_gate, w_up, w_down):
    dp_count = lax.axis_size("dp")
    ring = lax.axis_size("expert")
    groups = dp_count // 2
    bits = [1 << b for b in range(groups.bit_length() - 1)]
    orders = (bits, bits[::-1])
    token_count, width = tokens.shape
    hidden = w_gate.shape[2]
    rows = 3 * hidden
    cut = rows // 2
    packed = jnp.concatenate([w_gate[0].T, w_up[0].T, w_down[0]], axis=0)

    def spread(value):
        own = [value]
        for _ in range(ring - 1):
            own.append(rotate(own[-1], ring, 1))
        return own + [swap(v, dp_count, 1) for v in own]

    x_all = jnp.concatenate(spread(tokens), axis=0)
    c_all = jnp.concatenate(spread(cotangent), axis=0)
    coef = coefficients(expert_ids, gate_scores, hot_list, capacity)
    coef_all = jnp.concatenate(spread(coef), axis=1)

    first = gather_slots(packed[:cut], orders[0], dp_count)
    second = gather_slots(packed[cut:], orders[1], dp_count)
    full = [jnp.concatenate([first[r], second[r]], axis=0) for r in range(groups)]
    gate_t = jnp.concatenate([f[:hidden] for f in full], axis=0)
    up_t = jnp.concatenate([f[hidden : 2 * hidden] for f in full], axis=0)
    down = jnp.concatenate([f[2 * hidden :] for f in full], axis=0)

    my_dp = lax.axis_index("dp")
    my_expert = lax.axis_index("expert")
    slot_of = jnp.arange(groups * hidden, dtype=jnp.int32) // hidden
    expert_of = (((my_dp ^ (2 * slot_of)) * ring + my_expert) // 2).astype(jnp.int32)
    pick = (jnp.arange(capacity.shape[0], dtype=jnp.int32)[:, None] == expert_of[None, :]).astype(F32)

    def compute(x_part, c_part, coef_part):
        weight = tn(coef_part, pick, precision=lax.Precision.HIGHEST)
        gate_pre = nt(x_part, gate_t)
        up_pre = nt(x_part, up_t)
        back = nt(c_part, down) * weight
        sig = jax.nn.sigmoid(gate_pre)
        act = gate_pre * sig
        scaled_hidden = (act * up_pre * weight).astype(BF16)
        d_up = (back * act).astype(BF16)
        d_gate = (back * up_pre * (sig * (1.0 + gate_pre * (1.0 - sig)))).astype(BF16)
        out = jnp.dot(scaled_hidden, down, preferred_element_type=F32)
        grad = jnp.dot(d_gate, gate_t, preferred_element_type=F32) + jnp.dot(
            d_up, up_t, preferred_element_type=F32
        )
        return out, grad, tn(d_gate, x_part), tn(d_up, x_part), tn(scaled_hidden, c_part)

    all_tokens = x_all.shape[0]
    steps = max(1, all_tokens // 1024)
    if steps == 1:
        out, grad, gate_g, up_g, down_g = compute(x_all, c_all, coef_all)
    else:
        size = all_tokens // steps

        def step(carry, chunk):
            got = compute(*chunk)
            carry = tuple(a + b for a, b in zip(carry, got[2:]))
            return carry, (got[0].astype(BF16), got[1].astype(BF16))

        zero = jnp.zeros((groups * hidden, width), F32)
        chunks = (
            x_all.reshape(steps, size, width),
            c_all.reshape(steps, size, width),
            coef_all.reshape(-1, steps, size).swapaxes(0, 1),
        )
        (gate_g, up_g, down_g), (out, grad) = lax.scan(step, (zero, zero, zero), chunks)
        out = out.reshape(all_tokens, width).astype(F32)
        grad = grad.reshape(all_tokens, width).astype(F32)

    def collect(value):
        half = ring * token_count
        away = swap(value[half:].astype(BF16), dp_count, 1)
        mine = value[:half] + away.astype(F32)
        pieces = [mine[s * token_count : (s + 1) * token_count] for s in range(ring)]
        carry = pieces[ring - 1]
        for s in range(ring - 2, -1, -1):
            carry = pieces[s] + rotate(carry.astype(BF16), ring, -1).astype(F32)
        return carry.astype(BF16)

    parts = [
        jnp.concatenate([g[r * hidden : (r + 1) * hidden] for g in (gate_g, up_g, down_g)], axis=0)
        for r in range(groups)
    ]
    total_a = reduce_slots({r: parts[r][:cut] for r in range(groups)}, orders[0], dp_count)
    total_b = reduce_slots({r: parts[r][cut:] for r in range(groups)}, orders[1], dp_count)
    total = jnp.concatenate([total_a, total_b], axis=0).astype(BF16)
    return (
        collect(out),
        collect(grad),
        total[:hidden].T[None],
        total[hidden : 2 * hidden].T[None],
        total[2 * hidden :][None],
    )


LANES = 128


def staged(dp_count, ring):
    return dp_count == 8 and ring == 4


def prep_kernel(ids, gates, hot_list, capacity, tokens, out):
    size, width = tokens.shape
    out[:, :width] = tokens[...]
    shape = (1, size)
    gate_rows, present_rows, limits = [], [], []
    for x in range(capacity.shape[0]):
        match = ids[...] == x
        gate_rows.append(jnp.sum(jnp.where(match, gates[...], 0.0), axis=0, keepdims=True))
        present_rows.append(jnp.sum(match.astype(F32), axis=0, keepdims=True))
        limit = capacity[x]
        for h in range(hot_list.shape[0]):
            limit = jnp.where(hot_list[h] == x, size, limit)
        limits.append(jnp.full(shape, limit, jnp.int32).astype(F32))
    present = jnp.concatenate(present_rows, axis=0)
    before = lax.broadcasted_iota(jnp.int32, (size, size), 0) < lax.broadcasted_iota(
        jnp.int32, (size, size), 1
    )
    rank = jnp.dot(
        present.astype(BF16), before.astype(F32).astype(BF16), preferred_element_type=F32
    )
    kept = (present > 0.5) & (rank < jnp.concatenate(limits, axis=0))
    rest = jnp.where(kept, jnp.concatenate(gate_rows, axis=0), 0.0)
    parts = []
    for _ in range(3):
        part = rest.astype(BF16).astype(F32)
        parts.append(part)
        rest = rest - part
    fill = jnp.zeros((LANES - 3 * rest.shape[0], size), F32)
    out[:, width:] = jnp.concatenate([*parts, fill], axis=0).T.astype(BF16)


def act_block(coef, x_part, c_part, gates, ups, downs, slots, views):
    hidden = gates[0].shape[0]
    stack = jnp.concatenate([v[...] for v in (*gates, *ups)], axis=0)
    pre = nt(stack, x_part)
    back_all = nt(jnp.concatenate([d[...] for d in downs], axis=0), c_part)
    for i, (r, (scaled, d_gate, d_up)) in enumerate(zip(slots, views)):
        low, high = i * hidden, (i + len(slots)) * hidden
        weight = coef[r : r + 1]
        gate_pre = pre[low : low + hidden]
        up_pre = pre[high : high + hidden]
        sig = jax.nn.sigmoid(gate_pre)
        act = gate_pre * sig
        grad_hidden = back_all[low : low + hidden] * weight
        scaled[...] = (act * up_pre * weight).astype(BF16)
        d_up[...] = (grad_hidden * act).astype(BF16)
        d_gate[...] = (grad_hidden * up_pre * (sig * (1.0 + gate_pre * (1.0 - sig)))).astype(BF16)


def local_call(body, ins, outs, flops, after=None):
    whole = pl.BlockSpec(memory_space=pltpu.VMEM)
    specs = [whole] * len(ins)
    count = len(ins)
    if after is not None:
        ins = (*ins, after)
        specs = specs + [pl.BlockSpec(memory_space=pl.ANY)]

    def kernel(*refs):
        body(refs[:count], refs[len(ins) :])

    moved = sum(v.size * v.dtype.itemsize for v in (*ins, *outs))
    return pl.pallas_call(
        kernel,
        out_shape=list(outs),
        in_specs=specs,
        out_specs=[whole] * len(outs),
        compiler_params=pltpu.CompilerParams(vmem_limit_bytes=16 << 20),
        cost_estimate=pl.CostEstimate(flops=flops, bytes_accessed=moved, transcendentals=0),
    )(*ins)


def on_device(tokens, cotangent, expert_ids, gate_scores, hot_list, capacity, w_gate, w_up, w_down):
    dp_count = lax.axis_size("dp")
    ring = lax.axis_size("expert")
    groups = dp_count // 2
    size, width = tokens.shape
    experts = capacity.shape[0]
    if not staged(dp_count, ring):
        return large_device(
            tokens, cotangent, expert_ids, gate_scores, hot_list, capacity, w_gate, w_up, w_down
        )
    hidden = w_gate.shape[2]
    half = hidden // 2
    cut = hidden + half
    pair = 2 * size
    total = ring * pair
    last = ring - 1
    shape = jax.ShapeDtypeStruct

    gate0, up0, down0 = w_gate[0].T, w_up[0].T, w_down[0]
    gate1, up2 = swap(gate0, dp_count, 2), swap(up0, dp_count, 4)
    down1, down2 = swap(down0, dp_count, 2), swap(down0, dp_count, 4)
    up1, gate2 = swap(up0, dp_count, 2), swap(gate0, dp_count, 4)
    gate3, up3 = swap(gate1, dp_count, 4), swap(up2, dp_count, 2)

    vmem, smem = pl.BlockSpec(memory_space=pltpu.VMEM), pl.BlockSpec(memory_space=pltpu.SMEM)
    tokens = pl.pallas_call(
        prep_kernel,
        out_shape=shape((size, width + LANES), BF16),
        in_specs=[vmem, vmem, smem, smem, vmem],
        out_specs=vmem,
        compiler_params=pltpu.CompilerParams(vmem_limit_bytes=4 << 20),
        cost_estimate=pl.CostEstimate(flops=1 << 20, bytes_accessed=1 << 19, transcendentals=0),
        name="prep",
    )(expert_ids.T, gate_scores.T, hot_list, capacity, tokens)

    def spread(value):
        own = [value]
        for _ in range(1, ring):
            own.append(rotate(own[-1], ring, 1))
        return [(v, swap(v, dp_count, 1)) for v in own]

    cots, toks = spread(cotangent), spread(tokens)
    late1, late2, _ = lax.optimization_barrier((down1, down2, toks[last - 1][0]))
    low3 = swap(late1[:half], dp_count, 4)
    high3 = swap(late2[half:], dp_count, 2)
    gates = (gate0, gate1, gate2, gate3)
    ups = (up0, up1, up2, up3)
    downs = ((down0,), (down1,), (down2,), (low3, high3))
    slot = jnp.arange(8, dtype=jnp.int32)
    expert_of = ((lax.axis_index("dp") ^ (2 * slot)) * ring + lax.axis_index("expert")) // 2
    lane = jnp.arange(LANES, dtype=jnp.int32)
    lane = jnp.where(lane < 3 * experts, lane % experts, -1)
    pick = (expert_of[:, None] == lane[None, :]).astype(BF16)

    def flat(pairs):
        return [v for p in pairs for v in p]

    def block_of(refs, s):
        count = (len(refs) - 1) // 2
        t, c = refs[1 + 2 * s : 3 + 2 * s], refs[1 + count + 2 * s : 3 + count + 2 * s]
        x_part = jnp.concatenate([v[:, :width] for v in t], axis=0)
        extra = jnp.concatenate([v[:, width:] for v in t], axis=0)
        return nt(refs[0][...], extra), x_part, jnp.concatenate([v[...] for v in c], axis=0)

    def views_of(outs, slots, columns):
        return [
            [o.at[pl.ds(j * hidden, hidden), columns] for o in outs] for j in range(len(slots))
        ]

    near = (0, 1, 2)
    main_in = [pick, *flat(toks[:last]), *flat(cots[:last])]
    near_in = [*gates[:3], *ups[:3], *flat(downs[:3])]

    def main_body(refs, outs):
        g, u, d = (refs[len(main_in) + 3 * i : len(main_in) + 3 * i + 3] for i in range(3))
        for s in range(last):
            block = block_of(refs[: len(main_in)], s)
            act_block(*block, g, u, d, near, views_of(outs, near, pl.ds(s * pair, pair)))

    main = local_call(
        main_body,
        (*main_in, *near_in),
        [shape((3 * hidden, last * pair), BF16)] * 3,
        18 * hidden * last * pair * width,
    )

    def out_block(acts, g, u, d, outs):
        scaled, d_gate, d_up = acts
        out = tn(scaled, jnp.concatenate([v[...] for v in d], axis=0))
        outs[0][...] = out[:size]
        outs[2][:size] = out[size:].astype(BF16)
        both = jnp.concatenate([v[...] for v in (*g, *u)], axis=0)
        grad = tn(jnp.concatenate([d_gate, d_up], axis=0), both)
        outs[1][...] = grad[:size]
        outs[2][size:] = grad[size:].astype(BF16)

    weights_in = [*gates, *ups, *flat(downs)]
    out_shapes = [shape((size, width), F32)] * 2 + [shape((pair, width), BF16)]
    all_in = [pick, *flat(toks), *flat(cots)]

    def middle_body(refs, outs):
        rest = refs[len(all_in) :]
        g, u, d = rest[:groups], rest[groups : 2 * groups], rest[2 * groups :]
        tail_refs, diag_refs = outs[:3], outs[3:6]
        every = tuple(range(groups))
        whole = pl.ds(0, pair)
        final = pl.ds(last * pair, pair)
        views = views_of(tail_refs, near, whole) + views_of(diag_refs, (3,), final)
        act_block(*block_of(refs[: len(all_in)], last), g, u, d, every, views)
        for s in range(last):
            views = views_of(diag_refs, (3,), pl.ds(s * pair, pair))
            block = block_of(refs[: len(all_in)], s)
            act_block(*block, g[3:], u[3:], d[3:], (3,), views)
        acts = [
            jnp.concatenate([t[...], v[:, final]], axis=0) for t, v in zip(tail_refs, diag_refs)
        ]
        out_block(acts, g, u, d, outs[6:])

    got = local_call(
        middle_body,
        (*all_in, *weights_in),
        [shape((3 * hidden, pair), BF16)] * 3 + [shape((hidden, total), BF16)] * 3 + out_shapes,
        12 * groups * hidden * pair * width + 6 * hidden * last * pair * width,
        after=main[0],
    )
    tail, diag, part = got[:3], got[3:6], {last: got[6:]}

    def weight_parts(slots, types, diag, after):
        acts = list(diag) if diag else [*main, *tail]
        ins = acts + flat(toks) + flat(cots)
        count = len(acts)

        def body(refs, outs):
            x_all = jnp.concatenate([v[:, :width] for v in refs[count : count + 2 * ring]], axis=0)
            c_all = jnp.concatenate([v[...] for v in refs[count + 2 * ring :]], axis=0)
            acts = [[], [], []]
            for r in slots:
                rows = pl.ds(0 if diag else r * hidden, hidden)
                for k in range(3):
                    value = refs[k][rows]
                    if not diag:
                        value = jnp.concatenate([value, refs[k + 3][rows]], axis=1)
                    acts[k].append(value)
            down_g = jnp.dot(
                jnp.concatenate(acts[0], axis=0), c_all, preferred_element_type=F32
            )
            both_g = jnp.dot(
                jnp.concatenate([*acts[1], *acts[2]], axis=0), x_all, preferred_element_type=F32
            )
            for i in range(len(slots)):
                first, second = outs[2 * i], outs[2 * i + 1]
                low, high = i * hidden, (i + len(slots)) * hidden
                first[hidden:] = down_g[low : low + half].astype(first.dtype)
                second[hidden:] = down_g[low + half : low + hidden].astype(second.dtype)
                first[:hidden] = both_g[low : low + hidden].astype(first.dtype)
                second[:hidden] = both_g[high : high + hidden].astype(second.dtype)

        out = [shape((cut, width), t) for t in types]
        flops = 6 * len(slots) * hidden * total * width
        return local_call(body, ins, out, flops, after)

    first1, second1, first2, second2 = weight_parts(
        (1, 2), (BF16, F32, F32, BF16), None, part[last][0]
    )

    def outputs(s, after):
        acts = [*main, *diag]

        def body(refs, outs):
            rest = refs[6:]
            g, u, d = rest[:groups], rest[groups : 2 * groups], rest[2 * groups :]
            block = pl.ds(s * pair, pair)
            acts = [
                jnp.concatenate([refs[k][:, block], refs[k + 3][:, block]], axis=0)
                for k in range(3)
            ]
            out_block(acts, g, u, d, outs)

        flops = 6 * groups * hidden * pair * width
        return local_call(body, (*acts, *weights_in), out_shapes, flops, after)

    first3, second3 = weight_parts((3,), (BF16, BF16), diag, first1)
    a1, b2 = swap(first1, dp_count, 2), swap(second2, dp_count, 4)
    a3, b3 = swap(first3, dp_count, 2), swap(second3, dp_count, 4)
    after = first3
    for s in range(last - 1, -1, -1):
        part[s] = outputs(s, after)
        after = part[s][0]
    first0, second0 = weight_parts((0,), (F32, F32), None, after)

    def add(s, i, away, moved):
        rows = pl.ds(i * size, size)

        def body(refs, outs):
            value = refs[0][...] + refs[1][rows].astype(F32)
            if moved is not None:
                value = value + refs[2][...].astype(F32)
            outs[0][...] = value.astype(BF16)

        ins = (part[s][i], away) if moved is None else (part[s][i], away, moved)
        return local_call(body, ins, [shape((size, width), BF16)], 1 << 18)[0]

    away = {s: swap(part[s][2], dp_count, 1) for s in part}
    carry = [None, None]
    for s in range(last, -1, -1):
        if s < last:
            carry = [rotate(c, ring, -1) for c in carry]
        carry = [add(s, i, away[s], carry[i]) for i in range(2)]
    mixed, token_grad = carry

    a2 = swap((first2 + a3.astype(F32)).astype(BF16), dp_count, 4)
    b1 = swap((second1 + b3.astype(F32)).astype(BF16), dp_count, 2)

    def finish(refs, outs):
        first = refs[0][...] + refs[2][...].astype(F32) + refs[3][...].astype(F32)
        second = refs[1][...] + refs[4][...].astype(F32) + refs[5][...].astype(F32)
        outs[0][...] = first[:hidden].astype(BF16)
        outs[1][...] = second[:hidden].astype(BF16)
        outs[2][:half] = first[hidden:].astype(BF16)
        outs[2][half:] = second[hidden:].astype(BF16)

    gate_g, up_g, down_g = local_call(
        finish, (first0, second0, a1, a2, b2, b1), [shape((hidden, width), BF16)] * 3, 1 << 20
    )
    return mixed, token_grad, gate_g.T[None], up_g.T[None], down_g[None]


def solution(mesh):
    rows = P(("dp", "expert"), None)
    weights = P(("dp", "expert"), None, None)
    return jax.shard_map(
        on_device,
        mesh=mesh,
        in_specs=(rows, rows, rows, rows, P(), P(), weights, weights, weights),
        out_specs=(rows, rows, weights, weights, weights),
        check_vma=False,
    )
```

```python
import jax
import jax.numpy as jnp
from jax import lax
from jax.experimental import pallas as pl
from jax.experimental.pallas import tpu as pltpu
from jax.sharding import PartitionSpec as P


F32 = jnp.float32
BF16 = jnp.bfloat16


def swap(value, count, mask):
    return lax.ppermute(value, "dp", [(i, i ^ mask) for i in range(count)])


def rotate(value, count, step):
    return lax.ppermute(value, "expert", [(i, (i + step) % count) for i in range(count)])


def nt(left, right):
    return lax.dot_general(left, right, (((1,), (1,)), ((), ())), preferred_element_type=F32)


def tn(left, right, **kw):
    return lax.dot_general(left, right, (((0,), (0,)), ((), ())), preferred_element_type=F32, **kw)


def coefficients(expert_ids, gate_scores, hot_list, capacity):
    count = capacity.shape[0]
    tokens = expert_ids.shape[0]
    iota = jnp.arange(count, dtype=jnp.int32)
    match = expert_ids.T[:, None, :] == iota[None, :, None]
    gates = jnp.sum(jnp.where(match, gate_scores.T[:, None, :], 0.0), axis=0)
    present = jnp.any(match, axis=0)
    order = jnp.arange(tokens, dtype=jnp.int32)
    before = (order[:, None] < order[None, :]).astype(BF16)
    rank = jnp.dot(present.astype(BF16), before, preferred_element_type=F32)
    hot = jnp.any(iota[:, None] == hot_list[None, :], axis=1)
    kept = present & (hot[:, None] | (rank < capacity[:, None].astype(F32)))
    return jnp.where(kept, gates, 0.0)


def gather_slots(own, order, dp_count):
    slots = {0: own}
    for bit in order:
        slots.update({r | bit: swap(v, dp_count, 2 * bit) for r, v in list(slots.items())})
    return slots


def reduce_slots(parts, order, dp_count):
    parts = dict(parts)
    for bit in order:
        moved = {r: swap(parts[r].astype(BF16), dp_count, 2 * bit) for r in parts if r & bit}
        parts = {
            r: v.astype(F32) + moved[r | bit].astype(F32) for r, v in parts.items() if not r & bit
        }
    return parts[0]


def large_device(tokens, cotangent, expert_ids, gate_scores, hot_list, capacity, w_gate, w_up, w_down):
    dp_count = lax.axis_size("dp")
    ring = lax.axis_size("expert")
    groups = dp_count // 2
    bits = [1 << b for b in range(groups.bit_length() - 1)]
    orders = (bits, bits[::-1])
    token_count, width = tokens.shape
    hidden = w_gate.shape[2]
    rows = 3 * hidden
    cut = rows // 2
    packed = jnp.concatenate([w_gate[0].T, w_up[0].T, w_down[0]], axis=0)

    def spread(value):
        own = [value]
        for _ in range(ring - 1):
            own.append(rotate(own[-1], ring, 1))
        return own + [swap(v, dp_count, 1) for v in own]

    x_all = jnp.concatenate(spread(tokens), axis=0)
    c_all = jnp.concatenate(spread(cotangent), axis=0)
    coef = coefficients(expert_ids, gate_scores, hot_list, capacity)
    coef_all = jnp.concatenate(spread(coef), axis=1)

    first = gather_slots(packed[:cut], orders[0], dp_count)
    second = gather_slots(packed[cut:], orders[1], dp_count)
    full = [jnp.concatenate([first[r], second[r]], axis=0) for r in range(groups)]
    gate_t = jnp.concatenate([f[:hidden] for f in full], axis=0)
    up_t = jnp.concatenate([f[hidden : 2 * hidden] for f in full], axis=0)
    down = jnp.concatenate([f[2 * hidden :] for f in full], axis=0)

    my_dp = lax.axis_index("dp")
    my_expert = lax.axis_index("expert")
    slot_of = jnp.arange(groups * hidden, dtype=jnp.int32) // hidden
    expert_of = (((my_dp ^ (2 * slot_of)) * ring + my_expert) // 2).astype(jnp.int32)
    pick = (jnp.arange(capacity.shape[0], dtype=jnp.int32)[:, None] == expert_of[None, :]).astype(F32)

    def compute(x_part, c_part, coef_part):
        weight = tn(coef_part, pick, precision=lax.Precision.HIGHEST)
        gate_pre = nt(x_part, gate_t)
        up_pre = nt(x_part, up_t)
        back = nt(c_part, down) * weight
        sig = jax.nn.sigmoid(gate_pre)
        act = gate_pre * sig
        scaled_hidden = (act * up_pre * weight).astype(BF16)
        d_up = (back * act).astype(BF16)
        d_gate = (back * up_pre * (sig * (1.0 + gate_pre * (1.0 - sig)))).astype(BF16)
        out = jnp.dot(scaled_hidden, down, preferred_element_type=F32)
        grad = jnp.dot(d_gate, gate_t, preferred_element_type=F32) + jnp.dot(
            d_up, up_t, preferred_element_type=F32
        )
        return out, grad, tn(d_gate, x_part), tn(d_up, x_part), tn(scaled_hidden, c_part)

    all_tokens = x_all.shape[0]
    steps = max(1, all_tokens // 1024)
    if steps == 1:
        out, grad, gate_g, up_g, down_g = compute(x_all, c_all, coef_all)
    else:
        size = all_tokens // steps

        def step(carry, chunk):
            got = compute(*chunk)
            carry = tuple(a + b for a, b in zip(carry, got[2:]))
            return carry, (got[0].astype(BF16), got[1].astype(BF16))

        zero = jnp.zeros((groups * hidden, width), F32)
        chunks = (
            x_all.reshape(steps, size, width),
            c_all.reshape(steps, size, width),
            coef_all.reshape(-1, steps, size).swapaxes(0, 1),
        )
        (gate_g, up_g, down_g), (out, grad) = lax.scan(step, (zero, zero, zero), chunks)
        out = out.reshape(all_tokens, width).astype(F32)
        grad = grad.reshape(all_tokens, width).astype(F32)

    def collect(value):
        half = ring * token_count
        away = swap(value[half:].astype(BF16), dp_count, 1)
        mine = value[:half] + away.astype(F32)
        pieces = [mine[s * token_count : (s + 1) * token_count] for s in range(ring)]
        carry = pieces[ring - 1]
        for s in range(ring - 2, -1, -1):
            carry = pieces[s] + rotate(carry.astype(BF16), ring, -1).astype(F32)
        return carry.astype(BF16)

    parts = [
        jnp.concatenate([g[r * hidden : (r + 1) * hidden] for g in (gate_g, up_g, down_g)], axis=0)
        for r in range(groups)
    ]
    total_a = reduce_slots({r: parts[r][:cut] for r in range(groups)}, orders[0], dp_count)
    total_b = reduce_slots({r: parts[r][cut:] for r in range(groups)}, orders[1], dp_count)
    total = jnp.concatenate([total_a, total_b], axis=0).astype(BF16)
    return (
        collect(out),
        collect(grad),
        total[:hidden].T[None],
        total[hidden : 2 * hidden].T[None],
        total[2 * hidden :][None],
    )


def large_device(tokens, cotangent, expert_ids, gate_scores, hot_list, capacity, w_gate, w_up, w_down):
    dp_count = lax.axis_size("dp")
    ring = lax.axis_size("expert")
    groups = dp_count // 2
    bits = [1 << b for b in range(groups.bit_length() - 1)]
    orders = (bits, bits[::-1])
    token_count, width = tokens.shape
    hidden = w_gate.shape[2]
    rows = 3 * hidden
    cut = rows // 2
    packed = jnp.concatenate([w_gate[0].T, w_up[0].T, w_down[0]], axis=0)

    def spread(value):
        own = [value]
        for _ in range(ring - 1):
            own.append(rotate(own[-1], ring, 1))
        return own + [swap(v, dp_count, 1) for v in own]

    x_all = jnp.concatenate(spread(tokens), axis=0)
    c_all = jnp.concatenate(spread(cotangent), axis=0)
    coef = coefficients(expert_ids, gate_scores, hot_list, capacity)
    coef_all = jnp.concatenate(spread(coef), axis=1)

    first = gather_slots(packed[:cut], orders[0], dp_count)
    second = gather_slots(packed[cut:], orders[1], dp_count)
    full = [jnp.concatenate([first[r], second[r]], axis=0) for r in range(groups)]
    gate_t = jnp.concatenate([f[:hidden] for f in full], axis=0)
    up_t = jnp.concatenate([f[hidden : 2 * hidden] for f in full], axis=0)
    down = jnp.concatenate([f[2 * hidden :] for f in full], axis=0)

    my_dp = lax.axis_index("dp")
    my_expert = lax.axis_index("expert")
    slot_of = jnp.arange(groups * hidden, dtype=jnp.int32) // hidden
    expert_of = (((my_dp ^ (2 * slot_of)) * ring + my_expert) // 2).astype(jnp.int32)
    pick = (jnp.arange(capacity.shape[0], dtype=jnp.int32)[:, None] == expert_of[None, :]).astype(F32)

    def compute(x_part, c_part, coef_part):
        weight = tn(coef_part, pick, precision=lax.Precision.HIGHEST)
        gate_pre = nt(x_part, gate_t)
        up_pre = nt(x_part, up_t)
        back = nt(c_part, down) * weight
        sig = jax.nn.sigmoid(gate_pre)
        act = gate_pre * sig
        scaled_hidden = (act * up_pre * weight).astype(BF16)
        d_up = (back * act).astype(BF16)
        d_gate = (back * up_pre * (sig * (1.0 + gate_pre * (1.0 - sig)))).astype(BF16)
        out = jnp.dot(scaled_hidden, down, preferred_element_type=F32)
        grad = jnp.dot(d_gate, gate_t, preferred_element_type=F32) + jnp.dot(
            d_up, up_t, preferred_element_type=F32
        )
        return out, grad, tn(d_gate, x_part), tn(d_up, x_part), tn(scaled_hidden, c_part)

    all_tokens = x_all.shape[0]
    steps = max(1, all_tokens // 1024)
    if steps == 1:
        out, grad, gate_g, up_g, down_g = compute(x_all, c_all, coef_all)
    else:
        size = all_tokens // steps

        def step(carry, chunk):
            got = compute(*chunk)
            carry = tuple(a + b for a, b in zip(carry, got[2:]))
            return carry, (got[0].astype(BF16), got[1].astype(BF16))

        zero = jnp.zeros((groups * hidden, width), F32)
        chunks = (
            x_all.reshape(steps, size, width),
            c_all.reshape(steps, size, width),
            coef_all.reshape(-1, steps, size).swapaxes(0, 1),
        )
        (gate_g, up_g, down_g), (out, grad) = lax.scan(step, (zero, zero, zero), chunks)
        out = out.reshape(all_tokens, width).astype(F32)
        grad = grad.reshape(all_tokens, width).astype(F32)

    def collect(value):
        half = ring * token_count
        away = swap(value[half:].astype(BF16), dp_count, 1)
        mine = value[:half] + away.astype(F32)
        pieces = [mine[s * token_count : (s + 1) * token_count] for s in range(ring)]
        carry = pieces[ring - 1]
        for s in range(ring - 2, -1, -1):
            carry = pieces[s] + rotate(carry.astype(BF16), ring, -1).astype(F32)
        return carry.astype(BF16)

    parts = [
        jnp.concatenate([g[r * hidden : (r + 1) * hidden] for g in (gate_g, up_g, down_g)], axis=0)
        for r in range(groups)
    ]
    total_a = reduce_slots({r: parts[r][:cut] for r in range(groups)}, orders[0], dp_count)
    total_b = reduce_slots({r: parts[r][cut:] for r in range(groups)}, orders[1], dp_count)
    total = jnp.concatenate([total_a, total_b], axis=0).astype(BF16)
    return (
        collect(out),
        collect(grad),
        total[:hidden].T[None],
        total[hidden : 2 * hidden].T[None],
        total[2 * hidden :][None],
    )


LANES = 128


def staged(dp_count, ring):
    return dp_count == 8 and ring == 4


def prep_kernel(*refs):
    sources, out, held, sems = refs[:5], refs[5], refs[6:11], refs[11]
    copies = [
        pltpu.make_async_copy(source, target, sems.at[i])
        for i, (source, target) in enumerate(zip(sources, held))
    ]
    for copy in copies:
        copy.start()
    for copy in copies:
        copy.wait()
    ids, gates, hot_list, capacity, tokens = held
    size, width = tokens.shape
    out[:, :width] = tokens[...]
    shape = (1, size)
    gate_rows, present_rows, limits = [], [], []
    for x in range(capacity.shape[0]):
        match = ids[...] == x
        gate_rows.append(jnp.sum(jnp.where(match, gates[...], 0.0), axis=0, keepdims=True))
        present_rows.append(jnp.sum(match.astype(F32), axis=0, keepdims=True))
        limit = capacity[x]
        for h in range(hot_list.shape[0]):
            limit = jnp.where(hot_list[h] == x, size, limit)
        limits.append(jnp.full(shape, limit, jnp.int32).astype(F32))
    present = jnp.concatenate(present_rows, axis=0)
    before = lax.broadcasted_iota(jnp.int32, (size, size), 0) < lax.broadcasted_iota(
        jnp.int32, (size, size), 1
    )
    rank = jnp.dot(
        present.astype(BF16), before.astype(F32).astype(BF16), preferred_element_type=F32
    )
    kept = (present > 0.5) & (rank < jnp.concatenate(limits, axis=0))
    rest = jnp.where(kept, jnp.concatenate(gate_rows, axis=0), 0.0)
    parts = []
    for _ in range(3):
        part = rest.astype(BF16).astype(F32)
        parts.append(part)
        rest = rest - part
    fill = jnp.zeros((LANES - 3 * rest.shape[0], size), F32)
    out[:, width:] = jnp.concatenate([*parts, fill], axis=0).T.astype(BF16)


def act_block(coef, x_part, c_part, gates, ups, downs, slots, views):
    hidden = gates[0].shape[0]
    stack = jnp.concatenate([v[...] for v in (*gates, *ups)], axis=0)
    pre = nt(stack, x_part)
    back_all = nt(jnp.concatenate([d[...] for d in downs], axis=0), c_part)
    for i, (r, (scaled, d_gate, d_up)) in enumerate(zip(slots, views)):
        low, high = i * hidden, (i + len(slots)) * hidden
        weight = coef[r : r + 1]
        gate_pre = pre[low : low + hidden]
        up_pre = pre[high : high + hidden]
        sig = jax.nn.sigmoid(gate_pre)
        act = gate_pre * sig
        grad_hidden = back_all[low : low + hidden] * weight
        scaled[...] = (act * up_pre * weight).astype(BF16)
        d_up[...] = (grad_hidden * act).astype(BF16)
        d_gate[...] = (grad_hidden * up_pre * (sig * (1.0 + gate_pre * (1.0 - sig)))).astype(BF16)


def local_call(body, ins, outs, flops, after=None):
    whole = pl.BlockSpec(memory_space=pltpu.VMEM)
    specs = [whole] * len(ins)
    count = len(ins)
    if after is not None:
        ins = (*ins, after)
        specs = specs + [pl.BlockSpec(memory_space=pl.ANY)]

    def kernel(*refs):
        body(refs[:count], refs[len(ins) :])

    moved = sum(v.size * v.dtype.itemsize for v in (*ins, *outs))
    return pl.pallas_call(
        kernel,
        out_shape=list(outs),
        in_specs=specs,
        out_specs=[whole] * len(outs),
        compiler_params=pltpu.CompilerParams(vmem_limit_bytes=16 << 20),
        cost_estimate=pl.CostEstimate(flops=flops, bytes_accessed=moved, transcendentals=0),
    )(*ins)


def on_device(tokens, cotangent, expert_ids, gate_scores, hot_list, capacity, w_gate, w_up, w_down):
    dp_count = lax.axis_size("dp")
    ring = lax.axis_size("expert")
    groups = dp_count // 2
    size, width = tokens.shape
    experts = capacity.shape[0]
    if not staged(dp_count, ring):
        return large_device(
            tokens, cotangent, expert_ids, gate_scores, hot_list, capacity, w_gate, w_up, w_down
        )
    hidden = w_gate.shape[2]
    half = hidden // 2
    cut = hidden + half
    pair = 2 * size
    total = ring * pair
    last = ring - 1
    shape = jax.ShapeDtypeStruct

    gate0, up0, down0 = w_gate[0].T, w_up[0].T, w_down[0]
    gate1, up2 = swap(gate0, dp_count, 2), swap(up0, dp_count, 4)
    down1, down2 = swap(down0, dp_count, 2), swap(down0, dp_count, 4)
    up1, gate2 = swap(up0, dp_count, 2), swap(gate0, dp_count, 4)
    gate3, up3 = swap(gate1, dp_count, 4), swap(up2, dp_count, 2)

    hbm = pl.BlockSpec(memory_space=pltpu.HBM)
    prep_in = (expert_ids.T, gate_scores.T, hot_list, capacity, tokens)
    spaces = (pltpu.VMEM, pltpu.VMEM, pltpu.SMEM, pltpu.SMEM, pltpu.VMEM)
    tokens = pl.pallas_call(
        prep_kernel,
        out_shape=shape((size, width + LANES), BF16),
        in_specs=[hbm] * 5,
        out_specs=pl.BlockSpec(memory_space=pltpu.VMEM),
        scratch_shapes=[
            *[space(v.shape, v.dtype) for space, v in zip(spaces, prep_in)],
            pltpu.SemaphoreType.DMA((5,)),
        ],
        compiler_params=pltpu.CompilerParams(vmem_limit_bytes=60 << 20),
        cost_estimate=pl.CostEstimate(flops=1 << 20, bytes_accessed=1 << 19, transcendentals=0),
        name="prep",
    )(*prep_in)

    def spread(value):
        own = [value]
        for _ in range(1, ring):
            own.append(rotate(own[-1], ring, 1))
        return [(v, swap(v, dp_count, 1)) for v in own]

    cots, toks = spread(cotangent), spread(tokens)
    late1, late2, _ = lax.optimization_barrier((down1, down2, toks[last - 1][0]))
    low3 = swap(late1[:half], dp_count, 4)
    high3 = swap(late2[half:], dp_count, 2)
    gates = (gate0, gate1, gate2, gate3)
    ups = (up0, up1, up2, up3)
    downs = ((down0,), (down1,), (down2,), (low3, high3))
    slot = jnp.arange(8, dtype=jnp.int32)
    expert_of = ((lax.axis_index("dp") ^ (2 * slot)) * ring + lax.axis_index("expert")) // 2
    lane = jnp.arange(LANES, dtype=jnp.int32)
    lane = jnp.where(lane < 3 * experts, lane % experts, -1)
    pick = (expert_of[:, None] == lane[None, :]).astype(BF16)

    def flat(pairs):
        return [v for p in pairs for v in p]

    def block_of(refs, s):
        count = (len(refs) - 1) // 2
        t, c = refs[1 + 2 * s : 3 + 2 * s], refs[1 + count + 2 * s : 3 + count + 2 * s]
        x_part = jnp.concatenate([v[:, :width] for v in t], axis=0)
        extra = jnp.concatenate([v[:, width:] for v in t], axis=0)
        return nt(refs[0][...], extra), x_part, jnp.concatenate([v[...] for v in c], axis=0)

    def views_of(outs, slots, columns):
        return [
            [o.at[pl.ds(j * hidden, hidden), columns] for o in outs] for j in range(len(slots))
        ]

    near = (0, 1, 2)
    main_in = [pick, *flat(toks[:last]), *flat(cots[:last])]
    near_in = [*gates[:3], *ups[:3], *flat(downs[:3])]

    def main_body(refs, outs):
        g, u, d = (refs[len(main_in) + 3 * i : len(main_in) + 3 * i + 3] for i in range(3))
        for s in range(last):
            block = block_of(refs[: len(main_in)], s)
            act_block(*block, g, u, d, near, views_of(outs, near, pl.ds(s * pair, pair)))

    main = local_call(
        main_body,
        (*main_in, *near_in),
        [shape((3 * hidden, last * pair), BF16)] * 3,
        18 * hidden * last * pair * width,
    )

    def out_block(acts, g, u, d, outs):
        scaled, d_gate, d_up = acts
        out = tn(scaled, jnp.concatenate([v[...] for v in d], axis=0))
        outs[0][...] = out[:size]
        outs[2][:size] = out[size:].astype(BF16)
        both = jnp.concatenate([v[...] for v in (*g, *u)], axis=0)
        grad = tn(jnp.concatenate([d_gate, d_up], axis=0), both)
        outs[1][...] = grad[:size]
        outs[2][size:] = grad[size:].astype(BF16)

    weights_in = [*gates, *ups, *flat(downs)]
    out_shapes = [shape((size, width), F32)] * 2 + [shape((pair, width), BF16)]
    all_in = [pick, *flat(toks), *flat(cots)]

    def grad_block(slots, acts, refs, outs):
        count = len(refs) // 2
        x_all = jnp.concatenate([v[:, :width] for v in refs[:count]], axis=0)
        c_all = jnp.concatenate([v[...] for v in refs[count:]], axis=0)
        down_g = jnp.dot(acts[0], c_all, preferred_element_type=F32)
        both = jnp.concatenate([acts[1], acts[2]], axis=0)
        both_g = jnp.dot(both, x_all, preferred_element_type=F32)
        for i in range(slots):
            first, second = outs[2 * i], outs[2 * i + 1]
            low, high = i * hidden, (i + slots) * hidden
            first[hidden:] = down_g[low : low + half].astype(first.dtype)
            second[hidden:] = down_g[low + half : low + hidden].astype(second.dtype)
            first[:hidden] = both_g[low : low + hidden].astype(first.dtype)
            second[:hidden] = both_g[high : high + hidden].astype(second.dtype)

    def near_body(refs, outs):
        rest = refs[len(all_in) :]
        g, u, d = (rest[3 * i : 3 * i + 3] for i in range(3))
        block = block_of(refs[: len(all_in)], last)
        act_block(*block, g, u, d, near, views_of(outs[:3], near, pl.ds(0, pair)))
        rows = pl.ds(hidden, 2 * hidden)
        acts = [
            jnp.concatenate([m[rows], t[rows]], axis=1) for m, t in zip(rest[9:], outs[:3])
        ]
        grad_block(2, acts, refs[1 : len(all_in)], outs[3:])

    part_shapes = [shape((cut, width), t) for t in (BF16, F32, F32, BF16)]
    got = local_call(
        near_body,
        (*all_in, *near_in, *main),
        [shape((3 * hidden, pair), BF16)] * 3 + part_shapes,
        18 * hidden * pair * width + 12 * hidden * total * width,
    )
    tail, (first1, second1, first2, second2) = got[:3], got[3:]

    def middle_body(refs, outs):
        rest = refs[len(all_in) :]
        g, u, d = rest[:groups], rest[groups : 2 * groups], rest[2 * groups : -3]
        diag_refs = outs[:3]
        for s in range(ring):
            views = views_of(diag_refs, (3,), pl.ds(s * pair, pair))
            block = block_of(refs[: len(all_in)], s)
            act_block(*block, g[3:], u[3:], d[3:], (3,), views)
        final = pl.ds(last * pair, pair)
        acts = [jnp.concatenate([t[...], v[:, final]], axis=0) for t, v in zip(rest[-3:], diag_refs)]
        out_block(acts, g, u, d, outs[3:])

    got = local_call(
        middle_body,
        (*all_in, *weights_in, *tail),
        [shape((hidden, total), BF16)] * 3 + out_shapes,
        6 * groups * hidden * pair * width + 6 * hidden * total * width,
        after=first1,
    )
    diag, part = got[:3], {last: got[3:]}

    def weight_parts(r, types, after):
        acts = [*diag] if r == 3 else [*main, *tail]

        def body(refs, outs):
            if r == 3:
                acts_in = [v[...] for v in refs[:3]]
            else:
                rows = pl.ds(r * hidden, hidden)
                acts_in = [
                    jnp.concatenate([refs[k][rows], refs[k + 3][rows]], axis=1) for k in range(3)
                ]
            grad_block(1, acts_in, refs[len(acts) :], outs)

        ins = (*acts, *flat(toks), *flat(cots))
        out = [shape((cut, width), t) for t in types]
        return local_call(body, ins, out, 6 * hidden * total * width, after)

    def outputs(s, after):
        acts = [*main, *diag]

        def body(refs, outs):
            rest = refs[6:]
            g, u, d = rest[:groups], rest[groups : 2 * groups], rest[2 * groups :]
            block = pl.ds(s * pair, pair)
            acts = [
                jnp.concatenate([refs[k][:, block], refs[k + 3][:, block]], axis=0)
                for k in range(3)
            ]
            out_block(acts, g, u, d, outs)

        flops = 6 * groups * hidden * pair * width
        return local_call(body, (*acts, *weights_in), out_shapes, flops, after)

    first3, second3 = weight_parts(3, (BF16, BF16), part[last][0])
    a1, b2 = swap(first1, dp_count, 2), swap(second2, dp_count, 4)
    a3, b3 = swap(first3, dp_count, 2), swap(second3, dp_count, 4)
    after = first3
    for s in range(last - 1, -1, -1):
        part[s] = outputs(s, after)
        after = part[s][0]
    first0, second0 = weight_parts(0, (F32, F32), after)

    def add(s, i, away, moved):
        rows = pl.ds(i * size, size)

        def body(refs, outs):
            value = refs[0][...] + refs[1][rows].astype(F32)
            if moved is not None:
                value = value + refs[2][...].astype(F32)
            outs[0][...] = value.astype(BF16)

        ins = (part[s][i], away) if moved is None else (part[s][i], away, moved)
        return local_call(body, ins, [shape((size, width), BF16)], 1 << 18)[0]

    away = {s: swap(part[s][2], dp_count, 1) for s in part}
    carry = [None, None]
    for s in range(last, -1, -1):
        if s < last:
            carry = [rotate(c, ring, -1) for c in carry]
        carry = [add(s, i, away[s], carry[i]) for i in range(2)]
    mixed, token_grad = carry

    a2 = swap((first2 + a3.astype(F32)).astype(BF16), dp_count, 4)
    b1 = swap((second1 + b3.astype(F32)).astype(BF16), dp_count, 2)

    def finish(refs, outs):
        first = refs[0][...] + refs[2][...].astype(F32) + refs[3][...].astype(F32)
        second = refs[1][...] + refs[4][...].astype(F32) + refs[5][...].astype(F32)
        outs[0][...] = first[:hidden].astype(BF16)
        outs[1][...] = second[:hidden].astype(BF16)
        outs[2][:half] = first[hidden:].astype(BF16)
        outs[2][half:] = second[hidden:].astype(BF16)

    gate_g, up_g, down_g = local_call(
        finish, (first0, second0, a1, a2, b2, b1), [shape((hidden, width), BF16)] * 3, 1 << 20
    )
    return mixed, token_grad, gate_g.T[None], up_g.T[None], down_g[None]


def solution(mesh):
    rows = P(("dp", "expert"), None)
    weights = P(("dp", "expert"), None, None)
    return jax.shard_map(
        on_device,
        mesh=mesh,
        in_specs=(rows, rows, rows, rows, P(), P(), weights, weights, weights),
        out_specs=(rows, rows, weights, weights, weights),
        check_vma=False,
    )
```

```python
import jax
import jax.numpy as jnp
from jax import lax
from jax.experimental import pallas as pl
from jax.experimental.pallas import tpu as pltpu
from jax.sharding import PartitionSpec as P


F32 = jnp.float32
BF16 = jnp.bfloat16


def swap(value, count, mask):
    return lax.ppermute(value, "dp", [(i, i ^ mask) for i in range(count)])


def rotate(value, count, step):
    ring = [*range(0, count, 2), *range(count - 1 - count % 2, 0, -2)]
    pairs = [(ring[i], ring[(i + step) % count]) for i in range(count)]
    return lax.ppermute(value, "expert", sorted(pairs))


def nt(left, right):
    return lax.dot_general(left, right, (((1,), (1,)), ((), ())), preferred_element_type=F32)


def tn(left, right, **kw):
    return lax.dot_general(left, right, (((0,), (0,)), ((), ())), preferred_element_type=F32, **kw)


def coefficients(expert_ids, gate_scores, hot_list, capacity):
    count = capacity.shape[0]
    tokens = expert_ids.shape[0]
    iota = jnp.arange(count, dtype=jnp.int32)
    match = expert_ids.T[:, None, :] == iota[None, :, None]
    gates = jnp.sum(jnp.where(match, gate_scores.T[:, None, :], 0.0), axis=0)
    present = jnp.any(match, axis=0)
    order = jnp.arange(tokens, dtype=jnp.int32)
    before = (order[:, None] < order[None, :]).astype(BF16)
    rank = jnp.dot(present.astype(BF16), before, preferred_element_type=F32)
    hot = jnp.any(iota[:, None] == hot_list[None, :], axis=1)
    kept = present & (hot[:, None] | (rank < capacity[:, None].astype(F32)))
    return jnp.where(kept, gates, 0.0)


def gather_slots(own, order, dp_count):
    slots = {0: own}
    for bit in order:
        slots.update({r | bit: swap(v, dp_count, 2 * bit) for r, v in list(slots.items())})
    return slots


def reduce_slots(parts, order, dp_count):
    parts = dict(parts)
    for bit in order:
        moved = {r: swap(parts[r].astype(BF16), dp_count, 2 * bit) for r in parts if r & bit}
        parts = {
            r: v.astype(F32) + moved[r | bit].astype(F32) for r, v in parts.items() if not r & bit
        }
    return parts[0]


def large_device(tokens, cotangent, expert_ids, gate_scores, hot_list, capacity, w_gate, w_up, w_down):
    dp_count = lax.axis_size("dp")
    ring = lax.axis_size("expert")
    groups = dp_count // 2
    bits = [1 << b for b in range(groups.bit_length() - 1)]
    orders = (bits, bits[::-1])
    token_count, width = tokens.shape
    hidden = w_gate.shape[2]
    rows = 3 * hidden
    cut = rows // 2
    packed = jnp.concatenate([w_gate[0].T, w_up[0].T, w_down[0]], axis=0)

    def spread(value):
        own = [value]
        for _ in range(ring - 1):
            own.append(rotate(own[-1], ring, 1))
        return own + [swap(v, dp_count, 1) for v in own]

    x_all = jnp.concatenate(spread(tokens), axis=0)
    c_all = jnp.concatenate(spread(cotangent), axis=0)
    coef = coefficients(expert_ids, gate_scores, hot_list, capacity)
    coef_all = jnp.concatenate(spread(coef), axis=1)

    first = gather_slots(packed[:cut], orders[0], dp_count)
    second = gather_slots(packed[cut:], orders[1], dp_count)
    full = [jnp.concatenate([first[r], second[r]], axis=0) for r in range(groups)]
    gate_t = jnp.concatenate([f[:hidden] for f in full], axis=0)
    up_t = jnp.concatenate([f[hidden : 2 * hidden] for f in full], axis=0)
    down = jnp.concatenate([f[2 * hidden :] for f in full], axis=0)

    my_dp = lax.axis_index("dp")
    my_expert = lax.axis_index("expert")
    slot_of = jnp.arange(groups * hidden, dtype=jnp.int32) // hidden
    expert_of = (((my_dp ^ (2 * slot_of)) * ring + my_expert) // 2).astype(jnp.int32)
    pick = (jnp.arange(capacity.shape[0], dtype=jnp.int32)[:, None] == expert_of[None, :]).astype(F32)

    def compute(x_part, c_part, coef_part):
        weight = tn(coef_part, pick, precision=lax.Precision.HIGHEST)
        gate_pre = nt(x_part, gate_t)
        up_pre = nt(x_part, up_t)
        back = nt(c_part, down) * weight
        sig = jax.nn.sigmoid(gate_pre)
        act = gate_pre * sig
        scaled_hidden = (act * up_pre * weight).astype(BF16)
        d_up = (back * act).astype(BF16)
        d_gate = (back * up_pre * (sig * (1.0 + gate_pre * (1.0 - sig)))).astype(BF16)
        out = jnp.dot(scaled_hidden, down, preferred_element_type=F32)
        grad = jnp.dot(d_gate, gate_t, preferred_element_type=F32) + jnp.dot(
            d_up, up_t, preferred_element_type=F32
        )
        return out, grad, tn(d_gate, x_part), tn(d_up, x_part), tn(scaled_hidden, c_part)

    all_tokens = x_all.shape[0]
    steps = max(1, all_tokens // 1024)
    if steps == 1:
        out, grad, gate_g, up_g, down_g = compute(x_all, c_all, coef_all)
    else:
        size = all_tokens // steps

        def step(carry, chunk):
            got = compute(*chunk)
            carry = tuple(a + b for a, b in zip(carry, got[2:]))
            return carry, (got[0].astype(BF16), got[1].astype(BF16))

        zero = jnp.zeros((groups * hidden, width), F32)
        chunks = (
            x_all.reshape(steps, size, width),
            c_all.reshape(steps, size, width),
            coef_all.reshape(-1, steps, size).swapaxes(0, 1),
        )
        (gate_g, up_g, down_g), (out, grad) = lax.scan(step, (zero, zero, zero), chunks)
        out = out.reshape(all_tokens, width).astype(F32)
        grad = grad.reshape(all_tokens, width).astype(F32)

    def collect(value):
        half = ring * token_count
        away = swap(value[half:].astype(BF16), dp_count, 1)
        mine = value[:half] + away.astype(F32)
        pieces = [mine[s * token_count : (s + 1) * token_count] for s in range(ring)]
        carry = pieces[ring - 1]
        for s in range(ring - 2, -1, -1):
            carry = pieces[s] + rotate(carry.astype(BF16), ring, -1).astype(F32)
        return carry.astype(BF16)

    parts = [
        jnp.concatenate([g[r * hidden : (r + 1) * hidden] for g in (gate_g, up_g, down_g)], axis=0)
        for r in range(groups)
    ]
    total_a = reduce_slots({r: parts[r][:cut] for r in range(groups)}, orders[0], dp_count)
    total_b = reduce_slots({r: parts[r][cut:] for r in range(groups)}, orders[1], dp_count)
    total = jnp.concatenate([total_a, total_b], axis=0).astype(BF16)
    return (
        collect(out),
        collect(grad),
        total[:hidden].T[None],
        total[hidden : 2 * hidden].T[None],
        total[2 * hidden :][None],
    )


def large_device(tokens, cotangent, expert_ids, gate_scores, hot_list, capacity, w_gate, w_up, w_down):
    dp_count = lax.axis_size("dp")
    ring = lax.axis_size("expert")
    groups = dp_count // 2
    bits = [1 << b for b in range(groups.bit_length() - 1)]
    orders = (bits, bits[::-1])
    token_count, width = tokens.shape
    hidden = w_gate.shape[2]
    rows = 3 * hidden
    cut = rows // 2
    packed = jnp.concatenate([w_gate[0].T, w_up[0].T, w_down[0]], axis=0)

    def spread(value):
        own = [value]
        for _ in range(ring - 1):
            own.append(rotate(own[-1], ring, 1))
        return own + [swap(v, dp_count, 1) for v in own]

    x_all = jnp.concatenate(spread(tokens), axis=0)
    c_all = jnp.concatenate(spread(cotangent), axis=0)
    coef = coefficients(expert_ids, gate_scores, hot_list, capacity)
    coef_all = jnp.concatenate(spread(coef), axis=1)

    first = gather_slots(packed[:cut], orders[0], dp_count)
    second = gather_slots(packed[cut:], orders[1], dp_count)
    full = [jnp.concatenate([first[r], second[r]], axis=0) for r in range(groups)]
    gate_t = jnp.concatenate([f[:hidden] for f in full], axis=0)
    up_t = jnp.concatenate([f[hidden : 2 * hidden] for f in full], axis=0)
    down = jnp.concatenate([f[2 * hidden :] for f in full], axis=0)

    my_dp = lax.axis_index("dp")
    my_expert = lax.axis_index("expert")
    slot_of = jnp.arange(groups * hidden, dtype=jnp.int32) // hidden
    expert_of = (((my_dp ^ (2 * slot_of)) * ring + my_expert) // 2).astype(jnp.int32)
    pick = (jnp.arange(capacity.shape[0], dtype=jnp.int32)[:, None] == expert_of[None, :]).astype(F32)

    def compute(x_part, c_part, coef_part):
        weight = tn(coef_part, pick, precision=lax.Precision.HIGHEST)
        gate_pre = nt(x_part, gate_t)
        up_pre = nt(x_part, up_t)
        back = nt(c_part, down) * weight
        sig = jax.nn.sigmoid(gate_pre)
        act = gate_pre * sig
        scaled_hidden = (act * up_pre * weight).astype(BF16)
        d_up = (back * act).astype(BF16)
        d_gate = (back * up_pre * (sig * (1.0 + gate_pre * (1.0 - sig)))).astype(BF16)
        out = jnp.dot(scaled_hidden, down, preferred_element_type=F32)
        grad = jnp.dot(d_gate, gate_t, preferred_element_type=F32) + jnp.dot(
            d_up, up_t, preferred_element_type=F32
        )
        return out, grad, tn(d_gate, x_part), tn(d_up, x_part), tn(scaled_hidden, c_part)

    all_tokens = x_all.shape[0]
    steps = max(1, all_tokens // 1024)
    if steps == 1:
        out, grad, gate_g, up_g, down_g = compute(x_all, c_all, coef_all)
    else:
        size = all_tokens // steps

        def step(carry, chunk):
            got = compute(*chunk)
            carry = tuple(a + b for a, b in zip(carry, got[2:]))
            return carry, (got[0].astype(BF16), got[1].astype(BF16))

        zero = jnp.zeros((groups * hidden, width), F32)
        chunks = (
            x_all.reshape(steps, size, width),
            c_all.reshape(steps, size, width),
            coef_all.reshape(-1, steps, size).swapaxes(0, 1),
        )
        (gate_g, up_g, down_g), (out, grad) = lax.scan(step, (zero, zero, zero), chunks)
        out = out.reshape(all_tokens, width).astype(F32)
        grad = grad.reshape(all_tokens, width).astype(F32)

    def collect(value):
        half = ring * token_count
        away = swap(value[half:].astype(BF16), dp_count, 1)
        mine = value[:half] + away.astype(F32)
        pieces = [mine[s * token_count : (s + 1) * token_count] for s in range(ring)]
        carry = pieces[ring - 1]
        for s in range(ring - 2, -1, -1):
            carry = pieces[s] + rotate(carry.astype(BF16), ring, -1).astype(F32)
        return carry.astype(BF16)

    parts = [
        jnp.concatenate([g[r * hidden : (r + 1) * hidden] for g in (gate_g, up_g, down_g)], axis=0)
        for r in range(groups)
    ]
    total_a = reduce_slots({r: parts[r][:cut] for r in range(groups)}, orders[0], dp_count)
    total_b = reduce_slots({r: parts[r][cut:] for r in range(groups)}, orders[1], dp_count)
    total = jnp.concatenate([total_a, total_b], axis=0).astype(BF16)
    return (
        collect(out),
        collect(grad),
        total[:hidden].T[None],
        total[hidden : 2 * hidden].T[None],
        total[2 * hidden :][None],
    )


LANES = 128


def staged(dp_count, ring):
    return dp_count == 8 and ring == 4


def prep_kernel(*refs):
    sources, out, held, sems = refs[:5], refs[5], refs[6:11], refs[11]
    copies = [
        pltpu.make_async_copy(source, target, sems.at[i])
        for i, (source, target) in enumerate(zip(sources, held))
    ]
    for copy in copies:
        copy.start()
    for copy in copies:
        copy.wait()
    ids, gates, hot_list, capacity, tokens = held
    size, width = tokens.shape
    out[:, :width] = tokens[...]
    shape = (1, size)
    gate_rows, present_rows, limits = [], [], []
    for x in range(capacity.shape[0]):
        match = ids[...] == x
        gate_rows.append(jnp.sum(jnp.where(match, gates[...], 0.0), axis=0, keepdims=True))
        present_rows.append(jnp.sum(match.astype(F32), axis=0, keepdims=True))
        limit = capacity[x]
        for h in range(hot_list.shape[0]):
            limit = jnp.where(hot_list[h] == x, size, limit)
        limits.append(jnp.full(shape, limit, jnp.int32).astype(F32))
    present = jnp.concatenate(present_rows, axis=0)
    before = lax.broadcasted_iota(jnp.int32, (size, size), 0) < lax.broadcasted_iota(
        jnp.int32, (size, size), 1
    )
    rank = jnp.dot(
        present.astype(BF16), before.astype(F32).astype(BF16), preferred_element_type=F32
    )
    kept = (present > 0.5) & (rank < jnp.concatenate(limits, axis=0))
    rest = jnp.where(kept, jnp.concatenate(gate_rows, axis=0), 0.0)
    parts = []
    for _ in range(3):
        part = rest.astype(BF16).astype(F32)
        parts.append(part)
        rest = rest - part
    fill = jnp.zeros((LANES - 3 * rest.shape[0], size), F32)
    out[:, width:] = jnp.concatenate([*parts, fill], axis=0).T.astype(BF16)


def act_block(coef, x_part, c_part, gates, ups, downs, slots, views):
    hidden = gates[0].shape[0]
    stack = jnp.concatenate([v[...] for v in (*gates, *ups)], axis=0)
    pre = nt(stack, x_part)
    back_all = nt(jnp.concatenate([d[...] for d in downs], axis=0), c_part)
    for i, (r, (scaled, d_gate, d_up)) in enumerate(zip(slots, views)):
        low, high = i * hidden, (i + len(slots)) * hidden
        weight = coef[r : r + 1]
        gate_pre = pre[low : low + hidden]
        up_pre = pre[high : high + hidden]
        sig = jax.nn.sigmoid(gate_pre)
        act = gate_pre * sig
        grad_hidden = back_all[low : low + hidden] * weight
        scaled[...] = (act * up_pre * weight).astype(BF16)
        d_up[...] = (grad_hidden * act).astype(BF16)
        d_gate[...] = (grad_hidden * up_pre * (sig * (1.0 + gate_pre * (1.0 - sig)))).astype(BF16)


def local_call(body, ins, outs, flops, after=None):
    whole = pl.BlockSpec(memory_space=pltpu.VMEM)
    specs = [whole] * len(ins)
    count = len(ins)
    if after is not None:
        ins = (*ins, after)
        specs = specs + [pl.BlockSpec(memory_space=pl.ANY)]

    def kernel(*refs):
        body(refs[:count], refs[len(ins) :])

    moved = sum(v.size * v.dtype.itemsize for v in (*ins, *outs))
    return pl.pallas_call(
        kernel,
        out_shape=list(outs),
        in_specs=specs,
        out_specs=[whole] * len(outs),
        compiler_params=pltpu.CompilerParams(vmem_limit_bytes=16 << 20),
        cost_estimate=pl.CostEstimate(flops=flops, bytes_accessed=moved, transcendentals=0),
    )(*ins)


def on_device(tokens, cotangent, expert_ids, gate_scores, hot_list, capacity, w_gate, w_up, w_down):
    dp_count = lax.axis_size("dp")
    ring = lax.axis_size("expert")
    groups = dp_count // 2
    size, width = tokens.shape
    experts = capacity.shape[0]
    if not staged(dp_count, ring):
        return large_device(
            tokens, cotangent, expert_ids, gate_scores, hot_list, capacity, w_gate, w_up, w_down
        )
    hidden = w_gate.shape[2]
    half = hidden // 2
    cut = hidden + half
    pair = 2 * size
    total = ring * pair
    last = ring - 1
    shape = jax.ShapeDtypeStruct

    gate0, up0, down0 = w_gate[0].T, w_up[0].T, w_down[0]
    gate1, up2 = swap(gate0, dp_count, 2), swap(up0, dp_count, 4)
    down1, down2 = swap(down0, dp_count, 2), swap(down0, dp_count, 4)
    up1, gate2 = swap(up0, dp_count, 2), swap(gate0, dp_count, 4)
    gate3, up3 = swap(gate1, dp_count, 4), swap(up2, dp_count, 2)

    hbm = pl.BlockSpec(memory_space=pltpu.HBM)
    prep_in = (expert_ids.T, gate_scores.T, hot_list, capacity, tokens)
    spaces = (pltpu.VMEM, pltpu.VMEM, pltpu.SMEM, pltpu.SMEM, pltpu.VMEM)
    tokens = pl.pallas_call(
        prep_kernel,
        out_shape=shape((size, width + LANES), BF16),
        in_specs=[hbm] * 5,
        out_specs=pl.BlockSpec(memory_space=pltpu.VMEM),
        scratch_shapes=[
            *[space(v.shape, v.dtype) for space, v in zip(spaces, prep_in)],
            pltpu.SemaphoreType.DMA((5,)),
        ],
        compiler_params=pltpu.CompilerParams(vmem_limit_bytes=60 << 20),
        cost_estimate=pl.CostEstimate(flops=1 << 20, bytes_accessed=1 << 19, transcendentals=0),
        name="prep",
    )(*prep_in)

    def spread(value):
        own = [value]
        for _ in range(1, ring):
            own.append(rotate(own[-1], ring, 1))
        return [(v, swap(v, dp_count, 1)) for v in own]

    cots, toks = spread(cotangent), spread(tokens)
    late1, late2, _ = lax.optimization_barrier((down1, down2, toks[last - 1][0]))
    low3 = swap(late1[:half], dp_count, 4)
    high3 = swap(late2[half:], dp_count, 2)
    gates = (gate0, gate1, gate2, gate3)
    ups = (up0, up1, up2, up3)
    downs = ((down0,), (down1,), (down2,), (low3, high3))
    slot = jnp.arange(8, dtype=jnp.int32)
    expert_of = ((lax.axis_index("dp") ^ (2 * slot)) * ring + lax.axis_index("expert")) // 2
    lane = jnp.arange(LANES, dtype=jnp.int32)
    lane = jnp.where(lane < 3 * experts, lane % experts, -1)
    pick = (expert_of[:, None] == lane[None, :]).astype(BF16)

    def flat(pairs):
        return [v for p in pairs for v in p]

    def block_of(refs, s):
        count = (len(refs) - 1) // 2
        t, c = refs[1 + 2 * s : 3 + 2 * s], refs[1 + count + 2 * s : 3 + count + 2 * s]
        x_part = jnp.concatenate([v[:, :width] for v in t], axis=0)
        extra = jnp.concatenate([v[:, width:] for v in t], axis=0)
        return nt(refs[0][...], extra), x_part, jnp.concatenate([v[...] for v in c], axis=0)

    def views_of(outs, slots, columns):
        return [
            [o.at[pl.ds(j * hidden, hidden), columns] for o in outs] for j in range(len(slots))
        ]

    near = (0, 1, 2)
    main_in = [pick, *flat(toks[:last]), *flat(cots[:last])]
    near_in = [*gates[:3], *ups[:3], *flat(downs[:3])]

    def main_body(refs, outs):
        g, u, d = (refs[len(main_in) + 3 * i : len(main_in) + 3 * i + 3] for i in range(3))
        for s in range(last):
            block = block_of(refs[: len(main_in)], s)
            act_block(*block, g, u, d, near, views_of(outs, near, pl.ds(s * pair, pair)))

    main = local_call(
        main_body,
        (*main_in, *near_in),
        [shape((3 * hidden, last * pair), BF16)] * 3,
        18 * hidden * last * pair * width,
    )

    def out_block(acts, g, u, d, outs):
        scaled, d_gate, d_up = acts
        out = tn(scaled, jnp.concatenate([v[...] for v in d], axis=0))
        outs[0][...] = out[:size]
        outs[2][:size] = out[size:].astype(BF16)
        both = jnp.concatenate([v[...] for v in (*g, *u)], axis=0)
        grad = tn(jnp.concatenate([d_gate, d_up], axis=0), both)
        outs[1][...] = grad[:size]
        outs[2][size:] = grad[size:].astype(BF16)

    weights_in = [*gates, *ups, *flat(downs)]
    out_shapes = [shape((size, width), F32)] * 2 + [shape((pair, width), BF16)]
    all_in = [pick, *flat(toks), *flat(cots)]

    def grad_block(slots, acts, refs, outs):
        count = len(refs) // 2
        x_all = jnp.concatenate([v[:, :width] for v in refs[:count]], axis=0)
        c_all = jnp.concatenate([v[...] for v in refs[count:]], axis=0)
        down_g = jnp.dot(acts[0], c_all, preferred_element_type=F32)
        both = jnp.concatenate([acts[1], acts[2]], axis=0)
        both_g = jnp.dot(both, x_all, preferred_element_type=F32)
        for i in range(slots):
            first, second = outs[2 * i], outs[2 * i + 1]
            low, high = i * hidden, (i + slots) * hidden
            first[hidden:] = down_g[low : low + half].astype(first.dtype)
            second[hidden:] = down_g[low + half : low + hidden].astype(second.dtype)
            first[:hidden] = both_g[low : low + hidden].astype(first.dtype)
            second[:hidden] = both_g[high : high + hidden].astype(second.dtype)

    def near_body(refs, outs):
        rest = refs[len(all_in) :]
        g, u, d = (rest[3 * i : 3 * i + 3] for i in range(3))
        block = block_of(refs[: len(all_in)], last)
        act_block(*block, g, u, d, near, views_of(outs[:3], near, pl.ds(0, pair)))
        rows = pl.ds(hidden, 2 * hidden)
        acts = [
            jnp.concatenate([m[rows], t[rows]], axis=1) for m, t in zip(rest[9:], outs[:3])
        ]
        grad_block(2, acts, refs[1 : len(all_in)], outs[3:])

    part_shapes = [shape((cut, width), t) for t in (BF16, F32, F32, BF16)]
    got = local_call(
        near_body,
        (*all_in, *near_in, *main),
        [shape((3 * hidden, pair), BF16)] * 3 + part_shapes,
        18 * hidden * pair * width + 12 * hidden * total * width,
    )
    tail, (first1, second1, first2, second2) = got[:3], got[3:]

    far_in = [gates[3], ups[3], *downs[3]]

    def middle_body(refs, outs):
        rest = refs[len(all_in) :]
        g, u, d = rest[:groups], rest[groups : 2 * groups], rest[2 * groups : -3]
        diag_refs = outs[:3]
        views = views_of(diag_refs, (3,), pl.ds(0, pair))
        block = block_of(refs[: len(all_in)], last)
        act_block(*block, g[3:], u[3:], d[3:], (3,), views)
        acts = [jnp.concatenate([t[...], v[...]], axis=0) for t, v in zip(rest[-3:], diag_refs)]
        out_block(acts, g, u, d, outs[3:])

    got = local_call(
        middle_body,
        (*all_in, *weights_in, *tail),
        [shape((hidden, pair), BF16)] * 3 + out_shapes,
        6 * groups * hidden * pair * width + 6 * hidden * pair * width,
        after=first1,
    )
    diag_last, part = got[:3], {last: got[3:]}

    def far_body(refs, outs):
        rest = refs[len(all_in) :]
        for s in range(last):
            views = views_of(outs[:3], (3,), pl.ds(s * pair, pair))
            block = block_of(refs[: len(all_in)], s)
            act_block(*block, rest[:1], rest[1:2], rest[2:-3], (3,), views)
        acts = [jnp.concatenate([v[...], t[...]], axis=1) for v, t in zip(outs[:3], rest[-3:])]
        grad_block(1, acts, refs[1 : len(all_in)], outs[3:])

    got = local_call(
        far_body,
        (*all_in, *far_in, *diag_last),
        [shape((hidden, last * pair), BF16)] * 3 + [shape((cut, width), BF16)] * 2,
        12 * hidden * total * width,
    )
    diag, (first3, second3) = got[:3], got[3:]

    def own_body(refs, outs):
        rows = pl.ds(0, hidden)
        acts = [jnp.concatenate([refs[k][rows], refs[k + 3][rows]], axis=1) for k in range(3)]
        grad_block(1, acts, refs[6:], outs)

    def outputs(s, after):
        acts = [*main, *diag]

        def body(refs, outs):
            rest = refs[6:]
            g, u, d = rest[:groups], rest[groups : 2 * groups], rest[2 * groups :]
            block = pl.ds(s * pair, pair)
            acts = [
                jnp.concatenate([refs[k][:, block], refs[k + 3][:, block]], axis=0)
                for k in range(3)
            ]
            out_block(acts, g, u, d, outs)

        flops = 6 * groups * hidden * pair * width
        return local_call(body, (*acts, *weights_in), out_shapes, flops, after)

    a1, b2 = swap(first1, dp_count, 2), swap(second2, dp_count, 4)
    a3, b3 = swap(first3, dp_count, 2), swap(second3, dp_count, 4)
    after = first3
    for s in range(last - 1, -1, -1):
        part[s] = outputs(s, after)
        after = part[s][0]
    first0, second0 = local_call(
        own_body,
        (*main, *tail, *flat(toks), *flat(cots)),
        [shape((cut, width), F32)] * 2,
        6 * hidden * total * width,
        after,
    )

    def add(s, i, away, moved):
        rows = pl.ds(i * size, size)

        def body(refs, outs):
            value = refs[0][...] + refs[1][rows].astype(F32)
            if moved is not None:
                value = value + refs[2][...].astype(F32)
            outs[0][...] = value.astype(BF16)

        ins = (part[s][i], away) if moved is None else (part[s][i], away, moved)
        return local_call(body, ins, [shape((size, width), BF16)], 1 << 18)[0]

    away = {s: swap(part[s][2], dp_count, 1) for s in part}
    carry = [None, None]
    for s in range(last, -1, -1):
        if s < last:
            carry = [rotate(c, ring, -1) for c in carry]
        carry = [add(s, i, away[s], carry[i]) for i in range(2)]
    mixed, token_grad = carry

    a2 = swap((first2 + a3.astype(F32)).astype(BF16), dp_count, 4)
    b1 = swap((second1 + b3.astype(F32)).astype(BF16), dp_count, 2)

    def finish(refs, outs):
        first = refs[0][...] + refs[2][...].astype(F32) + refs[3][...].astype(F32)
        second = refs[1][...] + refs[4][...].astype(F32) + refs[5][...].astype(F32)
        outs[0][...] = first[:hidden].astype(BF16)
        outs[1][...] = second[:hidden].astype(BF16)
        outs[2][:half] = first[hidden:].astype(BF16)
        outs[2][half:] = second[hidden:].astype(BF16)

    gate_g, up_g, down_g = local_call(
        finish, (first0, second0, a1, a2, b2, b1), [shape((hidden, width), BF16)] * 3, 1 << 20
    )
    return mixed, token_grad, gate_g.T[None], up_g.T[None], down_g[None]


def solution(mesh):
    rows = P(("dp", "expert"), None)
    weights = P(("dp", "expert"), None, None)
    return jax.shard_map(
        on_device,
        mesh=mesh,
        in_specs=(rows, rows, rows, rows, P(), P(), weights, weights, weights),
        out_specs=(rows, rows, weights, weights, weights),
        check_vma=False,
    )
```

```python
import jax
import jax.numpy as jnp
from jax import lax
from jax.experimental import pallas as pl
from jax.experimental.pallas import tpu as pltpu
from jax.sharding import PartitionSpec as P


F32 = jnp.float32
BF16 = jnp.bfloat16


def swap(value, count, mask):
    return lax.ppermute(value, "dp", [(i, i ^ mask) for i in range(count)])


def rotate(value, count, step):
    ring = [*range(0, count, 2), *range(count - 1 - count % 2, 0, -2)]
    pairs = [(ring[i], ring[(i + step) % count]) for i in range(count)]
    return lax.ppermute(value, "expert", sorted(pairs))


def nt(left, right):
    return lax.dot_general(left, right, (((1,), (1,)), ((), ())), preferred_element_type=F32)


def tn(left, right, **kw):
    return lax.dot_general(left, right, (((0,), (0,)), ((), ())), preferred_element_type=F32, **kw)


def coefficients(expert_ids, gate_scores, hot_list, capacity):
    count = capacity.shape[0]
    tokens = expert_ids.shape[0]
    iota = jnp.arange(count, dtype=jnp.int32)
    match = expert_ids.T[:, None, :] == iota[None, :, None]
    gates = jnp.sum(jnp.where(match, gate_scores.T[:, None, :], 0.0), axis=0)
    present = jnp.any(match, axis=0)
    order = jnp.arange(tokens, dtype=jnp.int32)
    before = (order[:, None] < order[None, :]).astype(BF16)
    rank = jnp.dot(present.astype(BF16), before, preferred_element_type=F32)
    hot = jnp.any(iota[:, None] == hot_list[None, :], axis=1)
    kept = present & (hot[:, None] | (rank < capacity[:, None].astype(F32)))
    return jnp.where(kept, gates, 0.0)


def gather_slots(own, order, dp_count):
    slots = {0: own}
    for bit in order:
        slots.update({r | bit: swap(v, dp_count, 2 * bit) for r, v in list(slots.items())})
    return slots


def reduce_slots(parts, order, dp_count):
    parts = dict(parts)
    for bit in order:
        moved = {r: swap(parts[r].astype(BF16), dp_count, 2 * bit) for r in parts if r & bit}
        parts = {
            r: v.astype(F32) + moved[r | bit].astype(F32) for r, v in parts.items() if not r & bit
        }
    return parts[0]


def large_device(tokens, cotangent, expert_ids, gate_scores, hot_list, capacity, w_gate, w_up, w_down):
    dp_count = lax.axis_size("dp")
    ring = lax.axis_size("expert")
    groups = dp_count // 2
    bits = [1 << b for b in range(groups.bit_length() - 1)]
    orders = (bits, bits[::-1])
    token_count, width = tokens.shape
    hidden = w_gate.shape[2]
    rows = 3 * hidden
    cut = rows // 2
    packed = jnp.concatenate([w_gate[0].T, w_up[0].T, w_down[0]], axis=0)

    def spread(value):
        own = [value]
        for _ in range(ring - 1):
            own.append(rotate(own[-1], ring, 1))
        return own + [swap(v, dp_count, 1) for v in own]

    x_all = jnp.concatenate(spread(tokens), axis=0)
    c_all = jnp.concatenate(spread(cotangent), axis=0)
    coef = coefficients(expert_ids, gate_scores, hot_list, capacity)
    coef_all = jnp.concatenate(spread(coef), axis=1)

    first = gather_slots(packed[:cut], orders[0], dp_count)
    second = gather_slots(packed[cut:], orders[1], dp_count)
    full = [jnp.concatenate([first[r], second[r]], axis=0) for r in range(groups)]
    gate_t = jnp.concatenate([f[:hidden] for f in full], axis=0)
    up_t = jnp.concatenate([f[hidden : 2 * hidden] for f in full], axis=0)
    down = jnp.concatenate([f[2 * hidden :] for f in full], axis=0)

    my_dp = lax.axis_index("dp")
    my_expert = lax.axis_index("expert")
    slot_of = jnp.arange(groups * hidden, dtype=jnp.int32) // hidden
    expert_of = (((my_dp ^ (2 * slot_of)) * ring + my_expert) // 2).astype(jnp.int32)
    pick = (jnp.arange(capacity.shape[0], dtype=jnp.int32)[:, None] == expert_of[None, :]).astype(F32)

    def compute(x_part, c_part, coef_part):
        weight = tn(coef_part, pick, precision=lax.Precision.HIGHEST)
        gate_pre = nt(x_part, gate_t)
        up_pre = nt(x_part, up_t)
        back = nt(c_part, down) * weight
        sig = jax.nn.sigmoid(gate_pre)
        act = gate_pre * sig
        scaled_hidden = (act * up_pre * weight).astype(BF16)
        d_up = (back * act).astype(BF16)
        d_gate = (back * up_pre * (sig * (1.0 + gate_pre * (1.0 - sig)))).astype(BF16)
        out = jnp.dot(scaled_hidden, down, preferred_element_type=F32)
        grad = jnp.dot(d_gate, gate_t, preferred_element_type=F32) + jnp.dot(
            d_up, up_t, preferred_element_type=F32
        )
        return out, grad, tn(d_gate, x_part), tn(d_up, x_part), tn(scaled_hidden, c_part)

    all_tokens = x_all.shape[0]
    steps = max(1, all_tokens // 1024)
    if steps == 1:
        out, grad, gate_g, up_g, down_g = compute(x_all, c_all, coef_all)
    else:
        size = all_tokens // steps

        def step(carry, chunk):
            got = compute(*chunk)
            carry = tuple(a + b for a, b in zip(carry, got[2:]))
            return carry, (got[0].astype(BF16), got[1].astype(BF16))

        zero = jnp.zeros((groups * hidden, width), F32)
        chunks = (
            x_all.reshape(steps, size, width),
            c_all.reshape(steps, size, width),
            coef_all.reshape(-1, steps, size).swapaxes(0, 1),
        )
        (gate_g, up_g, down_g), (out, grad) = lax.scan(step, (zero, zero, zero), chunks)
        out = out.reshape(all_tokens, width).astype(F32)
        grad = grad.reshape(all_tokens, width).astype(F32)

    def collect(value):
        half = ring * token_count
        away = swap(value[half:].astype(BF16), dp_count, 1)
        mine = value[:half] + away.astype(F32)
        pieces = [mine[s * token_count : (s + 1) * token_count] for s in range(ring)]
        carry = pieces[ring - 1]
        for s in range(ring - 2, -1, -1):
            carry = pieces[s] + rotate(carry.astype(BF16), ring, -1).astype(F32)
        return carry.astype(BF16)

    parts = [
        jnp.concatenate([g[r * hidden : (r + 1) * hidden] for g in (gate_g, up_g, down_g)], axis=0)
        for r in range(groups)
    ]
    total_a = reduce_slots({r: parts[r][:cut] for r in range(groups)}, orders[0], dp_count)
    total_b = reduce_slots({r: parts[r][cut:] for r in range(groups)}, orders[1], dp_count)
    total = jnp.concatenate([total_a, total_b], axis=0).astype(BF16)
    return (
        collect(out),
        collect(grad),
        total[:hidden].T[None],
        total[hidden : 2 * hidden].T[None],
        total[2 * hidden :][None],
    )


def large_device(tokens, cotangent, expert_ids, gate_scores, hot_list, capacity, w_gate, w_up, w_down):
    dp_count = lax.axis_size("dp")
    ring = lax.axis_size("expert")
    groups = dp_count // 2
    bits = [1 << b for b in range(groups.bit_length() - 1)]
    orders = (bits, bits[::-1])
    token_count, width = tokens.shape
    hidden = w_gate.shape[2]
    rows = 3 * hidden
    cut = rows // 2
    packed = jnp.concatenate([w_gate[0].T, w_up[0].T, w_down[0]], axis=0)

    def spread(value):
        own = [value]
        for _ in range(ring - 1):
            own.append(rotate(own[-1], ring, 1))
        return own + [swap(v, dp_count, 1) for v in own]

    x_all = jnp.concatenate(spread(tokens), axis=0)
    c_all = jnp.concatenate(spread(cotangent), axis=0)
    coef = coefficients(expert_ids, gate_scores, hot_list, capacity)
    coef_all = jnp.concatenate(spread(coef), axis=1)

    first = gather_slots(packed[:cut], orders[0], dp_count)
    second = gather_slots(packed[cut:], orders[1], dp_count)
    full = [jnp.concatenate([first[r], second[r]], axis=0) for r in range(groups)]
    gate_t = jnp.concatenate([f[:hidden] for f in full], axis=0)
    up_t = jnp.concatenate([f[hidden : 2 * hidden] for f in full], axis=0)
    down = jnp.concatenate([f[2 * hidden :] for f in full], axis=0)

    my_dp = lax.axis_index("dp")
    my_expert = lax.axis_index("expert")
    slot_of = jnp.arange(groups * hidden, dtype=jnp.int32) // hidden
    expert_of = (((my_dp ^ (2 * slot_of)) * ring + my_expert) // 2).astype(jnp.int32)
    pick = (jnp.arange(capacity.shape[0], dtype=jnp.int32)[:, None] == expert_of[None, :]).astype(F32)

    def compute(x_part, c_part, coef_part):
        weight = tn(coef_part, pick, precision=lax.Precision.HIGHEST)
        gate_pre = nt(x_part, gate_t)
        up_pre = nt(x_part, up_t)
        back = nt(c_part, down) * weight
        sig = jax.nn.sigmoid(gate_pre)
        act = gate_pre * sig
        scaled_hidden = (act * up_pre * weight).astype(BF16)
        d_up = (back * act).astype(BF16)
        d_gate = (back * up_pre * (sig * (1.0 + gate_pre * (1.0 - sig)))).astype(BF16)
        out = jnp.dot(scaled_hidden, down, preferred_element_type=F32)
        grad = jnp.dot(d_gate, gate_t, preferred_element_type=F32) + jnp.dot(
            d_up, up_t, preferred_element_type=F32
        )
        return out, grad, tn(d_gate, x_part), tn(d_up, x_part), tn(scaled_hidden, c_part)

    all_tokens = x_all.shape[0]
    steps = max(1, all_tokens // 1024)
    if steps == 1:
        out, grad, gate_g, up_g, down_g = compute(x_all, c_all, coef_all)
    else:
        size = all_tokens // steps

        def step(carry, chunk):
            got = compute(*chunk)
            carry = tuple(a + b for a, b in zip(carry, got[2:]))
            return carry, (got[0].astype(BF16), got[1].astype(BF16))

        zero = jnp.zeros((groups * hidden, width), F32)
        chunks = (
            x_all.reshape(steps, size, width),
            c_all.reshape(steps, size, width),
            coef_all.reshape(-1, steps, size).swapaxes(0, 1),
        )
        (gate_g, up_g, down_g), (out, grad) = lax.scan(step, (zero, zero, zero), chunks)
        out = out.reshape(all_tokens, width).astype(F32)
        grad = grad.reshape(all_tokens, width).astype(F32)

    def collect(value):
        half = ring * token_count
        away = swap(value[half:].astype(BF16), dp_count, 1)
        mine = value[:half] + away.astype(F32)
        pieces = [mine[s * token_count : (s + 1) * token_count] for s in range(ring)]
        carry = pieces[ring - 1]
        for s in range(ring - 2, -1, -1):
            carry = pieces[s] + rotate(carry.astype(BF16), ring, -1).astype(F32)
        return carry.astype(BF16)

    parts = [
        jnp.concatenate([g[r * hidden : (r + 1) * hidden] for g in (gate_g, up_g, down_g)], axis=0)
        for r in range(groups)
    ]
    total_a = reduce_slots({r: parts[r][:cut] for r in range(groups)}, orders[0], dp_count)
    total_b = reduce_slots({r: parts[r][cut:] for r in range(groups)}, orders[1], dp_count)
    total = jnp.concatenate([total_a, total_b], axis=0).astype(BF16)
    return (
        collect(out),
        collect(grad),
        total[:hidden].T[None],
        total[hidden : 2 * hidden].T[None],
        total[2 * hidden :][None],
    )


LANES = 128


def staged(dp_count, ring):
    return dp_count == 8 and ring == 4


def prep_kernel(*refs):
    sources, out, held, sems = refs[:5], refs[5], refs[6:11], refs[11]
    copies = [
        pltpu.make_async_copy(source, target, sems.at[i])
        for i, (source, target) in enumerate(zip(sources, held))
    ]
    for copy in copies:
        copy.start()
    for copy in copies:
        copy.wait()
    ids, gates, hot_list, capacity, tokens = held
    size, width = tokens.shape
    out[:, :width] = tokens[...]
    shape = (1, size)
    gate_rows, present_rows, limits = [], [], []
    for x in range(capacity.shape[0]):
        match = ids[...] == x
        gate_rows.append(jnp.sum(jnp.where(match, gates[...], 0.0), axis=0, keepdims=True))
        present_rows.append(jnp.sum(match.astype(F32), axis=0, keepdims=True))
        limit = capacity[x]
        for h in range(hot_list.shape[0]):
            limit = jnp.where(hot_list[h] == x, size, limit)
        limits.append(jnp.full(shape, limit, jnp.int32).astype(F32))
    present = jnp.concatenate(present_rows, axis=0)
    before = lax.broadcasted_iota(jnp.int32, (size, size), 0) < lax.broadcasted_iota(
        jnp.int32, (size, size), 1
    )
    rank = jnp.dot(
        present.astype(BF16), before.astype(F32).astype(BF16), preferred_element_type=F32
    )
    kept = (present > 0.5) & (rank < jnp.concatenate(limits, axis=0))
    rest = jnp.where(kept, jnp.concatenate(gate_rows, axis=0), 0.0)
    parts = []
    for _ in range(3):
        part = rest.astype(BF16).astype(F32)
        parts.append(part)
        rest = rest - part
    fill = jnp.zeros((LANES - 3 * rest.shape[0], size), F32)
    out[:, width:] = jnp.concatenate([*parts, fill], axis=0).T.astype(BF16)


def act_block(coef, x_part, c_part, gates, ups, downs, slots, views):
    hidden = gates[0].shape[0]
    stack = jnp.concatenate([v[...] for v in (*gates, *ups)], axis=0)
    pre = nt(stack, x_part)
    back_all = nt(jnp.concatenate([d[...] for d in downs], axis=0), c_part)
    for i, (r, (scaled, d_gate, d_up)) in enumerate(zip(slots, views)):
        low, high = i * hidden, (i + len(slots)) * hidden
        weight = coef[r : r + 1]
        gate_pre = pre[low : low + hidden]
        up_pre = pre[high : high + hidden]
        sig = jax.nn.sigmoid(gate_pre)
        act = gate_pre * sig
        grad_hidden = back_all[low : low + hidden] * weight
        scaled[...] = (act * up_pre * weight).astype(BF16)
        d_up[...] = (grad_hidden * act).astype(BF16)
        d_gate[...] = (grad_hidden * up_pre * (sig * (1.0 + gate_pre * (1.0 - sig)))).astype(BF16)


def local_call(body, ins, outs, flops, after=None):
    whole = pl.BlockSpec(memory_space=pltpu.VMEM)
    specs = [whole] * len(ins)
    count = len(ins)
    if after is not None:
        ins = (*ins, after)
        specs = specs + [pl.BlockSpec(memory_space=pl.ANY)]

    def kernel(*refs):
        body(refs[:count], refs[len(ins) :])

    moved = sum(v.size * v.dtype.itemsize for v in (*ins, *outs))
    return pl.pallas_call(
        kernel,
        out_shape=list(outs),
        in_specs=specs,
        out_specs=[whole] * len(outs),
        compiler_params=pltpu.CompilerParams(vmem_limit_bytes=16 << 20),
        cost_estimate=pl.CostEstimate(flops=flops, bytes_accessed=moved, transcendentals=0),
    )(*ins)


def on_device(tokens, cotangent, expert_ids, gate_scores, hot_list, capacity, w_gate, w_up, w_down):
    dp_count = lax.axis_size("dp")
    ring = lax.axis_size("expert")
    groups = dp_count // 2
    size, width = tokens.shape
    experts = capacity.shape[0]
    if not staged(dp_count, ring):
        return large_device(
            tokens, cotangent, expert_ids, gate_scores, hot_list, capacity, w_gate, w_up, w_down
        )
    hidden = w_gate.shape[2]
    half = hidden // 2
    cut = hidden + half
    pair = 2 * size
    total = ring * pair
    last = ring - 1
    shape = jax.ShapeDtypeStruct

    gate0, up0, down0 = w_gate[0].T, w_up[0].T, w_down[0]
    gate1, up2 = swap(gate0, dp_count, 2), swap(up0, dp_count, 4)
    down1, down2 = swap(down0, dp_count, 2), swap(down0, dp_count, 4)
    up1, gate2 = swap(up0, dp_count, 2), swap(gate0, dp_count, 4)
    gate3, up3 = swap(gate1, dp_count, 4), swap(up2, dp_count, 2)

    hbm = pl.BlockSpec(memory_space=pltpu.HBM)
    prep_in = (expert_ids.T, gate_scores.T, hot_list, capacity, tokens)
    spaces = (pltpu.VMEM, pltpu.VMEM, pltpu.SMEM, pltpu.SMEM, pltpu.VMEM)
    tokens = pl.pallas_call(
        prep_kernel,
        out_shape=shape((size, width + LANES), BF16),
        in_specs=[hbm] * 5,
        out_specs=pl.BlockSpec(memory_space=pltpu.VMEM),
        scratch_shapes=[
            *[space(v.shape, v.dtype) for space, v in zip(spaces, prep_in)],
            pltpu.SemaphoreType.DMA((5,)),
        ],
        compiler_params=pltpu.CompilerParams(vmem_limit_bytes=60 << 20),
        cost_estimate=pl.CostEstimate(flops=1 << 20, bytes_accessed=1 << 19, transcendentals=0),
        name="prep",
    )(*prep_in)

    def spread(value):
        own = [value]
        for _ in range(1, ring):
            own.append(rotate(own[-1], ring, 1))
        return [(v, swap(v, dp_count, 1)) for v in own]

    cots, toks = spread(cotangent), spread(tokens)
    late1, late2, _ = lax.optimization_barrier((down1, down2, toks[last - 1][0]))
    low3 = swap(late1[:half], dp_count, 4)
    high3 = swap(late2[half:], dp_count, 2)
    gates = (gate0, gate1, gate2, gate3)
    ups = (up0, up1, up2, up3)
    downs = ((down0,), (down1,), (down2,), (low3, high3))
    slot = jnp.arange(8, dtype=jnp.int32)
    expert_of = ((lax.axis_index("dp") ^ (2 * slot)) * ring + lax.axis_index("expert")) // 2
    lane = jnp.arange(LANES, dtype=jnp.int32)
    lane = jnp.where(lane < 3 * experts, lane % experts, -1)
    pick = (expert_of[:, None] == lane[None, :]).astype(BF16)

    def flat(pairs):
        return [v for p in pairs for v in p]

    def stage_body(refs, outs):
        for source, target in zip(refs, outs):
            target[...] = source[...]

    own = (tokens, cotangent)
    own = local_call(stage_body, own, [shape(v.shape, v.dtype) for v in own], 1 << 20)
    toks[0], cots[0] = (own[0], toks[0][1]), (own[1], cots[0][1])

    def block_of(refs, s):
        count = (len(refs) - 1) // 2
        t, c = refs[1 + 2 * s : 3 + 2 * s], refs[1 + count + 2 * s : 3 + count + 2 * s]
        x_part = jnp.concatenate([v[:, :width] for v in t], axis=0)
        extra = jnp.concatenate([v[:, width:] for v in t], axis=0)
        return nt(refs[0][...], extra), x_part, jnp.concatenate([v[...] for v in c], axis=0)

    def views_of(outs, slots, columns):
        return [
            [o.at[pl.ds(j * hidden, hidden), columns] for o in outs] for j in range(len(slots))
        ]

    near = (0, 1, 2)
    main_in = [pick, *flat(toks[:last]), *flat(cots[:last])]
    near_in = [*gates[:3], *ups[:3], *flat(downs[:3])]

    def main_body(refs, outs):
        g, u, d = (refs[len(main_in) + 3 * i : len(main_in) + 3 * i + 3] for i in range(3))
        for s in range(last):
            block = block_of(refs[: len(main_in)], s)
            act_block(*block, g, u, d, near, views_of(outs, near, pl.ds(s * pair, pair)))

    main = local_call(
        main_body,
        (*main_in, *near_in),
        [shape((3 * hidden, last * pair), BF16)] * 3,
        18 * hidden * last * pair * width,
    )

    def out_block(acts, g, u, d, outs):
        scaled, d_gate, d_up = acts
        out = tn(scaled, jnp.concatenate([v[...] for v in d], axis=0))
        outs[0][...] = out[:size]
        outs[2][:size] = out[size:].astype(BF16)
        both = jnp.concatenate([v[...] for v in (*g, *u)], axis=0)
        grad = tn(jnp.concatenate([d_gate, d_up], axis=0), both)
        outs[1][...] = grad[:size]
        outs[2][size:] = grad[size:].astype(BF16)

    weights_in = [*gates, *ups, *flat(downs)]
    out_shapes = [shape((size, width), F32)] * 2 + [shape((pair, width), BF16)]
    all_in = [pick, *flat(toks), *flat(cots)]

    def grad_block(slots, acts, refs, outs):
        count = len(refs) // 2
        x_all = jnp.concatenate([v[:, :width] for v in refs[:count]], axis=0)
        c_all = jnp.concatenate([v[...] for v in refs[count:]], axis=0)
        down_g = jnp.dot(acts[0], c_all, preferred_element_type=F32)
        both = jnp.concatenate([acts[1], acts[2]], axis=0)
        both_g = jnp.dot(both, x_all, preferred_element_type=F32)
        for i in range(slots):
            first, second = outs[2 * i], outs[2 * i + 1]
            low, high = i * hidden, (i + slots) * hidden
            first[hidden:] = down_g[low : low + half].astype(first.dtype)
            second[hidden:] = down_g[low + half : low + hidden].astype(second.dtype)
            first[:hidden] = both_g[low : low + hidden].astype(first.dtype)
            second[:hidden] = both_g[high : high + hidden].astype(second.dtype)

    def near_body(refs, outs):
        rest = refs[len(all_in) :]
        g, u, d = (rest[3 * i : 3 * i + 3] for i in range(3))
        block = block_of(refs[: len(all_in)], last)
        act_block(*block, g, u, d, near, views_of(outs[:3], near, pl.ds(0, pair)))
        rows = pl.ds(hidden, 2 * hidden)
        acts = [
            jnp.concatenate([m[rows], t[rows]], axis=1) for m, t in zip(rest[9:], outs[:3])
        ]
        grad_block(2, acts, refs[1 : len(all_in)], outs[3:])

    part_shapes = [shape((cut, width), t) for t in (BF16, F32, F32, BF16)]
    got = local_call(
        near_body,
        (*all_in, *near_in, *main),
        [shape((3 * hidden, pair), BF16)] * 3 + part_shapes,
        18 * hidden * pair * width + 12 * hidden * total * width,
    )
    tail, (first1, second1, first2, second2) = got[:3], got[3:]

    far_in = [gates[3], ups[3], *downs[3]]

    def middle_body(refs, outs):
        rest = refs[len(all_in) :]
        g, u, d = rest[:groups], rest[groups : 2 * groups], rest[2 * groups : -3]
        diag_refs = outs[:3]
        views = views_of(diag_refs, (3,), pl.ds(0, pair))
        block = block_of(refs[: len(all_in)], last)
        act_block(*block, g[3:], u[3:], d[3:], (3,), views)
        acts = [jnp.concatenate([t[...], v[...]], axis=0) for t, v in zip(rest[-3:], diag_refs)]
        out_block(acts, g, u, d, outs[3:])

    got = local_call(
        middle_body,
        (*all_in, *weights_in, *tail),
        [shape((hidden, pair), BF16)] * 3 + out_shapes,
        6 * groups * hidden * pair * width + 6 * hidden * pair * width,
        after=first1,
    )
    diag_last, part = got[:3], {last: got[3:]}

    def far_body(refs, outs):
        rest = refs[len(all_in) :]
        for s in range(last):
            views = views_of(outs[:3], (3,), pl.ds(s * pair, pair))
            block = block_of(refs[: len(all_in)], s)
            act_block(*block, rest[:1], rest[1:2], rest[2:-3], (3,), views)
        acts = [jnp.concatenate([v[...], t[...]], axis=1) for v, t in zip(outs[:3], rest[-3:])]
        grad_block(1, acts, refs[1 : len(all_in)], outs[3:])

    got = local_call(
        far_body,
        (*all_in, *far_in, *diag_last),
        [shape((hidden, last * pair), BF16)] * 3 + [shape((cut, width), BF16)] * 2,
        12 * hidden * total * width,
    )
    diag, (first3, second3) = got[:3], got[3:]

    def own_body(refs, outs):
        rows = pl.ds(0, hidden)
        acts = [jnp.concatenate([refs[k][rows], refs[k + 3][rows]], axis=1) for k in range(3)]
        grad_block(1, acts, refs[6:], outs)

    def outputs(s, after):
        acts = [*main, *diag]

        def body(refs, outs):
            rest = refs[6:]
            g, u, d = rest[:groups], rest[groups : 2 * groups], rest[2 * groups :]
            block = pl.ds(s * pair, pair)
            acts = [
                jnp.concatenate([refs[k][:, block], refs[k + 3][:, block]], axis=0)
                for k in range(3)
            ]
            out_block(acts, g, u, d, outs)

        flops = 6 * groups * hidden * pair * width
        return local_call(body, (*acts, *weights_in), out_shapes, flops, after)

    a1, b2 = swap(first1, dp_count, 2), swap(second2, dp_count, 4)
    a3, b3 = swap(first3, dp_count, 2), swap(second3, dp_count, 4)
    after = first3
    for s in range(last - 1, -1, -1):
        part[s] = outputs(s, after)
        after = part[s][0]
    first0, second0 = local_call(
        own_body,
        (*main, *tail, *flat(toks), *flat(cots)),
        [shape((cut, width), F32)] * 2,
        6 * hidden * total * width,
        after,
    )

    def add(s, i, away, moved):
        rows = pl.ds(i * size, size)

        def body(refs, outs):
            value = refs[0][...] + refs[1][rows].astype(F32)
            if moved is not None:
                value = value + refs[2][...].astype(F32)
            outs[0][...] = value.astype(BF16)

        ins = (part[s][i], away) if moved is None else (part[s][i], away, moved)
        return local_call(body, ins, [shape((size, width), BF16)], 1 << 18)[0]

    away = {s: swap(part[s][2], dp_count, 1) for s in part}
    carry = [None, None]
    for s in range(last, -1, -1):
        if s < last:
            carry = [rotate(c, ring, -1) for c in carry]
        carry = [add(s, i, away[s], carry[i]) for i in range(2)]
    mixed, token_grad = carry

    a2 = swap((first2 + a3.astype(F32)).astype(BF16), dp_count, 4)
    b1 = swap((second1 + b3.astype(F32)).astype(BF16), dp_count, 2)

    def finish(refs, outs):
        first = refs[0][...] + refs[2][...].astype(F32) + refs[3][...].astype(F32)
        second = refs[1][...] + refs[4][...].astype(F32) + refs[5][...].astype(F32)
        outs[0][...] = first[:hidden].astype(BF16)
        outs[1][...] = second[:hidden].astype(BF16)
        outs[2][:half] = first[hidden:].astype(BF16)
        outs[2][half:] = second[hidden:].astype(BF16)

    gate_g, up_g, down_g = local_call(
        finish, (first0, second0, a1, a2, b2, b1), [shape((hidden, width), BF16)] * 3, 1 << 20
    )
    return mixed, token_grad, gate_g.T[None], up_g.T[None], down_g[None]


def solution(mesh):
    rows = P(("dp", "expert"), None)
    weights = P(("dp", "expert"), None, None)
    return jax.shard_map(
        on_device,
        mesh=mesh,
        in_specs=(rows, rows, rows, rows, P(), P(), weights, weights, weights),
        out_specs=(rows, rows, weights, weights, weights),
        check_vma=False,
    )
```

```python
import jax
import jax.numpy as jnp
from jax import lax
from jax.experimental import pallas as pl
from jax.experimental.pallas import tpu as pltpu
from jax.sharding import PartitionSpec as P


F32 = jnp.float32
BF16 = jnp.bfloat16


def swap(value, count, mask):
    return lax.ppermute(value, "dp", [(i, i ^ mask) for i in range(count)])


def rotate(value, count, step):
    ring = [*range(0, count, 2), *range(count - 1 - count % 2, 0, -2)]
    pairs = [(ring[i], ring[(i + step) % count]) for i in range(count)]
    return lax.ppermute(value, "expert", sorted(pairs))


def nt(left, right):
    return lax.dot_general(left, right, (((1,), (1,)), ((), ())), preferred_element_type=F32)


def tn(left, right, **kw):
    return lax.dot_general(left, right, (((0,), (0,)), ((), ())), preferred_element_type=F32, **kw)


def coefficients(expert_ids, gate_scores, hot_list, capacity):
    count = capacity.shape[0]
    tokens = expert_ids.shape[0]
    iota = jnp.arange(count, dtype=jnp.int32)
    match = expert_ids.T[:, None, :] == iota[None, :, None]
    gates = jnp.sum(jnp.where(match, gate_scores.T[:, None, :], 0.0), axis=0)
    present = jnp.any(match, axis=0)
    order = jnp.arange(tokens, dtype=jnp.int32)
    before = (order[:, None] < order[None, :]).astype(BF16)
    rank = jnp.dot(present.astype(BF16), before, preferred_element_type=F32)
    hot = jnp.any(iota[:, None] == hot_list[None, :], axis=1)
    kept = present & (hot[:, None] | (rank < capacity[:, None].astype(F32)))
    return jnp.where(kept, gates, 0.0)


def gather_slots(own, order, dp_count):
    slots = {0: own}
    for bit in order:
        slots.update({r | bit: swap(v, dp_count, 2 * bit) for r, v in list(slots.items())})
    return slots


def reduce_slots(parts, order, dp_count):
    parts = dict(parts)
    for bit in order:
        moved = {r: swap(parts[r].astype(BF16), dp_count, 2 * bit) for r in parts if r & bit}
        parts = {
            r: v.astype(F32) + moved[r | bit].astype(F32) for r, v in parts.items() if not r & bit
        }
    return parts[0]


def large_device(tokens, cotangent, expert_ids, gate_scores, hot_list, capacity, w_gate, w_up, w_down):
    dp_count = lax.axis_size("dp")
    ring = lax.axis_size("expert")
    groups = dp_count // 2
    bits = [1 << b for b in range(groups.bit_length() - 1)]
    orders = (bits, bits[::-1])
    token_count, width = tokens.shape
    hidden = w_gate.shape[2]
    rows = 3 * hidden
    cut = rows // 2
    packed = jnp.concatenate([w_gate[0].T, w_up[0].T, w_down[0]], axis=0)

    def spread(value):
        own = [value]
        for _ in range(ring - 1):
            own.append(rotate(own[-1], ring, 1))
        return own + [swap(v, dp_count, 1) for v in own]

    x_all = jnp.concatenate(spread(tokens), axis=0)
    c_all = jnp.concatenate(spread(cotangent), axis=0)
    coef = coefficients(expert_ids, gate_scores, hot_list, capacity)
    coef_all = jnp.concatenate(spread(coef), axis=1)

    first = gather_slots(packed[:cut], orders[0], dp_count)
    second = gather_slots(packed[cut:], orders[1], dp_count)
    full = [jnp.concatenate([first[r], second[r]], axis=0) for r in range(groups)]
    gate_t = jnp.concatenate([f[:hidden] for f in full], axis=0)
    up_t = jnp.concatenate([f[hidden : 2 * hidden] for f in full], axis=0)
    down = jnp.concatenate([f[2 * hidden :] for f in full], axis=0)

    my_dp = lax.axis_index("dp")
    my_expert = lax.axis_index("expert")
    slot_of = jnp.arange(groups * hidden, dtype=jnp.int32) // hidden
    expert_of = (((my_dp ^ (2 * slot_of)) * ring + my_expert) // 2).astype(jnp.int32)
    pick = (jnp.arange(capacity.shape[0], dtype=jnp.int32)[:, None] == expert_of[None, :]).astype(F32)

    def compute(x_part, c_part, coef_part):
        weight = tn(coef_part, pick, precision=lax.Precision.HIGHEST)
        gate_pre = nt(x_part, gate_t)
        up_pre = nt(x_part, up_t)
        back = nt(c_part, down) * weight
        sig = jax.nn.sigmoid(gate_pre)
        act = gate_pre * sig
        scaled_hidden = (act * up_pre * weight).astype(BF16)
        d_up = (back * act).astype(BF16)
        d_gate = (back * up_pre * (sig * (1.0 + gate_pre * (1.0 - sig)))).astype(BF16)
        out = jnp.dot(scaled_hidden, down, preferred_element_type=F32)
        grad = jnp.dot(d_gate, gate_t, preferred_element_type=F32) + jnp.dot(
            d_up, up_t, preferred_element_type=F32
        )
        return out, grad, tn(d_gate, x_part), tn(d_up, x_part), tn(scaled_hidden, c_part)

    all_tokens = x_all.shape[0]
    steps = max(1, all_tokens // 1024)
    if steps == 1:
        out, grad, gate_g, up_g, down_g = compute(x_all, c_all, coef_all)
    else:
        size = all_tokens // steps

        def step(carry, chunk):
            got = compute(*chunk)
            carry = tuple(a + b for a, b in zip(carry, got[2:]))
            return carry, (got[0].astype(BF16), got[1].astype(BF16))

        zero = jnp.zeros((groups * hidden, width), F32)
        chunks = (
            x_all.reshape(steps, size, width),
            c_all.reshape(steps, size, width),
            coef_all.reshape(-1, steps, size).swapaxes(0, 1),
        )
        (gate_g, up_g, down_g), (out, grad) = lax.scan(step, (zero, zero, zero), chunks)
        out = out.reshape(all_tokens, width).astype(F32)
        grad = grad.reshape(all_tokens, width).astype(F32)

    def collect(value):
        half = ring * token_count
        away = swap(value[half:].astype(BF16), dp_count, 1)
        mine = value[:half] + away.astype(F32)
        pieces = [mine[s * token_count : (s + 1) * token_count] for s in range(ring)]
        carry = pieces[ring - 1]
        for s in range(ring - 2, -1, -1):
            carry = pieces[s] + rotate(carry.astype(BF16), ring, -1).astype(F32)
        return carry.astype(BF16)

    parts = [
        jnp.concatenate([g[r * hidden : (r + 1) * hidden] for g in (gate_g, up_g, down_g)], axis=0)
        for r in range(groups)
    ]
    total_a = reduce_slots({r: parts[r][:cut] for r in range(groups)}, orders[0], dp_count)
    total_b = reduce_slots({r: parts[r][cut:] for r in range(groups)}, orders[1], dp_count)
    total = jnp.concatenate([total_a, total_b], axis=0).astype(BF16)
    return (
        collect(out),
        collect(grad),
        total[:hidden].T[None],
        total[hidden : 2 * hidden].T[None],
        total[2 * hidden :][None],
    )


def large_device(tokens, cotangent, expert_ids, gate_scores, hot_list, capacity, w_gate, w_up, w_down):
    dp_count = lax.axis_size("dp")
    ring = lax.axis_size("expert")
    groups = dp_count // 2
    bits = [1 << b for b in range(groups.bit_length() - 1)]
    orders = (bits, bits[::-1])
    token_count, width = tokens.shape
    hidden = w_gate.shape[2]
    rows = 3 * hidden
    cut = rows // 2
    packed = jnp.concatenate([w_gate[0].T, w_up[0].T, w_down[0]], axis=0)

    def spread(value):
        own = [value]
        for _ in range(ring - 1):
            own.append(rotate(own[-1], ring, 1))
        return own + [swap(v, dp_count, 1) for v in own]

    x_all = jnp.concatenate(spread(tokens), axis=0)
    c_all = jnp.concatenate(spread(cotangent), axis=0)
    coef = coefficients(expert_ids, gate_scores, hot_list, capacity)
    coef_all = jnp.concatenate(spread(coef), axis=1)

    first = gather_slots(packed[:cut], orders[0], dp_count)
    second = gather_slots(packed[cut:], orders[1], dp_count)
    full = [jnp.concatenate([first[r], second[r]], axis=0) for r in range(groups)]
    gate_t = jnp.concatenate([f[:hidden] for f in full], axis=0)
    up_t = jnp.concatenate([f[hidden : 2 * hidden] for f in full], axis=0)
    down = jnp.concatenate([f[2 * hidden :] for f in full], axis=0)

    my_dp = lax.axis_index("dp")
    my_expert = lax.axis_index("expert")
    slot_of = jnp.arange(groups * hidden, dtype=jnp.int32) // hidden
    expert_of = (((my_dp ^ (2 * slot_of)) * ring + my_expert) // 2).astype(jnp.int32)
    pick = (jnp.arange(capacity.shape[0], dtype=jnp.int32)[:, None] == expert_of[None, :]).astype(F32)

    def compute(x_part, c_part, coef_part):
        weight = tn(coef_part, pick, precision=lax.Precision.HIGHEST)
        gate_pre = nt(x_part, gate_t)
        up_pre = nt(x_part, up_t)
        back = nt(c_part, down) * weight
        sig = jax.nn.sigmoid(gate_pre)
        act = gate_pre * sig
        scaled_hidden = (act * up_pre * weight).astype(BF16)
        d_up = (back * act).astype(BF16)
        d_gate = (back * up_pre * (sig * (1.0 + gate_pre * (1.0 - sig)))).astype(BF16)
        out = jnp.dot(scaled_hidden, down, preferred_element_type=F32)
        grad = jnp.dot(d_gate, gate_t, preferred_element_type=F32) + jnp.dot(
            d_up, up_t, preferred_element_type=F32
        )
        return out, grad, tn(d_gate, x_part), tn(d_up, x_part), tn(scaled_hidden, c_part)

    all_tokens = x_all.shape[0]
    steps = max(1, all_tokens // 1024)
    if steps == 1:
        out, grad, gate_g, up_g, down_g = compute(x_all, c_all, coef_all)
    else:
        size = all_tokens // steps

        def step(carry, chunk):
            got = compute(*chunk)
            carry = tuple(a + b for a, b in zip(carry, got[2:]))
            return carry, (got[0].astype(BF16), got[1].astype(BF16))

        zero = jnp.zeros((groups * hidden, width), F32)
        chunks = (
            x_all.reshape(steps, size, width),
            c_all.reshape(steps, size, width),
            coef_all.reshape(-1, steps, size).swapaxes(0, 1),
        )
        (gate_g, up_g, down_g), (out, grad) = lax.scan(step, (zero, zero, zero), chunks)
        out = out.reshape(all_tokens, width).astype(F32)
        grad = grad.reshape(all_tokens, width).astype(F32)

    def collect(value):
        half = ring * token_count
        away = swap(value[half:].astype(BF16), dp_count, 1)
        mine = value[:half] + away.astype(F32)
        pieces = [mine[s * token_count : (s + 1) * token_count] for s in range(ring)]
        carry = pieces[ring - 1]
        for s in range(ring - 2, -1, -1):
            carry = pieces[s] + rotate(carry.astype(BF16), ring, -1).astype(F32)
        return carry.astype(BF16)

    parts = [
        jnp.concatenate([g[r * hidden : (r + 1) * hidden] for g in (gate_g, up_g, down_g)], axis=0)
        for r in range(groups)
    ]
    total_a = reduce_slots({r: parts[r][:cut] for r in range(groups)}, orders[0], dp_count)
    total_b = reduce_slots({r: parts[r][cut:] for r in range(groups)}, orders[1], dp_count)
    total = jnp.concatenate([total_a, total_b], axis=0).astype(BF16)
    return (
        collect(out),
        collect(grad),
        total[:hidden].T[None],
        total[hidden : 2 * hidden].T[None],
        total[2 * hidden :][None],
    )


EXTRA = 8


def staged(dp_count, ring):
    return dp_count == 8 and ring == 4


def prep_kernel(*refs):
    sources, out, held, sems = refs[:5], refs[5], refs[6:11], refs[11]
    copies = [
        pltpu.make_async_copy(source, target, sems.at[i])
        for i, (source, target) in enumerate(zip(sources, held))
    ]
    for copy in copies:
        copy.start()
    for copy in copies:
        copy.wait()
    ids, gates, hot_list, capacity, tokens = held
    size, width = tokens.shape
    out[:size] = tokens[...]
    shape = (1, size)
    gate_rows, present_rows, limits = [], [], []
    for x in range(capacity.shape[0]):
        match = ids[...] == x
        gate_rows.append(jnp.sum(jnp.where(match, gates[...], 0.0), axis=0, keepdims=True))
        present_rows.append(jnp.sum(match.astype(F32), axis=0, keepdims=True))
        limit = capacity[x]
        for h in range(hot_list.shape[0]):
            limit = jnp.where(hot_list[h] == x, size, limit)
        limits.append(jnp.full(shape, limit, jnp.int32).astype(F32))
    present = jnp.concatenate(present_rows, axis=0)
    before = lax.broadcasted_iota(jnp.int32, (size, size), 0) < lax.broadcasted_iota(
        jnp.int32, (size, size), 1
    )
    rank = jnp.dot(
        present.astype(BF16), before.astype(F32).astype(BF16), preferred_element_type=F32
    )
    kept = (present > 0.5) & (rank < jnp.concatenate(limits, axis=0))
    rest = jnp.where(kept, jnp.concatenate(gate_rows, axis=0), 0.0)
    parts = []
    for _ in range(3):
        part = rest.astype(BF16).astype(F32)
        parts.append(part)
        rest = rest - part
    places = EXTRA * (width // size)
    parts.append(jnp.zeros((places - 3 * rest.shape[0], size), F32))
    packed = jnp.concatenate(parts, axis=0)
    packed = [packed[i : i + EXTRA] for i in range(0, places, EXTRA)]
    out[size:] = jnp.concatenate(packed, axis=1).astype(BF16)


def act_block(coef, x_part, c_part, gates, ups, downs, slots, views):
    hidden = gates[0].shape[0]
    stack = jnp.concatenate([v[...] for v in (*gates, *ups)], axis=0)
    pre = nt(stack, x_part)
    back_all = nt(jnp.concatenate([d[...] for d in downs], axis=0), c_part)
    for i, (r, (scaled, d_gate, d_up)) in enumerate(zip(slots, views)):
        low, high = i * hidden, (i + len(slots)) * hidden
        weight = coef[r : r + 1]
        gate_pre = pre[low : low + hidden]
        up_pre = pre[high : high + hidden]
        sig = jax.nn.sigmoid(gate_pre)
        act = gate_pre * sig
        grad_hidden = back_all[low : low + hidden] * weight
        scaled[...] = (act * up_pre * weight).astype(BF16)
        d_up[...] = (grad_hidden * act).astype(BF16)
        d_gate[...] = (grad_hidden * up_pre * (sig * (1.0 + gate_pre * (1.0 - sig)))).astype(BF16)


def local_call(body, ins, outs, flops, after=None):
    whole = pl.BlockSpec(memory_space=pltpu.VMEM)
    specs = [whole] * len(ins)
    count = len(ins)
    if after is not None:
        ins = (*ins, after)
        specs = specs + [pl.BlockSpec(memory_space=pl.ANY)]

    def kernel(*refs):
        body(refs[:count], refs[len(ins) :])

    moved = sum(v.size * v.dtype.itemsize for v in (*ins, *outs))
    return pl.pallas_call(
        kernel,
        out_shape=list(outs),
        in_specs=specs,
        out_specs=[whole] * len(outs),
        compiler_params=pltpu.CompilerParams(vmem_limit_bytes=16 << 20),
        cost_estimate=pl.CostEstimate(flops=flops, bytes_accessed=moved, transcendentals=0),
    )(*ins)


def on_device(tokens, cotangent, expert_ids, gate_scores, hot_list, capacity, w_gate, w_up, w_down):
    dp_count = lax.axis_size("dp")
    ring = lax.axis_size("expert")
    groups = dp_count // 2
    size, width = tokens.shape
    experts = capacity.shape[0]
    if not staged(dp_count, ring):
        return large_device(
            tokens, cotangent, expert_ids, gate_scores, hot_list, capacity, w_gate, w_up, w_down
        )
    hidden = w_gate.shape[2]
    half = hidden // 2
    cut = hidden + half
    pair = 2 * size
    total = ring * pair
    last = ring - 1
    shape = jax.ShapeDtypeStruct

    gate0, up0, down0 = w_gate[0].T, w_up[0].T, w_down[0]
    gate1, up2 = swap(gate0, dp_count, 2), swap(up0, dp_count, 4)
    down1, down2 = swap(down0, dp_count, 2), swap(down0, dp_count, 4)
    up1, gate2 = swap(up0, dp_count, 2), swap(gate0, dp_count, 4)
    gate3, up3 = swap(gate1, dp_count, 4), swap(up2, dp_count, 2)

    hbm = pl.BlockSpec(memory_space=pltpu.HBM)
    prep_in = (expert_ids.T, gate_scores.T, hot_list, capacity, tokens)
    spaces = (pltpu.VMEM, pltpu.VMEM, pltpu.SMEM, pltpu.SMEM, pltpu.VMEM)
    tokens = pl.pallas_call(
        prep_kernel,
        out_shape=shape((size + EXTRA, width), BF16),
        in_specs=[hbm] * 5,
        out_specs=pl.BlockSpec(memory_space=pltpu.VMEM),
        scratch_shapes=[
            *[space(v.shape, v.dtype) for space, v in zip(spaces, prep_in)],
            pltpu.SemaphoreType.DMA((5,)),
        ],
        compiler_params=pltpu.CompilerParams(vmem_limit_bytes=60 << 20),
        cost_estimate=pl.CostEstimate(flops=1 << 20, bytes_accessed=1 << 19, transcendentals=0),
        name="prep",
    )(*prep_in)

    def spread(value):
        own = [value]
        for _ in range(1, ring):
            own.append(rotate(own[-1], ring, 1))
        return [(v, swap(v, dp_count, 1)) for v in own]

    cots, toks = spread(cotangent), spread(tokens)
    late1, late2, _ = lax.optimization_barrier((down1, down2, toks[last - 1][0]))
    low3 = swap(late1[:half], dp_count, 4)
    high3 = swap(late2[half:], dp_count, 2)
    gates = (gate0, gate1, gate2, gate3)
    ups = (up0, up1, up2, up3)
    downs = ((down0,), (down1,), (down2,), (low3, high3))
    slot = jnp.arange(8, dtype=jnp.int32)
    expert_of = ((lax.axis_index("dp") ^ (2 * slot)) * ring + lax.axis_index("expert")) // 2
    lane = jnp.arange(EXTRA * (width // size), dtype=jnp.int32)
    lane = jnp.where(lane < 3 * experts, lane % experts, -1)
    pick = (expert_of[:, None] == lane[None, :]).astype(BF16)

    def flat(pairs):
        return [v for p in pairs for v in p]

    def stage_body(refs, outs):
        for source, target in zip(refs, outs):
            target[...] = source[...]

    own = (tokens, cotangent)
    own = local_call(stage_body, own, [shape(v.shape, v.dtype) for v in own], 1 << 20)
    toks[0], cots[0] = (own[0], toks[0][1]), (own[1], cots[0][1])

    def block_of(refs, s):
        count = (len(refs) - 1) // 2
        t, c = refs[1 + 2 * s : 3 + 2 * s], refs[1 + count + 2 * s : 3 + count + 2 * s]
        x_part = jnp.concatenate([v[:size] for v in t], axis=0)
        coef = []
        for v in t:
            extra = v[size:].astype(F32)
            packed = [extra[:, i : i + size] for i in range(0, width, size)]
            packed = jnp.concatenate(packed, axis=0).astype(BF16)
            coef.append(jnp.dot(refs[0][...], packed, preferred_element_type=F32))
        coef = jnp.concatenate(coef, axis=1)
        return coef, x_part, jnp.concatenate([v[...] for v in c], axis=0)

    def views_of(outs, slots, columns):
        return [
            [o.at[pl.ds(j * hidden, hidden), columns] for o in outs] for j in range(len(slots))
        ]

    near = (0, 1, 2)
    main_in = [pick, *flat(toks[:last]), *flat(cots[:last])]
    near_in = [*gates[:3], *ups[:3], *flat(downs[:3])]

    def main_body(refs, outs):
        g, u, d = (refs[len(main_in) + 3 * i : len(main_in) + 3 * i + 3] for i in range(3))
        for s in range(last):
            block = block_of(refs[: len(main_in)], s)
            act_block(*block, g, u, d, near, views_of(outs, near, pl.ds(s * pair, pair)))

    main = local_call(
        main_body,
        (*main_in, *near_in),
        [shape((3 * hidden, last * pair), BF16)] * 3,
        18 * hidden * last * pair * width,
    )

    def out_block(acts, g, u, d, outs):
        scaled, d_gate, d_up = acts
        out = tn(scaled, jnp.concatenate([v[...] for v in d], axis=0))
        outs[0][...] = out[:size]
        outs[2][:size] = out[size:].astype(BF16)
        both = jnp.concatenate([v[...] for v in (*g, *u)], axis=0)
        grad = tn(jnp.concatenate([d_gate, d_up], axis=0), both)
        outs[1][...] = grad[:size]
        outs[2][size:] = grad[size:].astype(BF16)

    weights_in = [*gates, *ups, *flat(downs)]
    out_shapes = [shape((size, width), F32)] * 2 + [shape((pair, width), BF16)]
    all_in = [pick, *flat(toks), *flat(cots)]

    def grad_block(slots, acts, refs, outs):
        count = len(refs) // 2
        x_all = jnp.concatenate([v[:size] for v in refs[:count]], axis=0)
        c_all = jnp.concatenate([v[...] for v in refs[count:]], axis=0)
        down_g = jnp.dot(acts[0], c_all, preferred_element_type=F32)
        both = jnp.concatenate([acts[1], acts[2]], axis=0)
        both_g = jnp.dot(both, x_all, preferred_element_type=F32)
        for i in range(slots):
            first, second = outs[2 * i], outs[2 * i + 1]
            low, high = i * hidden, (i + slots) * hidden
            first[hidden:] = down_g[low : low + half].astype(first.dtype)
            second[hidden:] = down_g[low + half : low + hidden].astype(second.dtype)
            first[:hidden] = both_g[low : low + hidden].astype(first.dtype)
            second[:hidden] = both_g[high : high + hidden].astype(second.dtype)

    def near_body(refs, outs):
        rest = refs[len(all_in) :]
        g, u, d = (rest[3 * i : 3 * i + 3] for i in range(3))
        block = block_of(refs[: len(all_in)], last)
        act_block(*block, g, u, d, near, views_of(outs[:3], near, pl.ds(0, pair)))
        rows = pl.ds(hidden, 2 * hidden)
        acts = [
            jnp.concatenate([m[rows], t[rows]], axis=1) for m, t in zip(rest[9:], outs[:3])
        ]
        grad_block(2, acts, refs[1 : len(all_in)], outs[3:])

    part_shapes = [shape((cut, width), t) for t in (BF16, F32, F32, BF16)]
    got = local_call(
        near_body,
        (*all_in, *near_in, *main),
        [shape((3 * hidden, pair), BF16)] * 3 + part_shapes,
        18 * hidden * pair * width + 12 * hidden * total * width,
    )
    tail, (first1, second1, first2, second2) = got[:3], got[3:]

    far_in = [gates[3], ups[3], *downs[3]]

    def middle_body(refs, outs):
        rest = refs[5 + len(far_in) :]
        block = block_of(refs[:5], 0)
        g, u, d = refs[5:6], refs[6:7], refs[7 : 5 + len(far_in)]
        act_block(*block, g, u, d, (3,), views_of(outs[:3], (3,), pl.ds(0, pair)))
        scaled = jnp.concatenate([rest[-1][...], outs[0][...]], axis=0)
        out = tn(scaled, jnp.concatenate([v[...] for v in rest[:-1]], axis=0))
        outs[3][...] = out[:size]
        outs[4][...] = out[size:].astype(BF16)

    halves = [shape((size, width), F32), shape((size, width), BF16)]
    got = local_call(
        middle_body,
        (pick, *toks[last], *cots[last], *far_in, *flat(downs), tail[0]),
        [shape((hidden, pair), BF16)] * 3 + halves,
        8 * groups * hidden * pair * width // 2,
        after=first1,
    )
    diag_last, mixed_part = got[:3], got[3:]

    def mid_grad_body(refs, outs):
        acts = jnp.concatenate([v[...] for v in refs[:4]], axis=0)
        grad = tn(acts, jnp.concatenate([v[...] for v in refs[4:]], axis=0))
        outs[0][...] = grad[:size]
        outs[1][...] = grad[size:].astype(BF16)

    grad_part = local_call(
        mid_grad_body,
        (tail[1], diag_last[1], tail[2], diag_last[2], *gates, *ups),
        halves,
        4 * groups * hidden * pair * width,
    )
    part = {last: (mixed_part[0], grad_part[0])}

    def far_body(refs, outs):
        rest = refs[len(all_in) :]
        for s in range(last):
            views = views_of(outs[:3], (3,), pl.ds(s * pair, pair))
            block = block_of(refs[: len(all_in)], s)
            act_block(*block, rest[:1], rest[1:2], rest[2:-3], (3,), views)
        acts = [jnp.concatenate([v[...], t[...]], axis=1) for v, t in zip(outs[:3], rest[-3:])]
        grad_block(1, acts, refs[1 : len(all_in)], outs[3:])

    got = local_call(
        far_body,
        (*all_in, *far_in, *diag_last),
        [shape((hidden, last * pair), BF16)] * 3 + [shape((cut, width), BF16)] * 2,
        12 * hidden * total * width,
    )
    diag, (first3, second3) = got[:3], got[3:]

    def own_body(refs, outs):
        rows = pl.ds(0, hidden)
        acts = [jnp.concatenate([refs[k][rows], refs[k + 3][rows]], axis=1) for k in range(3)]
        grad_block(1, acts, refs[6:], outs)

    def outputs(s, after):
        acts = [*main, *diag]

        def body(refs, outs):
            rest = refs[6:]
            g, u, d = rest[:groups], rest[groups : 2 * groups], rest[2 * groups :]
            block = pl.ds(s * pair, pair)
            acts = [
                jnp.concatenate([refs[k][:, block], refs[k + 3][:, block]], axis=0)
                for k in range(3)
            ]
            out_block(acts, g, u, d, outs)

        flops = 6 * groups * hidden * pair * width
        return local_call(body, (*acts, *weights_in), out_shapes, flops, after)

    a1, b2 = swap(first1, dp_count, 2), swap(second2, dp_count, 4)
    a3, b3 = swap(first3, dp_count, 2), swap(second3, dp_count, 4)
    after = first3
    for s in range(last - 1, -1, -1):
        part[s] = outputs(s, after)
        after = part[s][0]
    first0, second0 = local_call(
        own_body,
        (*main, *tail, *flat(toks), *flat(cots)),
        [shape((cut, width), F32)] * 2,
        6 * hidden * total * width,
        after,
    )

    def add(s, i, away, moved):
        rows = pl.ds(0 if s == last else i * size, size)

        def body(refs, outs):
            value = refs[0][...] + refs[1][rows].astype(F32)
            if moved is not None:
                value = value + refs[2][...].astype(F32)
            outs[0][...] = value.astype(BF16)

        ins = (part[s][i], away) if moved is None else (part[s][i], away, moved)
        return local_call(body, ins, [shape((size, width), BF16)], 1 << 18)[0]

    away = {s: [swap(part[s][2], dp_count, 1)] * 2 for s in range(last)}
    away[last] = [swap(v[1], dp_count, 1) for v in (mixed_part, grad_part)]
    carry = [None, None]
    for s in range(last, -1, -1):
        if s < last:
            carry = [rotate(c, ring, -1) for c in carry]
        carry = [add(s, i, away[s][i], carry[i]) for i in range(2)]
    mixed, token_grad = carry

    a2 = swap((first2 + a3.astype(F32)).astype(BF16), dp_count, 4)
    b1 = swap((second1 + b3.astype(F32)).astype(BF16), dp_count, 2)

    def finish(refs, outs):
        first = refs[0][...] + refs[2][...].astype(F32) + refs[3][...].astype(F32)
        second = refs[1][...] + refs[4][...].astype(F32) + refs[5][...].astype(F32)
        outs[0][...] = first[:hidden].astype(BF16)
        outs[1][...] = second[:hidden].astype(BF16)
        outs[2][:half] = first[hidden:].astype(BF16)
        outs[2][half:] = second[hidden:].astype(BF16)

    gate_g, up_g, down_g = local_call(
        finish, (first0, second0, a1, a2, b2, b1), [shape((hidden, width), BF16)] * 3, 1 << 20
    )
    return mixed, token_grad, gate_g.T[None], up_g.T[None], down_g[None]


def solution(mesh):
    rows = P(("dp", "expert"), None)
    weights = P(("dp", "expert"), None, None)
    return jax.shard_map(
        on_device,
        mesh=mesh,
        in_specs=(rows, rows, rows, rows, P(), P(), weights, weights, weights),
        out_specs=(rows, rows, weights, weights, weights),
        check_vma=False,
    )
```

```python
import jax
import jax.numpy as jnp
from jax import lax
from jax.experimental import pallas as pl
from jax.experimental.pallas import tpu as pltpu
from jax.sharding import PartitionSpec as P


F32 = jnp.float32
BF16 = jnp.bfloat16


def swap(value, count, mask):
    return lax.ppermute(value, "dp", [(i, i ^ mask) for i in range(count)])


def rotate(value, count, step):
    ring = [*range(0, count, 2), *range(count - 1 - count % 2, 0, -2)]
    pairs = [(ring[i], ring[(i + step) % count]) for i in range(count)]
    return lax.ppermute(value, "expert", sorted(pairs))


def nt(left, right):
    return lax.dot_general(left, right, (((1,), (1,)), ((), ())), preferred_element_type=F32)


def tn(left, right, **kw):
    return lax.dot_general(left, right, (((0,), (0,)), ((), ())), preferred_element_type=F32, **kw)


def coefficients(expert_ids, gate_scores, hot_list, capacity):
    count = capacity.shape[0]
    tokens = expert_ids.shape[0]
    iota = jnp.arange(count, dtype=jnp.int32)
    match = expert_ids.T[:, None, :] == iota[None, :, None]
    gates = jnp.sum(jnp.where(match, gate_scores.T[:, None, :], 0.0), axis=0)
    present = jnp.any(match, axis=0)
    order = jnp.arange(tokens, dtype=jnp.int32)
    before = (order[:, None] < order[None, :]).astype(BF16)
    rank = jnp.dot(present.astype(BF16), before, preferred_element_type=F32)
    hot = jnp.any(iota[:, None] == hot_list[None, :], axis=1)
    kept = present & (hot[:, None] | (rank < capacity[:, None].astype(F32)))
    return jnp.where(kept, gates, 0.0)


def gather_slots(own, order, dp_count):
    slots = {0: own}
    for bit in order:
        slots.update({r | bit: swap(v, dp_count, 2 * bit) for r, v in list(slots.items())})
    return slots


def reduce_slots(parts, order, dp_count):
    parts = dict(parts)
    for bit in order:
        moved = {r: swap(parts[r].astype(BF16), dp_count, 2 * bit) for r in parts if r & bit}
        parts = {
            r: v.astype(F32) + moved[r | bit].astype(F32) for r, v in parts.items() if not r & bit
        }
    return parts[0]


def large_device(tokens, cotangent, expert_ids, gate_scores, hot_list, capacity, w_gate, w_up, w_down):
    dp_count = lax.axis_size("dp")
    ring = lax.axis_size("expert")
    groups = dp_count // 2
    bits = [1 << b for b in range(groups.bit_length() - 1)]
    orders = (bits, bits[::-1])
    token_count, width = tokens.shape
    hidden = w_gate.shape[2]
    rows = 3 * hidden
    cut = rows // 2
    packed = jnp.concatenate([w_gate[0].T, w_up[0].T, w_down[0]], axis=0)

    def spread(value):
        own = [value]
        for _ in range(ring - 1):
            own.append(rotate(own[-1], ring, 1))
        return own + [swap(v, dp_count, 1) for v in own]

    x_all = jnp.concatenate(spread(tokens), axis=0)
    c_all = jnp.concatenate(spread(cotangent), axis=0)
    coef = coefficients(expert_ids, gate_scores, hot_list, capacity)
    coef_all = jnp.concatenate(spread(coef), axis=1)

    first = gather_slots(packed[:cut], orders[0], dp_count)
    second = gather_slots(packed[cut:], orders[1], dp_count)
    full = [jnp.concatenate([first[r], second[r]], axis=0) for r in range(groups)]
    gate_t = jnp.concatenate([f[:hidden] for f in full], axis=0)
    up_t = jnp.concatenate([f[hidden : 2 * hidden] for f in full], axis=0)
    down = jnp.concatenate([f[2 * hidden :] for f in full], axis=0)

    my_dp = lax.axis_index("dp")
    my_expert = lax.axis_index("expert")
    slot_of = jnp.arange(groups * hidden, dtype=jnp.int32) // hidden
    expert_of = (((my_dp ^ (2 * slot_of)) * ring + my_expert) // 2).astype(jnp.int32)
    pick = (jnp.arange(capacity.shape[0], dtype=jnp.int32)[:, None] == expert_of[None, :]).astype(F32)

    def compute(x_part, c_part, coef_part):
        weight = tn(coef_part, pick, precision=lax.Precision.HIGHEST)
        gate_pre = nt(x_part, gate_t)
        up_pre = nt(x_part, up_t)
        back = nt(c_part, down) * weight
        sig = jax.nn.sigmoid(gate_pre)
        act = gate_pre * sig
        scaled_hidden = (act * up_pre * weight).astype(BF16)
        d_up = (back * act).astype(BF16)
        d_gate = (back * up_pre * (sig * (1.0 + gate_pre * (1.0 - sig)))).astype(BF16)
        out = jnp.dot(scaled_hidden, down, preferred_element_type=F32)
        grad = jnp.dot(d_gate, gate_t, preferred_element_type=F32) + jnp.dot(
            d_up, up_t, preferred_element_type=F32
        )
        return out, grad, tn(d_gate, x_part), tn(d_up, x_part), tn(scaled_hidden, c_part)

    all_tokens = x_all.shape[0]
    steps = max(1, all_tokens // 1024)
    if steps == 1:
        out, grad, gate_g, up_g, down_g = compute(x_all, c_all, coef_all)
    else:
        size = all_tokens // steps

        def step(carry, chunk):
            got = compute(*chunk)
            carry = tuple(a + b for a, b in zip(carry, got[2:]))
            return carry, (got[0].astype(BF16), got[1].astype(BF16))

        zero = jnp.zeros((groups * hidden, width), F32)
        chunks = (
            x_all.reshape(steps, size, width),
            c_all.reshape(steps, size, width),
            coef_all.reshape(-1, steps, size).swapaxes(0, 1),
        )
        (gate_g, up_g, down_g), (out, grad) = lax.scan(step, (zero, zero, zero), chunks)
        out = out.reshape(all_tokens, width).astype(F32)
        grad = grad.reshape(all_tokens, width).astype(F32)

    def collect(value):
        half = ring * token_count
        away = swap(value[half:].astype(BF16), dp_count, 1)
        mine = value[:half] + away.astype(F32)
        pieces = [mine[s * token_count : (s + 1) * token_count] for s in range(ring)]
        carry = pieces[ring - 1]
        for s in range(ring - 2, -1, -1):
            carry = pieces[s] + rotate(carry.astype(BF16), ring, -1).astype(F32)
        return carry.astype(BF16)

    parts = [
        jnp.concatenate([g[r * hidden : (r + 1) * hidden] for g in (gate_g, up_g, down_g)], axis=0)
        for r in range(groups)
    ]
    total_a = reduce_slots({r: parts[r][:cut] for r in range(groups)}, orders[0], dp_count)
    total_b = reduce_slots({r: parts[r][cut:] for r in range(groups)}, orders[1], dp_count)
    total = jnp.concatenate([total_a, total_b], axis=0).astype(BF16)
    return (
        collect(out),
        collect(grad),
        total[:hidden].T[None],
        total[hidden : 2 * hidden].T[None],
        total[2 * hidden :][None],
    )


def large_device(tokens, cotangent, expert_ids, gate_scores, hot_list, capacity, w_gate, w_up, w_down):
    dp_count = lax.axis_size("dp")
    ring = lax.axis_size("expert")
    groups = dp_count // 2
    bits = [1 << b for b in range(groups.bit_length() - 1)]
    orders = (bits, bits[::-1])
    token_count, width = tokens.shape
    hidden = w_gate.shape[2]
    rows = 3 * hidden
    cut = rows // 2
    packed = jnp.concatenate([w_gate[0].T, w_up[0].T, w_down[0]], axis=0)

    def spread(value):
        own = [value]
        for _ in range(ring - 1):
            own.append(rotate(own[-1], ring, 1))
        return own + [swap(v, dp_count, 1) for v in own]

    x_all = jnp.concatenate(spread(tokens), axis=0)
    c_all = jnp.concatenate(spread(cotangent), axis=0)
    coef = coefficients(expert_ids, gate_scores, hot_list, capacity)
    coef_all = jnp.concatenate(spread(coef), axis=1)

    first = gather_slots(packed[:cut], orders[0], dp_count)
    second = gather_slots(packed[cut:], orders[1], dp_count)
    full = [jnp.concatenate([first[r], second[r]], axis=0) for r in range(groups)]
    gate_t = jnp.concatenate([f[:hidden] for f in full], axis=0)
    up_t = jnp.concatenate([f[hidden : 2 * hidden] for f in full], axis=0)
    down = jnp.concatenate([f[2 * hidden :] for f in full], axis=0)

    my_dp = lax.axis_index("dp")
    my_expert = lax.axis_index("expert")
    slot_of = jnp.arange(groups * hidden, dtype=jnp.int32) // hidden
    expert_of = (((my_dp ^ (2 * slot_of)) * ring + my_expert) // 2).astype(jnp.int32)
    pick = (jnp.arange(capacity.shape[0], dtype=jnp.int32)[:, None] == expert_of[None, :]).astype(F32)

    def compute(x_part, c_part, coef_part):
        weight = tn(coef_part, pick, precision=lax.Precision.HIGHEST)
        gate_pre = nt(x_part, gate_t)
        up_pre = nt(x_part, up_t)
        back = nt(c_part, down) * weight
        sig = jax.nn.sigmoid(gate_pre)
        act = gate_pre * sig
        scaled_hidden = (act * up_pre * weight).astype(BF16)
        d_up = (back * act).astype(BF16)
        d_gate = (back * up_pre * (sig * (1.0 + gate_pre * (1.0 - sig)))).astype(BF16)
        out = jnp.dot(scaled_hidden, down, preferred_element_type=F32)
        grad = jnp.dot(d_gate, gate_t, preferred_element_type=F32) + jnp.dot(
            d_up, up_t, preferred_element_type=F32
        )
        return out, grad, tn(d_gate, x_part), tn(d_up, x_part), tn(scaled_hidden, c_part)

    all_tokens = x_all.shape[0]
    steps = max(1, all_tokens // 1024)
    if steps == 1:
        out, grad, gate_g, up_g, down_g = compute(x_all, c_all, coef_all)
    else:
        size = all_tokens // steps

        def step(carry, chunk):
            got = compute(*chunk)
            carry = tuple(a + b for a, b in zip(carry, got[2:]))
            return carry, (got[0].astype(BF16), got[1].astype(BF16))

        zero = jnp.zeros((groups * hidden, width), F32)
        chunks = (
            x_all.reshape(steps, size, width),
            c_all.reshape(steps, size, width),
            coef_all.reshape(-1, steps, size).swapaxes(0, 1),
        )
        (gate_g, up_g, down_g), (out, grad) = lax.scan(step, (zero, zero, zero), chunks)
        out = out.reshape(all_tokens, width).astype(F32)
        grad = grad.reshape(all_tokens, width).astype(F32)

    def collect(value):
        half = ring * token_count
        away = swap(value[half:].astype(BF16), dp_count, 1)
        mine = value[:half] + away.astype(F32)
        pieces = [mine[s * token_count : (s + 1) * token_count] for s in range(ring)]
        carry = pieces[ring - 1]
        for s in range(ring - 2, -1, -1):
            carry = pieces[s] + rotate(carry.astype(BF16), ring, -1).astype(F32)
        return carry.astype(BF16)

    parts = [
        jnp.concatenate([g[r * hidden : (r + 1) * hidden] for g in (gate_g, up_g, down_g)], axis=0)
        for r in range(groups)
    ]
    total_a = reduce_slots({r: parts[r][:cut] for r in range(groups)}, orders[0], dp_count)
    total_b = reduce_slots({r: parts[r][cut:] for r in range(groups)}, orders[1], dp_count)
    total = jnp.concatenate([total_a, total_b], axis=0).astype(BF16)
    return (
        collect(out),
        collect(grad),
        total[:hidden].T[None],
        total[hidden : 2 * hidden].T[None],
        total[2 * hidden :][None],
    )


EXTRA = 8


def staged(dp_count, ring):
    return dp_count == 8 and ring == 4


def prep_kernel(*refs):
    sources, out, held, sems = refs[:5], refs[5], refs[6:11], refs[11]
    copies = [
        pltpu.make_async_copy(source, target, sems.at[i])
        for i, (source, target) in enumerate(zip(sources, held))
    ]
    for copy in copies:
        copy.start()
    for copy in copies:
        copy.wait()
    ids, gates, hot_list, capacity, tokens = held
    size, width = tokens.shape
    out[:size] = tokens[...]
    shape = (1, size)
    gate_rows, present_rows, limits = [], [], []
    for x in range(capacity.shape[0]):
        match = ids[...] == x
        gate_rows.append(jnp.sum(jnp.where(match, gates[...], 0.0), axis=0, keepdims=True))
        present_rows.append(jnp.sum(match.astype(F32), axis=0, keepdims=True))
        limit = capacity[x]
        for h in range(hot_list.shape[0]):
            limit = jnp.where(hot_list[h] == x, size, limit)
        limits.append(jnp.full(shape, limit, jnp.int32).astype(F32))
    present = jnp.concatenate(present_rows, axis=0)
    before = lax.broadcasted_iota(jnp.int32, (size, size), 0) < lax.broadcasted_iota(
        jnp.int32, (size, size), 1
    )
    rank = jnp.dot(
        present.astype(BF16), before.astype(F32).astype(BF16), preferred_element_type=F32
    )
    kept = (present > 0.5) & (rank < jnp.concatenate(limits, axis=0))
    rest = jnp.where(kept, jnp.concatenate(gate_rows, axis=0), 0.0)
    parts = []
    for _ in range(3):
        part = rest.astype(BF16).astype(F32)
        parts.append(part)
        rest = rest - part
    places = EXTRA * (width // size)
    parts.append(jnp.zeros((places - 3 * rest.shape[0], size), F32))
    packed = jnp.concatenate(parts, axis=0)
    packed = [packed[i : i + EXTRA] for i in range(0, places, EXTRA)]
    out[size:] = jnp.concatenate(packed, axis=1).astype(BF16)


def act_block(coef, x_part, c_part, gates, ups, downs, slots, views):
    hidden = gates[0].shape[0]
    stack = jnp.concatenate([v[...] for v in (*gates, *ups)], axis=0)
    pre = nt(stack, x_part)
    back_all = nt(jnp.concatenate([d[...] for d in downs], axis=0), c_part)
    for i, (r, (scaled, d_gate, d_up)) in enumerate(zip(slots, views)):
        low, high = i * hidden, (i + len(slots)) * hidden
        weight = coef[r : r + 1]
        gate_pre = pre[low : low + hidden]
        up_pre = pre[high : high + hidden]
        sig = jax.nn.sigmoid(gate_pre)
        act = gate_pre * sig
        grad_hidden = back_all[low : low + hidden] * weight
        scaled[...] = (act * up_pre * weight).astype(BF16)
        d_up[...] = (grad_hidden * act).astype(BF16)
        d_gate[...] = (grad_hidden * up_pre * (sig * (1.0 + gate_pre * (1.0 - sig)))).astype(BF16)


def local_call(body, ins, outs, flops, after=None):
    whole = pl.BlockSpec(memory_space=pltpu.VMEM)
    specs = [whole] * len(ins)
    count = len(ins)
    if after is not None:
        ins = (*ins, after)
        specs = specs + [pl.BlockSpec(memory_space=pl.ANY)]

    def kernel(*refs):
        body(refs[:count], refs[len(ins) :])

    moved = sum(v.size * v.dtype.itemsize for v in (*ins, *outs))
    return pl.pallas_call(
        kernel,
        out_shape=list(outs),
        in_specs=specs,
        out_specs=[whole] * len(outs),
        compiler_params=pltpu.CompilerParams(vmem_limit_bytes=16 << 20),
        cost_estimate=pl.CostEstimate(flops=flops, bytes_accessed=moved, transcendentals=0),
    )(*ins)


def on_device(tokens, cotangent, expert_ids, gate_scores, hot_list, capacity, w_gate, w_up, w_down):
    dp_count = lax.axis_size("dp")
    ring = lax.axis_size("expert")
    groups = dp_count // 2
    size, width = tokens.shape
    experts = capacity.shape[0]
    if not staged(dp_count, ring):
        return large_device(
            tokens, cotangent, expert_ids, gate_scores, hot_list, capacity, w_gate, w_up, w_down
        )
    hidden = w_gate.shape[2]
    half = hidden // 2
    cut = hidden + half
    pair = 2 * size
    total = ring * pair
    last = ring - 1
    shape = jax.ShapeDtypeStruct

    gate0, up0, down0 = w_gate[0].T, w_up[0].T, w_down[0]
    gate1, up2 = swap(gate0, dp_count, 2), swap(up0, dp_count, 4)
    down1, down2 = swap(down0, dp_count, 2), swap(down0, dp_count, 4)
    up1, gate2 = swap(up0, dp_count, 2), swap(gate0, dp_count, 4)
    gate3, up3 = swap(gate1, dp_count, 4), swap(up2, dp_count, 2)

    hbm = pl.BlockSpec(memory_space=pltpu.HBM)
    prep_in = (expert_ids.T, gate_scores.T, hot_list, capacity, tokens)
    spaces = (pltpu.VMEM, pltpu.VMEM, pltpu.SMEM, pltpu.SMEM, pltpu.VMEM)
    tokens = pl.pallas_call(
        prep_kernel,
        out_shape=shape((size + EXTRA, width), BF16),
        in_specs=[hbm] * 5,
        out_specs=pl.BlockSpec(memory_space=pltpu.VMEM),
        scratch_shapes=[
            *[space(v.shape, v.dtype) for space, v in zip(spaces, prep_in)],
            pltpu.SemaphoreType.DMA((5,)),
        ],
        compiler_params=pltpu.CompilerParams(vmem_limit_bytes=60 << 20),
        cost_estimate=pl.CostEstimate(flops=1 << 20, bytes_accessed=1 << 19, transcendentals=0),
        name="prep",
    )(*prep_in)

    def spread(value):
        own = [value]
        for _ in range(1, ring):
            own.append(rotate(own[-1], ring, 1))
        return [(v, swap(v, dp_count, 1)) for v in own]

    cots, toks = spread(cotangent), spread(tokens)
    late1, late2, _ = lax.optimization_barrier((down1, down2, toks[last - 1][0]))
    low3 = swap(late1[:half], dp_count, 4)
    high3 = swap(late2[half:], dp_count, 2)
    gates = (gate0, gate1, gate2, gate3)
    ups = (up0, up1, up2, up3)
    downs = ((down0,), (down1,), (down2,), (low3, high3))
    slot = jnp.arange(8, dtype=jnp.int32)
    expert_of = ((lax.axis_index("dp") ^ (2 * slot)) * ring + lax.axis_index("expert")) // 2
    lane = jnp.arange(EXTRA * (width // size), dtype=jnp.int32)
    lane = jnp.where(lane < 3 * experts, lane % experts, -1)
    pick = (expert_of[:, None] == lane[None, :]).astype(BF16)

    def flat(pairs):
        return [v for p in pairs for v in p]

    def stage_body(refs, outs):
        for source, target in zip(refs, outs):
            target[...] = source[...]

    own = (tokens, cotangent)
    own = local_call(stage_body, own, [shape(v.shape, v.dtype) for v in own], 1 << 20)
    toks[0], cots[0] = (own[0], toks[0][1]), (own[1], cots[0][1])

    def block_of(refs, s):
        count = (len(refs) - 1) // 2
        t, c = refs[1 + 2 * s : 3 + 2 * s], refs[1 + count + 2 * s : 3 + count + 2 * s]
        x_part = jnp.concatenate([v[:size] for v in t], axis=0)
        coef = []
        for v in t:
            extra = v[size:].astype(F32)
            packed = [extra[:, i : i + size] for i in range(0, width, size)]
            packed = jnp.concatenate(packed, axis=0).astype(BF16)
            coef.append(jnp.dot(refs[0][...], packed, preferred_element_type=F32))
        coef = jnp.concatenate(coef, axis=1)
        return coef, x_part, jnp.concatenate([v[...] for v in c], axis=0)

    def views_of(outs, slots, columns):
        return [
            [o.at[pl.ds(j * hidden, hidden), columns] for o in outs] for j in range(len(slots))
        ]

    near = (0, 1, 2)
    main_in = [pick, *flat(toks[:last]), *flat(cots[:last])]
    near_in = [*gates[:3], *ups[:3], *flat(downs[:3])]

    def main_body(refs, outs):
        g, u, d = (refs[len(main_in) + 3 * i : len(main_in) + 3 * i + 3] for i in range(3))
        for s in range(last):
            block = block_of(refs[: len(main_in)], s)
            act_block(*block, g, u, d, near, views_of(outs, near, pl.ds(s * pair, pair)))

    main = local_call(
        main_body,
        (*main_in, *near_in),
        [shape((3 * hidden, last * pair), BF16)] * 3,
        18 * hidden * last * pair * width,
    )

    def out_block(acts, g, u, d, outs):
        scaled, d_gate, d_up = acts
        out = tn(scaled, jnp.concatenate([v[...] for v in d], axis=0))
        outs[0][...] = out[:size]
        outs[2][:size] = out[size:].astype(BF16)
        both = jnp.concatenate([v[...] for v in (*g, *u)], axis=0)
        grad = tn(jnp.concatenate([d_gate, d_up], axis=0), both)
        outs[1][...] = grad[:size]
        outs[2][size:] = grad[size:].astype(BF16)

    weights_in = [*gates, *ups, *flat(downs)]
    out_shapes = [shape((size, width), F32)] * 2 + [shape((pair, width), BF16)]
    all_in = [pick, *flat(toks), *flat(cots)]

    def grad_block(slots, acts, refs, outs):
        count = len(refs) // 2
        x_all = jnp.concatenate([v[:size] for v in refs[:count]], axis=0)
        c_all = jnp.concatenate([v[...] for v in refs[count:]], axis=0)
        down_g = jnp.dot(acts[0], c_all, preferred_element_type=F32)
        both = jnp.concatenate([acts[1], acts[2]], axis=0)
        both_g = jnp.dot(both, x_all, preferred_element_type=F32)
        for i in range(slots):
            first, second = outs[2 * i], outs[2 * i + 1]
            low, high = i * hidden, (i + slots) * hidden
            first[hidden:] = down_g[low : low + half].astype(first.dtype)
            second[hidden:] = down_g[low + half : low + hidden].astype(second.dtype)
            first[:hidden] = both_g[low : low + hidden].astype(first.dtype)
            second[:hidden] = both_g[high : high + hidden].astype(second.dtype)

    near_two = (1, 2)

    def near_body(refs, outs):
        rest = refs[len(all_in) :]
        g, u, d = (rest[2 * i : 2 * i + 2] for i in range(3))
        block = block_of(refs[: len(all_in)], last)
        act_block(*block, g, u, d, near_two, views_of(outs[:3], near_two, pl.ds(0, pair)))
        rows = pl.ds(hidden, 2 * hidden)
        acts = [
            jnp.concatenate([m[rows], t[...]], axis=1) for m, t in zip(rest[6:], outs[:3])
        ]
        grad_block(2, acts, refs[1 : len(all_in)], outs[3:])

    part_shapes = [shape((cut, width), t) for t in (BF16, F32, F32, BF16)]
    got = local_call(
        near_body,
        (*all_in, *gates[1:3], *ups[1:3], *flat(downs[1:3]), *main),
        [shape((2 * hidden, pair), BF16)] * 3 + part_shapes,
        12 * hidden * pair * width + 12 * hidden * total * width,
    )
    tail, (first1, second1, first2, second2) = got[:3], got[3:]

    far_in = [gates[3], ups[3], *downs[3]]

    ends = (0, 3)
    ends_in = [gates[0], gates[3], ups[0], ups[3], *downs[0], *downs[3]]

    def ordered(end, inner):
        return jnp.concatenate([end[:hidden], inner[...], end[hidden:]], axis=0)

    def middle_body(refs, outs):
        rest = refs[5 + len(ends_in) :]
        block = block_of(refs[:5], 0)
        g, u, d = refs[5:7], refs[7:9], refs[9 : 5 + len(ends_in)]
        act_block(*block, g, u, d, ends, views_of(outs[:3], ends, pl.ds(0, pair)))
        down = jnp.concatenate([v[...] for v in rest[:-1]], axis=0)
        out = tn(ordered(outs[0], rest[-1]), down)
        outs[3][...] = out[:size]
        outs[4][...] = out[size:].astype(BF16)

    halves = [shape((size, width), F32), shape((size, width), BF16)]
    got = local_call(
        middle_body,
        (pick, *toks[last], *cots[last], *ends_in, *flat(downs), tail[0]),
        [shape((2 * hidden, pair), BF16)] * 3 + halves,
        10 * groups * hidden * pair * width // 2,
        after=first1,
    )
    end_acts, mixed_part = got[:3], got[3:]

    def mid_grad_body(refs, outs):
        acts = jnp.concatenate([ordered(refs[0], refs[1]), ordered(refs[2], refs[3])], axis=0)
        grad = tn(acts, jnp.concatenate([v[...] for v in refs[4:]], axis=0))
        outs[0][...] = grad[:size]
        outs[1][...] = grad[size:].astype(BF16)

    grad_part = local_call(
        mid_grad_body,
        (end_acts[1], tail[1], end_acts[2], tail[2], *gates, *ups),
        halves,
        4 * groups * hidden * pair * width,
    )
    part = {last: (mixed_part[0], grad_part[0])}

    def far_body(refs, outs):
        rest = refs[len(all_in) :]
        for s in range(last):
            views = views_of(outs[:3], (3,), pl.ds(s * pair, pair))
            block = block_of(refs[: len(all_in)], s)
            act_block(*block, rest[:1], rest[1:2], rest[2:-3], (3,), views)
        acts = [
            jnp.concatenate([v[...], t[hidden:]], axis=1) for v, t in zip(outs[:3], rest[-3:])
        ]
        grad_block(1, acts, refs[1 : len(all_in)], outs[3:])

    got = local_call(
        far_body,
        (*all_in, *far_in, *end_acts),
        [shape((hidden, last * pair), BF16)] * 3 + [shape((cut, width), BF16)] * 2,
        12 * hidden * total * width,
    )
    diag, (first3, second3) = got[:3], got[3:]

    def own_body(refs, outs):
        rows = pl.ds(0, hidden)
        acts = [jnp.concatenate([refs[k][rows], refs[k + 3][rows]], axis=1) for k in range(3)]
        grad_block(1, acts, refs[6:], outs)

    def outputs(s, after):
        acts = [*main, *diag]

        def body(refs, outs):
            rest = refs[6:]
            g, u, d = rest[:groups], rest[groups : 2 * groups], rest[2 * groups :]
            block = pl.ds(s * pair, pair)
            acts = [
                jnp.concatenate([refs[k][:, block], refs[k + 3][:, block]], axis=0)
                for k in range(3)
            ]
            out_block(acts, g, u, d, outs)

        flops = 6 * groups * hidden * pair * width
        return local_call(body, (*acts, *weights_in), out_shapes, flops, after)

    a1, b2 = swap(first1, dp_count, 2), swap(second2, dp_count, 4)
    a3, b3 = swap(first3, dp_count, 2), swap(second3, dp_count, 4)
    after = first3
    for s in range(last - 1, -1, -1):
        part[s] = outputs(s, after)
        after = part[s][0]
    first0, second0 = local_call(
        own_body,
        (*main, *end_acts, *flat(toks), *flat(cots)),
        [shape((cut, width), F32)] * 2,
        6 * hidden * total * width,
        after,
    )

    done = [shape((size, width), BF16), shape((8, 128), F32)]

    def add(s, i, away, moved):
        rows = pl.ds(0 if s == last else i * size, size)

        def body(refs, outs):
            value = refs[0][...] + refs[1][rows].astype(F32)
            if moved is not None:
                value = value + refs[2][...].astype(F32)
            outs[0][...] = value.astype(BF16)
            outs[1][...] = jnp.zeros_like(outs[1])

        ins = (part[s][i], away) if moved is None else (part[s][i], away, moved)
        return local_call(body, ins, done, 1 << 18)

    away = {s: [swap(part[s][2], dp_count, 1)] * 2 for s in range(last)}
    away[last] = [swap(v[1], dp_count, 1) for v in (mixed_part, grad_part)]
    carry = [None, None]
    for s in range(last, -1, -1):
        if s < last:
            carry = [rotate(c[0], ring, -1) for c in carry]
        carry = [add(s, i, away[s][i], carry[i]) for i in range(2)]
    (mixed, _), (token_grad, finished) = carry

    a2 = swap((first2 + a3.astype(F32)).astype(BF16), dp_count, 4)
    b1 = swap((second1 + b3.astype(F32)).astype(BF16), dp_count, 2)

    def finish(refs, outs):
        first = refs[0][...] + refs[2][...].astype(F32) + refs[3][...].astype(F32)
        second = refs[1][...] + refs[4][...].astype(F32) + refs[5][...].astype(F32)
        outs[0][...] = first[:hidden].astype(BF16)
        outs[1][...] = second[:hidden].astype(BF16)
        outs[2][:half] = first[hidden:].astype(BF16)
        outs[2][half:] = second[hidden:].astype(BF16)

    gate_g, up_g, down_g = local_call(
        finish,
        (first0, second0, a1, a2, b2, b1),
        [shape((hidden, width), BF16)] * 3,
        1 << 20,
        finished,
    )
    return mixed, token_grad, gate_g.T[None], up_g.T[None], down_g[None]


def solution(mesh):
    rows = P(("dp", "expert"), None)
    weights = P(("dp", "expert"), None, None)
    return jax.shard_map(
        on_device,
        mesh=mesh,
        in_specs=(rows, rows, rows, rows, P(), P(), weights, weights, weights),
        out_specs=(rows, rows, weights, weights, weights),
        check_vma=False,
    )
```

```python
import jax
import jax.numpy as jnp
from jax import lax
from jax.experimental import pallas as pl
from jax.experimental.pallas import tpu as pltpu
from jax.sharding import PartitionSpec as P


F32 = jnp.float32
BF16 = jnp.bfloat16


def swap(value, count, mask):
    return lax.ppermute(value, "dp", [(i, i ^ mask) for i in range(count)])


def rotate(value, count, step):
    ring = [*range(0, count, 2), *range(count - 1 - count % 2, 0, -2)]
    pairs = [(ring[i], ring[(i + step) % count]) for i in range(count)]
    return lax.ppermute(value, "expert", sorted(pairs))


def nt(left, right):
    return lax.dot_general(left, right, (((1,), (1,)), ((), ())), preferred_element_type=F32)


def tn(left, right, **kw):
    return lax.dot_general(left, right, (((0,), (0,)), ((), ())), preferred_element_type=F32, **kw)


def coefficients(expert_ids, gate_scores, hot_list, capacity):
    count = capacity.shape[0]
    tokens = expert_ids.shape[0]
    iota = jnp.arange(count, dtype=jnp.int32)
    match = expert_ids.T[:, None, :] == iota[None, :, None]
    gates = jnp.sum(jnp.where(match, gate_scores.T[:, None, :], 0.0), axis=0)
    present = jnp.any(match, axis=0)
    order = jnp.arange(tokens, dtype=jnp.int32)
    before = (order[:, None] < order[None, :]).astype(BF16)
    rank = jnp.dot(present.astype(BF16), before, preferred_element_type=F32)
    hot = jnp.any(iota[:, None] == hot_list[None, :], axis=1)
    kept = present & (hot[:, None] | (rank < capacity[:, None].astype(F32)))
    return jnp.where(kept, gates, 0.0)


def gather_slots(own, order, dp_count):
    slots = {0: own}
    for bit in order:
        slots.update({r | bit: swap(v, dp_count, 2 * bit) for r, v in list(slots.items())})
    return slots


def reduce_slots(parts, order, dp_count):
    parts = dict(parts)
    for bit in order:
        moved = {r: swap(parts[r].astype(BF16), dp_count, 2 * bit) for r in parts if r & bit}
        parts = {
            r: v.astype(F32) + moved[r | bit].astype(F32) for r, v in parts.items() if not r & bit
        }
    return parts[0]


def large_device(tokens, cotangent, expert_ids, gate_scores, hot_list, capacity, w_gate, w_up, w_down):
    dp_count = lax.axis_size("dp")
    ring = lax.axis_size("expert")
    groups = dp_count // 2
    bits = [1 << b for b in range(groups.bit_length() - 1)]
    orders = (bits, bits[::-1])
    token_count, width = tokens.shape
    hidden = w_gate.shape[2]
    rows = 3 * hidden
    cut = rows // 2
    packed = jnp.concatenate([w_gate[0].T, w_up[0].T, w_down[0]], axis=0)

    def spread(value):
        own = [value]
        for _ in range(ring - 1):
            own.append(rotate(own[-1], ring, 1))
        return own + [swap(v, dp_count, 1) for v in own]

    x_all = jnp.concatenate(spread(tokens), axis=0)
    c_all = jnp.concatenate(spread(cotangent), axis=0)
    coef = coefficients(expert_ids, gate_scores, hot_list, capacity)
    coef_all = jnp.concatenate(spread(coef), axis=1)

    first = gather_slots(packed[:cut], orders[0], dp_count)
    second = gather_slots(packed[cut:], orders[1], dp_count)
    full = [jnp.concatenate([first[r], second[r]], axis=0) for r in range(groups)]
    gate_t = jnp.concatenate([f[:hidden] for f in full], axis=0)
    up_t = jnp.concatenate([f[hidden : 2 * hidden] for f in full], axis=0)
    down = jnp.concatenate([f[2 * hidden :] for f in full], axis=0)

    my_dp = lax.axis_index("dp")
    my_expert = lax.axis_index("expert")
    slot_of = jnp.arange(groups * hidden, dtype=jnp.int32) // hidden
    expert_of = (((my_dp ^ (2 * slot_of)) * ring + my_expert) // 2).astype(jnp.int32)
    pick = (jnp.arange(capacity.shape[0], dtype=jnp.int32)[:, None] == expert_of[None, :]).astype(F32)

    def compute(x_part, c_part, coef_part):
        weight = tn(coef_part, pick, precision=lax.Precision.HIGHEST)
        gate_pre = nt(x_part, gate_t)
        up_pre = nt(x_part, up_t)
        back = nt(c_part, down) * weight
        sig = jax.nn.sigmoid(gate_pre)
        act = gate_pre * sig
        scaled_hidden = (act * up_pre * weight).astype(BF16)
        d_up = (back * act).astype(BF16)
        d_gate = (back * up_pre * (sig * (1.0 + gate_pre * (1.0 - sig)))).astype(BF16)
        out = jnp.dot(scaled_hidden, down, preferred_element_type=F32)
        grad = jnp.dot(d_gate, gate_t, preferred_element_type=F32) + jnp.dot(
            d_up, up_t, preferred_element_type=F32
        )
        return out, grad, tn(d_gate, x_part), tn(d_up, x_part), tn(scaled_hidden, c_part)

    all_tokens = x_all.shape[0]
    steps = max(1, all_tokens // 1024)
    if steps == 1:
        out, grad, gate_g, up_g, down_g = compute(x_all, c_all, coef_all)
    else:
        size = all_tokens // steps

        def step(carry, chunk):
            got = compute(*chunk)
            carry = tuple(a + b for a, b in zip(carry, got[2:]))
            return carry, (got[0].astype(BF16), got[1].astype(BF16))

        zero = jnp.zeros((groups * hidden, width), F32)
        chunks = (
            x_all.reshape(steps, size, width),
            c_all.reshape(steps, size, width),
            coef_all.reshape(-1, steps, size).swapaxes(0, 1),
        )
        (gate_g, up_g, down_g), (out, grad) = lax.scan(step, (zero, zero, zero), chunks)
        out = out.reshape(all_tokens, width).astype(F32)
        grad = grad.reshape(all_tokens, width).astype(F32)

    def collect(value):
        half = ring * token_count
        away = swap(value[half:].astype(BF16), dp_count, 1)
        mine = value[:half] + away.astype(F32)
        pieces = [mine[s * token_count : (s + 1) * token_count] for s in range(ring)]
        carry = pieces[ring - 1]
        for s in range(ring - 2, -1, -1):
            carry = pieces[s] + rotate(carry.astype(BF16), ring, -1).astype(F32)
        return carry.astype(BF16)

    parts = [
        jnp.concatenate([g[r * hidden : (r + 1) * hidden] for g in (gate_g, up_g, down_g)], axis=0)
        for r in range(groups)
    ]
    total_a = reduce_slots({r: parts[r][:cut] for r in range(groups)}, orders[0], dp_count)
    total_b = reduce_slots({r: parts[r][cut:] for r in range(groups)}, orders[1], dp_count)
    total = jnp.concatenate([total_a, total_b], axis=0).astype(BF16)
    return (
        collect(out),
        collect(grad),
        total[:hidden].T[None],
        total[hidden : 2 * hidden].T[None],
        total[2 * hidden :][None],
    )


def large_device(tokens, cotangent, expert_ids, gate_scores, hot_list, capacity, w_gate, w_up, w_down):
    dp_count = lax.axis_size("dp")
    ring = lax.axis_size("expert")
    groups = dp_count // 2
    bits = [1 << b for b in range(groups.bit_length() - 1)]
    orders = (bits, bits[::-1])
    token_count, width = tokens.shape
    hidden = w_gate.shape[2]
    rows = 3 * hidden
    cut = rows // 2
    packed = jnp.concatenate([w_gate[0].T, w_up[0].T, w_down[0]], axis=0)

    def spread(value):
        own = [value]
        for _ in range(ring - 1):
            own.append(rotate(own[-1], ring, 1))
        return own + [swap(v, dp_count, 1) for v in own]

    x_all = jnp.concatenate(spread(tokens), axis=0)
    c_all = jnp.concatenate(spread(cotangent), axis=0)
    coef = coefficients(expert_ids, gate_scores, hot_list, capacity)
    coef_all = jnp.concatenate(spread(coef), axis=1)

    first = gather_slots(packed[:cut], orders[0], dp_count)
    second = gather_slots(packed[cut:], orders[1], dp_count)
    full = [jnp.concatenate([first[r], second[r]], axis=0) for r in range(groups)]
    gate_t = jnp.concatenate([f[:hidden] for f in full], axis=0)
    up_t = jnp.concatenate([f[hidden : 2 * hidden] for f in full], axis=0)
    down = jnp.concatenate([f[2 * hidden :] for f in full], axis=0)

    my_dp = lax.axis_index("dp")
    my_expert = lax.axis_index("expert")
    slot_of = jnp.arange(groups * hidden, dtype=jnp.int32) // hidden
    expert_of = (((my_dp ^ (2 * slot_of)) * ring + my_expert) // 2).astype(jnp.int32)
    pick = (jnp.arange(capacity.shape[0], dtype=jnp.int32)[:, None] == expert_of[None, :]).astype(F32)

    def compute(x_part, c_part, coef_part):
        weight = tn(coef_part, pick, precision=lax.Precision.HIGHEST)
        gate_pre = nt(x_part, gate_t)
        up_pre = nt(x_part, up_t)
        back = nt(c_part, down) * weight
        sig = jax.nn.sigmoid(gate_pre)
        act = gate_pre * sig
        scaled_hidden = (act * up_pre * weight).astype(BF16)
        d_up = (back * act).astype(BF16)
        d_gate = (back * up_pre * (sig * (1.0 + gate_pre * (1.0 - sig)))).astype(BF16)
        out = jnp.dot(scaled_hidden, down, preferred_element_type=F32)
        grad = jnp.dot(d_gate, gate_t, preferred_element_type=F32) + jnp.dot(
            d_up, up_t, preferred_element_type=F32
        )
        return out, grad, tn(d_gate, x_part), tn(d_up, x_part), tn(scaled_hidden, c_part)

    all_tokens = x_all.shape[0]
    steps = max(1, all_tokens // 1024)
    if steps == 1:
        out, grad, gate_g, up_g, down_g = compute(x_all, c_all, coef_all)
    else:
        size = all_tokens // steps

        def step(carry, chunk):
            got = compute(*chunk)
            carry = tuple(a + b for a, b in zip(carry, got[2:]))
            return carry, (got[0].astype(BF16), got[1].astype(BF16))

        zero = jnp.zeros((groups * hidden, width), F32)
        chunks = (
            x_all.reshape(steps, size, width),
            c_all.reshape(steps, size, width),
            coef_all.reshape(-1, steps, size).swapaxes(0, 1),
        )
        (gate_g, up_g, down_g), (out, grad) = lax.scan(step, (zero, zero, zero), chunks)
        out = out.reshape(all_tokens, width).astype(F32)
        grad = grad.reshape(all_tokens, width).astype(F32)

    def collect(value):
        half = ring * token_count
        away = swap(value[half:].astype(BF16), dp_count, 1)
        mine = value[:half] + away.astype(F32)
        pieces = [mine[s * token_count : (s + 1) * token_count] for s in range(ring)]
        carry = pieces[ring - 1]
        for s in range(ring - 2, -1, -1):
            carry = pieces[s] + rotate(carry.astype(BF16), ring, -1).astype(F32)
        return carry.astype(BF16)

    parts = [
        jnp.concatenate([g[r * hidden : (r + 1) * hidden] for g in (gate_g, up_g, down_g)], axis=0)
        for r in range(groups)
    ]
    total_a = reduce_slots({r: parts[r][:cut] for r in range(groups)}, orders[0], dp_count)
    total_b = reduce_slots({r: parts[r][cut:] for r in range(groups)}, orders[1], dp_count)
    total = jnp.concatenate([total_a, total_b], axis=0).astype(BF16)
    return (
        collect(out),
        collect(grad),
        total[:hidden].T[None],
        total[hidden : 2 * hidden].T[None],
        total[2 * hidden :][None],
    )


EXTRA = 8


def staged(dp_count, ring):
    return dp_count == 8 and ring == 4


def prep_kernel(*refs):
    sources, out, held, sems = refs[:5], refs[5], refs[6:11], refs[11]
    copies = [
        pltpu.make_async_copy(source, target, sems.at[i])
        for i, (source, target) in enumerate(zip(sources, held))
    ]
    for copy in copies:
        copy.start()
    for copy in copies:
        copy.wait()
    ids, gates, hot_list, capacity, tokens = held
    size, width = tokens.shape
    out[:size] = tokens[...]
    shape = (1, size)
    gate_rows, present_rows, limits = [], [], []
    for x in range(capacity.shape[0]):
        match = ids[...] == x
        gate_rows.append(jnp.sum(jnp.where(match, gates[...], 0.0), axis=0, keepdims=True))
        present_rows.append(jnp.sum(match.astype(F32), axis=0, keepdims=True))
        limit = capacity[x]
        for h in range(hot_list.shape[0]):
            limit = jnp.where(hot_list[h] == x, size, limit)
        limits.append(jnp.full(shape, limit, jnp.int32).astype(F32))
    present = jnp.concatenate(present_rows, axis=0)
    before = lax.broadcasted_iota(jnp.int32, (size, size), 0) < lax.broadcasted_iota(
        jnp.int32, (size, size), 1
    )
    rank = jnp.dot(
        present.astype(BF16), before.astype(F32).astype(BF16), preferred_element_type=F32
    )
    kept = (present > 0.5) & (rank < jnp.concatenate(limits, axis=0))
    rest = jnp.where(kept, jnp.concatenate(gate_rows, axis=0), 0.0)
    parts = []
    for _ in range(3):
        part = rest.astype(BF16).astype(F32)
        parts.append(part)
        rest = rest - part
    places = EXTRA * (width // size)
    parts.append(jnp.zeros((places - 3 * rest.shape[0], size), F32))
    packed = jnp.concatenate(parts, axis=0)
    packed = [packed[i : i + EXTRA] for i in range(0, places, EXTRA)]
    out[size:] = jnp.concatenate(packed, axis=1).astype(BF16)


def act_block(coef, x_part, c_part, gates, ups, downs, slots, views):
    hidden = gates[0].shape[0]
    stack = jnp.concatenate([v[...] for v in (*gates, *ups)], axis=0)
    pre = nt(stack, x_part)
    back_all = nt(jnp.concatenate([d[...] for d in downs], axis=0), c_part)
    for i, (r, (scaled, d_gate, d_up)) in enumerate(zip(slots, views)):
        low, high = i * hidden, (i + len(slots)) * hidden
        weight = coef[r : r + 1]
        gate_pre = pre[low : low + hidden]
        up_pre = pre[high : high + hidden]
        sig = jax.nn.sigmoid(gate_pre)
        act = gate_pre * sig
        grad_hidden = back_all[low : low + hidden] * weight
        scaled[...] = (act * up_pre * weight).astype(BF16)
        d_up[...] = (grad_hidden * act).astype(BF16)
        d_gate[...] = (grad_hidden * up_pre * (sig * (1.0 + gate_pre * (1.0 - sig)))).astype(BF16)


def local_call(body, ins, outs, flops, after=None):
    whole = pl.BlockSpec(memory_space=pltpu.VMEM)
    specs = [whole] * len(ins)
    count = len(ins)
    if after is not None:
        ins = (*ins, after)
        specs = specs + [pl.BlockSpec(memory_space=pl.ANY)]

    def kernel(*refs):
        body(refs[:count], refs[len(ins) :])

    moved = sum(v.size * v.dtype.itemsize for v in (*ins, *outs))
    return pl.pallas_call(
        kernel,
        out_shape=list(outs),
        in_specs=specs,
        out_specs=[whole] * len(outs),
        compiler_params=pltpu.CompilerParams(vmem_limit_bytes=16 << 20),
        cost_estimate=pl.CostEstimate(flops=flops, bytes_accessed=moved, transcendentals=0),
    )(*ins)


def on_device(tokens, cotangent, expert_ids, gate_scores, hot_list, capacity, w_gate, w_up, w_down):
    dp_count = lax.axis_size("dp")
    ring = lax.axis_size("expert")
    groups = dp_count // 2
    size, width = tokens.shape
    experts = capacity.shape[0]
    if not staged(dp_count, ring):
        return large_device(
            tokens, cotangent, expert_ids, gate_scores, hot_list, capacity, w_gate, w_up, w_down
        )
    hidden = w_gate.shape[2]
    half = hidden // 2
    cut = hidden + half
    pair = 2 * size
    total = ring * pair
    last = ring - 1
    shape = jax.ShapeDtypeStruct

    gate0, up0, down0 = w_gate[0].T, w_up[0].T, w_down[0]
    gate1, up2 = swap(gate0, dp_count, 2), swap(up0, dp_count, 4)
    down1, down2 = swap(down0, dp_count, 2), swap(down0, dp_count, 4)
    up1, gate2 = swap(up0, dp_count, 2), swap(gate0, dp_count, 4)
    gate3, up3 = swap(gate1, dp_count, 4), swap(up2, dp_count, 2)

    hbm = pl.BlockSpec(memory_space=pltpu.HBM)
    prep_in = (expert_ids.T, gate_scores.T, hot_list, capacity, tokens)
    spaces = (pltpu.VMEM, pltpu.VMEM, pltpu.SMEM, pltpu.SMEM, pltpu.VMEM)
    tokens = pl.pallas_call(
        prep_kernel,
        out_shape=shape((size + EXTRA, width), BF16),
        in_specs=[hbm] * 5,
        out_specs=pl.BlockSpec(memory_space=pltpu.VMEM),
        scratch_shapes=[
            *[space(v.shape, v.dtype) for space, v in zip(spaces, prep_in)],
            pltpu.SemaphoreType.DMA((5,)),
        ],
        compiler_params=pltpu.CompilerParams(vmem_limit_bytes=60 << 20),
        cost_estimate=pl.CostEstimate(flops=1 << 20, bytes_accessed=1 << 19, transcendentals=0),
        name="prep",
    )(*prep_in)

    def spread(value):
        own = [value]
        for _ in range(1, ring):
            own.append(rotate(own[-1], ring, 1))
        return [(v, swap(v, dp_count, 1)) for v in own]

    cots, toks = spread(cotangent), spread(tokens)
    late1, late2, _ = lax.optimization_barrier((down1, down2, toks[last - 1][0]))
    low3 = swap(late1[:half], dp_count, 4)
    high3 = swap(late2[half:], dp_count, 2)
    gates = (gate0, gate1, gate2, gate3)
    ups = (up0, up1, up2, up3)
    downs = ((down0,), (down1,), (down2,), (low3, high3))
    slot = jnp.arange(8, dtype=jnp.int32)
    expert_of = ((lax.axis_index("dp") ^ (2 * slot)) * ring + lax.axis_index("expert")) // 2
    lane = jnp.arange(EXTRA * (width // size), dtype=jnp.int32)
    lane = jnp.where(lane < 3 * experts, lane % experts, -1)
    pick = (expert_of[:, None] == lane[None, :]).astype(BF16)

    def flat(pairs):
        return [v for p in pairs for v in p]

    def stage_body(refs, outs):
        for source, target in zip(refs, outs):
            target[...] = source[...]

    own = (tokens, cotangent)
    own = local_call(stage_body, own, [shape(v.shape, v.dtype) for v in own], 1 << 20)
    toks[0], cots[0] = (own[0], toks[0][1]), (own[1], cots[0][1])

    def block_of(refs, s):
        count = (len(refs) - 1) // 2
        t, c = refs[1 + 2 * s : 3 + 2 * s], refs[1 + count + 2 * s : 3 + count + 2 * s]
        x_part = jnp.concatenate([v[:size] for v in t], axis=0)
        coef = []
        for v in t:
            extra = v[size:].astype(F32)
            packed = [extra[:, i : i + size] for i in range(0, width, size)]
            packed = jnp.concatenate(packed, axis=0).astype(BF16)
            coef.append(jnp.dot(refs[0][...], packed, preferred_element_type=F32))
        coef = jnp.concatenate(coef, axis=1)
        return coef, x_part, jnp.concatenate([v[...] for v in c], axis=0)

    def views_of(outs, slots, columns):
        return [
            [o.at[pl.ds(j * hidden, hidden), columns] for o in outs] for j in range(len(slots))
        ]

    near = (0, 1, 2)
    main_in = [pick, *flat(toks[:last]), *flat(cots[:last])]
    near_in = [*gates[:3], *ups[:3], *flat(downs[:3])]

    def main_body(refs, outs):
        g, u, d = (refs[len(main_in) + 3 * i : len(main_in) + 3 * i + 3] for i in range(3))
        for s in range(last):
            block = block_of(refs[: len(main_in)], s)
            act_block(*block, g, u, d, near, views_of(outs, near, pl.ds(s * pair, pair)))

    main = local_call(
        main_body,
        (*main_in, *near_in),
        [shape((3 * hidden, last * pair), BF16)] * 3,
        18 * hidden * last * pair * width,
    )

    def out_block(acts, g, u, d, outs):
        scaled, d_gate, d_up = acts
        out = tn(scaled, jnp.concatenate([v[...] for v in d], axis=0))
        outs[0][...] = out[:size]
        outs[2][:size] = out[size:].astype(BF16)
        both = jnp.concatenate([v[...] for v in (*g, *u)], axis=0)
        grad = tn(jnp.concatenate([d_gate, d_up], axis=0), both)
        outs[1][...] = grad[:size]
        outs[2][size:] = grad[size:].astype(BF16)

    weights_in = [*gates, *ups, *flat(downs)]
    out_shapes = [shape((size, width), F32)] * 2 + [shape((pair, width), BF16)]
    all_in = [pick, *flat(toks), *flat(cots)]

    def grad_block(slots, acts, refs, outs):
        count = len(refs) // 2
        x_all = jnp.concatenate([v[:size] for v in refs[:count]], axis=0)
        c_all = jnp.concatenate([v[...] for v in refs[count:]], axis=0)
        down_g = jnp.dot(acts[0], c_all, preferred_element_type=F32)
        both = jnp.concatenate([acts[1], acts[2]], axis=0)
        both_g = jnp.dot(both, x_all, preferred_element_type=F32)
        for i in range(slots):
            first, second = outs[2 * i], outs[2 * i + 1]
            low, high = i * hidden, (i + slots) * hidden
            first[hidden:] = down_g[low : low + half].astype(first.dtype)
            second[hidden:] = down_g[low + half : low + hidden].astype(second.dtype)
            first[:hidden] = both_g[low : low + hidden].astype(first.dtype)
            second[:hidden] = both_g[high : high + hidden].astype(second.dtype)

    near_two = (1, 2)

    def near_body(refs, outs):
        rest = refs[len(all_in) :]
        g, u, d = (rest[2 * i : 2 * i + 2] for i in range(3))
        block = block_of(refs[: len(all_in)], last)
        act_block(*block, g, u, d, near_two, views_of(outs[:3], near_two, pl.ds(0, pair)))
        rows = pl.ds(hidden, 2 * hidden)
        acts = [
            jnp.concatenate([m[rows], t[...]], axis=1) for m, t in zip(rest[6:], outs[:3])
        ]
        grad_block(2, acts, refs[1 : len(all_in)], outs[3:])

    part_shapes = [shape((cut, width), t) for t in (BF16, F32, F32, BF16)]
    got = local_call(
        near_body,
        (*all_in, *gates[1:3], *ups[1:3], *flat(downs[1:3]), *main),
        [shape((2 * hidden, pair), BF16)] * 3 + part_shapes,
        12 * hidden * pair * width + 12 * hidden * total * width,
    )
    tail, (first1, second1, first2, second2) = got[:3], got[3:]

    far_in = [gates[3], ups[3], *downs[3]]

    ends = (0, 3)
    ends_in = [gates[0], gates[3], ups[0], ups[3], *downs[0], *downs[3]]

    def ordered(end, inner):
        return jnp.concatenate([end[:hidden], inner[...], end[hidden:]], axis=0)

    def middle_body(refs, outs):
        rest = refs[5 + len(ends_in) :]
        block = block_of(refs[:5], 0)
        g, u, d = refs[5:7], refs[7:9], refs[9 : 5 + len(ends_in)]
        act_block(*block, g, u, d, ends, views_of(outs[:3], ends, pl.ds(0, pair)))
        down = jnp.concatenate([v[...] for v in rest[:-1]], axis=0)
        out = tn(ordered(outs[0], rest[-1]), down)
        outs[3][...] = out[:size]
        outs[4][...] = out[size:].astype(BF16)

    halves = [shape((size, width), F32), shape((size, width), BF16)]
    got = local_call(
        middle_body,
        (pick, *toks[last], *cots[last], *ends_in, *flat(downs), tail[0]),
        [shape((2 * hidden, pair), BF16)] * 3 + halves,
        10 * groups * hidden * pair * width // 2,
        after=first1,
    )
    end_acts, mixed_part = got[:3], got[3:]

    def mid_grad_body(refs, outs):
        acts = jnp.concatenate([ordered(refs[0], refs[1]), ordered(refs[2], refs[3])], axis=0)
        grad = tn(acts, jnp.concatenate([v[...] for v in refs[4:]], axis=0))
        outs[0][...] = grad[:size]
        outs[1][...] = grad[size:].astype(BF16)

    grad_part = local_call(
        mid_grad_body,
        (end_acts[1], tail[1], end_acts[2], tail[2], *gates, *ups),
        halves,
        4 * groups * hidden * pair * width,
    )
    part = {last: (mixed_part[0], grad_part[0])}

    def far_body(refs, outs):
        rest = refs[len(all_in) :]
        for s in range(last):
            views = views_of(outs[:3], (3,), pl.ds(s * pair, pair))
            block = block_of(refs[: len(all_in)], s)
            act_block(*block, rest[:1], rest[1:2], rest[2:-3], (3,), views)
        acts = [
            jnp.concatenate([v[...], t[hidden:]], axis=1) for v, t in zip(outs[:3], rest[-3:])
        ]
        grad_block(1, acts, refs[1 : len(all_in)], outs[3:])

    got = local_call(
        far_body,
        (*all_in, *far_in, *end_acts),
        [shape((hidden, last * pair), BF16)] * 3 + [shape((cut, width), BF16)] * 2,
        12 * hidden * total * width,
    )
    diag, (first3, second3) = got[:3], got[3:]

    def own_body(refs, outs):
        rows = pl.ds(0, hidden)
        acts = [jnp.concatenate([refs[k][rows], refs[k + 3][rows]], axis=1) for k in range(3)]
        grad_block(1, acts, refs[6:], outs)

    def outputs(s, after):
        acts = [*main, *diag]

        def body(refs, outs):
            rest = refs[6:]
            g, u, d = rest[:groups], rest[groups : 2 * groups], rest[2 * groups :]
            block = pl.ds(s * pair, pair)
            acts = [
                jnp.concatenate([refs[k][:, block], refs[k + 3][:, block]], axis=0)
                for k in range(3)
            ]
            out_block(acts, g, u, d, outs)

        flops = 6 * groups * hidden * pair * width
        return local_call(body, (*acts, *weights_in), out_shapes, flops, after)

    a1, b2 = swap(first1, dp_count, 2), swap(second2, dp_count, 4)
    a3, b3 = swap(first3, dp_count, 2), swap(second3, dp_count, 4)
    after = first3
    for s in range(last - 1, -1, -1):
        part[s] = outputs(s, after)
        after = part[s][0]
    first0, second0 = local_call(
        own_body,
        (*main, *end_acts, *flat(toks), *flat(cots)),
        [shape((cut, width), F32)] * 2,
        6 * hidden * total * width,
        after,
    )

    def add(s, i, away, moved):
        rows = pl.ds(0 if s == last else i * size, size)

        def body(refs, outs):
            value = refs[0][...] + refs[1][rows].astype(F32)
            if moved is not None:
                value = value + refs[2][...].astype(F32)
            outs[0][...] = value.astype(BF16)

        ins = (part[s][i], away) if moved is None else (part[s][i], away, moved)
        return local_call(body, ins, [shape((size, width), BF16)], 1 << 18)[0]

    away = {s: [swap(part[s][2], dp_count, 1)] * 2 for s in range(last)}
    away[last] = [swap(v[1], dp_count, 1) for v in (mixed_part, grad_part)]
    carry = [None, None]
    for s in range(last, -1, -1):
        if s < last:
            carry = [rotate(c, ring, -1) for c in carry]
        carry = [add(s, i, away[s][i], carry[i]) for i in range(2)]
    mixed, token_grad = carry

    a2 = swap((first2 + a3.astype(F32)).astype(BF16), dp_count, 4)
    b1 = swap((second1 + b3.astype(F32)).astype(BF16), dp_count, 2)

    def finish(refs, outs):
        first = refs[0][...] + refs[2][...].astype(F32) + refs[3][...].astype(F32)
        second = refs[1][...] + refs[4][...].astype(F32) + refs[5][...].astype(F32)
        outs[0][...] = first[:hidden].astype(BF16)
        outs[1][...] = second[:hidden].astype(BF16)
        outs[2][:half] = first[hidden:].astype(BF16)
        outs[2][half:] = second[hidden:].astype(BF16)

    gate_g, up_g, down_g = local_call(
        finish, (first0, second0, a1, a2, b2, b1), [shape((hidden, width), BF16)] * 3, 1 << 20
    )
    return mixed, token_grad, gate_g.T[None], up_g.T[None], down_g[None]


def solution(mesh):
    rows = P(("dp", "expert"), None)
    weights = P(("dp", "expert"), None, None)
    return jax.shard_map(
        on_device,
        mesh=mesh,
        in_specs=(rows, rows, rows, rows, P(), P(), weights, weights, weights),
        out_specs=(rows, rows, weights, weights, weights),
        check_vma=False,
    )
```
